32 devices in a mesh: shard: 2 (over x), ctx: 4 (over z), tp: 4 (over y, core).
Axes of the slice: x: 2, y: 2, z: 4, core: 2. Of those that a mesh axis runs over, the one named last changes fastest.
Arguments:
- tokens: bfloat16 [4, 1024, 768], P('shard', ('ctx', 'tp')), may hold values from -6 to 6
- cotangent: bfloat16 [4, 1024, 768], P('shard', ('ctx', 'tp')), may hold values from -6 to 6
- segment_ids: int32 [4, 1024], P('shard'), may hold values from 0 to 7, never falling along the last dimension, each value on 1 to 512 neighbouring positions
- lengths: int32 [4], P('shard'), may hold values from 768 to 1024
- query_weight: bfloat16 [2, 768, 768], P(None, 'shard', 'tp'), may hold values from -0.21875 to 0.21875
- key_weight: bfloat16 [2, 768, 768], P(None, 'shard', 'tp'), may hold values from -0.21875 to 0.21875
- value_weight: bfloat16 [2, 768, 768], P(None, 'shard', 'tp'), may hold values from -0.21875 to 0.21875
- output_weight: bfloat16 [2, 768, 768], P(None, 'tp', 'shard'), may hold values from -1.75 to 1.75
- inner_weight: bfloat16 [2, 768, 3072], P(None, 'shard', 'tp'), may hold values from -0.21875 to 0.21875
- outer_weight: bfloat16 [2, 3072, 768], P(None, 'tp', 'shard'), may hold values from -0.109375 to 0.109375
- query_bias: bfloat16 [2, 768], P(None, 'shard'), may hold values from -3 to 3
- value_bias: bfloat16 [2, 768], P(None, 'shard'), may hold values from -0.29882812 to 0.29882812
- output_bias: bfloat16 [2, 768], P(None, 'shard'), may hold values from -0.59765625 to 0.59765625
- inner_bias: bfloat16 [2, 3072], P(None, 'shard'), may hold values from -1.1953125 to 1.1953125
- outer_bias: bfloat16 [2, 768], P(None, 'shard'), may hold values from -0.59765625 to 0.59765625
- first_gain: bfloat16 [2, 768], P(None, 'shard'), may hold values from 0.5 to 1.5
- first_shift: bfloat16 [2, 768], P(None, 'shard'), may hold values from -0.59765625 to 0.59765625
- second_gain: bfloat16 [2, 768], P(None, 'shard'), may hold values from 0.5 to 1.5
- second_shift: bfloat16 [2, 768], P(None, 'shard'), may hold values from -0.59765625 to 0.59765625
Outputs:
- layer_out: bfloat16 [4, 1024, 768], P('shard', ('ctx', 'tp'))
- grad_tokens: float32 [4, 1024, 768], P('shard', ('ctx', 'tp'))
- grad_query_weight: float32 [2, 768, 768], P(None, 'shard', 'tp')
- grad_key_weight: float32 [2, 768, 768], P(None, 'shard', 'tp')
- grad_value_weight: float32 [2, 768, 768], P(None, 'shard', 'tp')
- grad_output_weight: float32 [2, 768, 768], P(None, 'tp', 'shard')
- grad_inner_weight: float32 [2, 768, 3072], P(None, 'shard', 'tp')
- grad_outer_weight: float32 [2, 3072, 768], P(None, 'tp', 'shard')
- grad_query_bias: float32 [2, 768], P(None, 'shard')
- grad_value_bias: float32 [2, 768], P(None, 'shard')
- grad_output_bias: float32 [2, 768], P(None, 'shard')
- grad_inner_bias: float32 [2, 3072], P(None, 'shard')
- grad_outer_bias: float32 [2, 768], P(None, 'shard')
- grad_first_gain: float32 [2, 768], P(None, 'shard')
- grad_first_shift: float32 [2, 768], P(None, 'shard')
- grad_second_gain: float32 [2, 768], P(None, 'shard')
- grad_second_shift: float32 [2, 768], P(None, 'shard')
The draws below stay inside these ranges and needn't reach their ends.
Inputs may be any that keep to these rules, and one draw needn't show every extreme that they name: `segment_ids`: along each sequence the document numbers never fall, and no document has more than 512 positions. `lengths`: positions at or past a sequence's length are padding.
All inputs are finite; a program needn't handle non-finite values.
Results may differ from the reference program's by a relative error of at most 0.04.
Values may be sent and summed in bfloat16 or wider, within the bound.
A program may use at most 128 MiB of HBM per device.

```python
import math
import jax
import jax.numpy as jnp
import numpy as np
from jax import lax

D = 768
HD = 64
FF = 3072
LAYERS = 2
LEN = 1024
DOCS = 8
SEQ_DEV = 2
SEQS = 4


def plant(array, stream_key, smallest, largest):
    shape = array.shape
    place = [jax.random.randint(jax.random.fold_in(stream_key, axis), (), 0, shape[axis]) for axis in range(len(shape))]
    array = array.at[tuple(place)].set(smallest)
    longest = shape.index(max(shape))
    place[longest] = (place[longest] + 1) % shape[longest]
    return array.at[tuple(place)].set(largest)


def raised(drawn, stream_key, source, target, parts, factor):
    def block_of(position):
        return (jnp.arange(drawn.shape[position]) // (drawn.shape[position] // parts)).reshape((-1,) + (1,) * (drawn.ndim - 1 - position))

    first = jax.random.permutation(stream_key, parts)[block_of(target)]
    far = (block_of(target) + parts // 2) % parts
    return jnp.where((block_of(source) == first) | (block_of(source) == far), factor * drawn, drawn)


def levels(key, extent, shards, least, top_value):
    def one(dim, shards_of):
        draws = jax.random.uniform(jax.random.fold_in(jax.random.fold_in(key, 6), dim), (shards_of,), jnp.float32, least / len(shards), top_value / len(shards))
        return jnp.repeat(jnp.exp(draws), extent[dim] // shards_of).reshape((-1,) + (1,) * (len(extent) - dim - 1))

    level = one(*shards[0])
    for cut in shards[1:]:
        level = level * one(*cut)
    return level


def split_up(number_of, total, most, skew):
    portions = [(1 << 20) // math.isqrt(standing ** skew) + 1 for standing in range(2, number_of + 1)]
    surplus, counts = total - most - (number_of - 1), [1] * (number_of - 1)
    while surplus > 0:
        movable = [i for i in range(number_of - 1) if counts[i] < most]
        mass, budget = sum([portions[i] for i in movable]), surplus
        for i in movable:
            more = min(most - counts[i], max(1, budget * portions[i] // mass), surplus)
            counts[i] = counts[i] + more
            surplus = surplus - more
    return np.array([most] + counts)


def uneven_parts(rng, amount, total, limit, skew):
    if amount == 2:
        one = jax.random.randint(rng, (), max(1, total - limit), min(limit, total - 1) + 1)
        return jnp.stack([one, total - one])
    tallies = jnp.asarray(split_up(amount, total, limit, skew), jnp.int32)
    twos = (amount - 1) // 2
    source_of, taker = tallies[1:1 + 2 * twos:2], tallies[2:2 + 2 * twos:2]
    slack = jnp.minimum(source_of - 1, limit - taker)
    shifted = jax.random.randint(jax.random.fold_in(rng, 1), (twos,), 0, 1 << 20) % (slack + 1)
    tallies = tallies.at[1:1 + 2 * twos:2].set(source_of - shifted).at[2:2 + 2 * twos:2].set(taker + shifted)
    return tallies[jax.random.permutation(jax.random.fold_in(rng, 2), amount)]


def normal_values(key, extent, width, limit, pieces=(), kind=jnp.bfloat16):
    drawn = jax.random.normal(key, extent, jnp.float32) * width
    if len(pieces) > 0:
        drawn = levels(key, extent, pieces, -0.22, 0.18) * drawn
    return jnp.clip(drawn, min=-limit, max=limit).astype(kind)


def heavy_noise(stream_key, dims, width, most, cuts, heavy, held_as=jnp.bfloat16):
    values = width * jax.random.normal(stream_key, dims, jnp.float32)
    if cuts:
        values = values * levels(stream_key, dims, cuts, -0.22, 0.18)
    return jnp.clip(raised(values, jax.random.fold_in(stream_key, 3), *heavy), -most, most).astype(held_as)


def setup_inputs(seed: int = 0) -> dict:
    splits = jax.random.split(jax.random.key(seed), 20)
    return {
        "tokens": heavy_noise(splits[0], (SEQS, LEN, D), 1.0, 6.0, ((0, 2), (1, 16)), (0, 2, 2, 2.0)),
        "cotangent": normal_values(splits[1], (SEQS, LEN, D), 1.0, 6.0, ((0, 2), (1, 16))),
        "segment_ids": jax.vmap(lambda own: jnp.searchsorted(jnp.cumsum(uneven_parts(own, DOCS, LEN, LEN // 2, 2)), jnp.arange(LEN), side="right"))(jax.random.split(splits[2], SEQS)).reshape((SEQS, LEN)).astype(jnp.int32),
        "lengths": plant(jax.random.randint(splits[3], (SEQS,), 3 * LEN // 4, LEN + 1), jax.random.fold_in(splits[3], 1), 3 * LEN // 4, LEN).astype(jnp.int32),
        "query_weight": normal_values(splits[4], (LAYERS, D, D), D ** -0.5, 0.21875, ((1, 2), (2, 4))),
        "key_weight": normal_values(splits[5], (LAYERS, D, D), D ** -0.5, 0.21875, ((1, 2), (2, 4))),
        "value_weight": normal_values(splits[6], (LAYERS, D, D), D ** -0.5, 0.21875, ((1, 2), (2, 4))),
        "output_weight": normal_values(splits[7], (LAYERS, D, D), (2 * D * DOCS // LEN) ** -0.5, 1.75, ((1, 4), (2, 2))),
        "inner_weight": normal_values(splits[8], (LAYERS, D, FF), D ** -0.5, 0.21875, ((1, 2), (2, 4))),
        "outer_weight": normal_values(splits[9], (LAYERS, FF, D), FF ** -0.5, 0.109375, ((1, 4), (2, 2))),
        "query_bias": normal_values(splits[10], (LAYERS, D), 0.5, 3.0, ((1, 2),)),
        "value_bias": normal_values(splits[11], (LAYERS, D), 0.05, 0.29882812, ((1, 2),)),
        "output_bias": normal_values(splits[12], (LAYERS, D), 0.1, 0.59765625, ((1, 2),)),
        "inner_bias": normal_values(splits[13], (LAYERS, FF), 0.2, 1.1953125, ((1, 2),)),
        "outer_bias": normal_values(splits[14], (LAYERS, D), 0.1, 0.59765625, ((1, 2),)),
        "first_gain": jnp.clip(1.0 + 0.1 * jax.random.normal(splits[15], (LAYERS, D), jnp.float32), 0.5, 1.5).astype(jnp.bfloat16),
        "first_shift": normal_values(splits[16], (LAYERS, D), 0.1, 0.59765625, ((1, 2),)),
        "second_gain": jnp.clip(1.0 + 0.1 * jax.random.normal(splits[17], (LAYERS, D), jnp.float32), 0.5, 1.5).astype(jnp.bfloat16),
        "second_shift": normal_values(splits[18], (LAYERS, D), 0.1, 0.59765625, ((1, 2),)),
    }


@jax.custom_vjp
def low(v):
    return lax.optimization_barrier(v.astype(jnp.bfloat16)).astype(jnp.float32)

@jax.custom_vjp
def low_back(v):
    return v

def low_keep(v):
    return (low(v), None)

def low_pass(kept, grad):
    return (grad,)

def back_keep(v):
    return (v, None)

def back_low(kept, grad):
    return (low(grad),)
low.defvjp(low_keep, low_pass)
low_back.defvjp(back_keep, back_low)
EPSILON = 1e-05
HIGH = lax.Precision.HIGHEST

def layer_norm(resid, gain, shift):
    center = resid - lax.optimization_barrier(jnp.mean(resid, axis=-1, keepdims=True))
    spread = lax.optimization_barrier(jnp.mean(center * center, axis=-1, keepdims=True))
    return center * lax.rsqrt(spread + EPSILON) * gain + shift

def product(left, right):
    return jnp.dot(left, right, precision=HIGH)

def one_layer(resid, key_ids, weights):
    query_weight, key_weight, value_weight, output_weight, inner_weight, outer_weight, query_bias, value_bias, output_bias, inner_bias, outer_bias, first_gain, first_shift, second_gain, second_shift = weights
    group_count, seq_len, model_width = resid.shape
    head_count = model_width // HD
    row_data = low(resid)
    query_rows = low(low_back(product(row_data, query_weight) + query_bias)).reshape(group_count, seq_len, head_count, HD)
    key_rows = low(low_back(product(row_data, key_weight))).reshape(group_count, seq_len, head_count, HD)
    value_rows = low(low_back(product(row_data, value_weight) + value_bias)).reshape(group_count, seq_len, head_count, HD)
    scores = low_back(jnp.einsum('gqhd,gkhd->ghqk', query_rows, key_rows, precision=HIGH) * HD ** (-0.5))
    allowed = key_ids[:, None, :, None] == key_ids[:, None, None, :]
    scores = jnp.where(allowed, scores, -1e+30)
    row_top = lax.optimization_barrier(jnp.max(scores, axis=-1, keepdims=True))
    expo = jnp.exp(scores - row_top)
    attn_probs = expo / lax.optimization_barrier(jnp.sum(expo, axis=-1, keepdims=True))
    mixed = jnp.einsum('ghqk,gkhd->gqhd', low(attn_probs), value_rows, precision=HIGH).reshape(group_count, seq_len, model_width)
    mixed = low(low_back(mixed))
    branch = low_back(product(mixed, output_weight) + output_bias)
    normed = layer_norm(resid + branch, first_gain, first_shift)
    inner_pre = low_back(product(low(normed), inner_weight) + inner_bias)
    active = low(jax.nn.gelu(inner_pre, approximate=False))
    outer_sum = low_back(product(active, outer_weight) + outer_bias)
    return layer_norm(normed + outer_sum, second_gain, second_shift)

def reference(tokens, cotangent, segment_ids, lengths, query_weight, key_weight, value_weight, output_weight, inner_weight, outer_weight, query_bias, value_bias, output_bias, inner_bias, outer_bias, first_gain, first_shift, second_gain, second_shift):
    params = tuple((item.astype(jnp.float32) for item in (query_weight, key_weight, value_weight, output_weight, inner_weight, outer_weight, query_bias, value_bias, output_bias, inner_bias, outer_bias, first_gain, first_shift, second_gain, second_shift)))
    positions = jnp.arange(LEN, dtype=jnp.int32)[None, :]
    key_ids = jnp.where(positions < lengths[:, None], segment_ids, -1).astype(jnp.int32)
    block_count = SEQS // SEQ_DEV
    id_blocks = key_ids.reshape(block_count, SEQ_DEV, LEN)

    def group_layers(block_data, block_ids, weights):
        for layer_at in range(LAYERS):
            block_data = one_layer(block_data, block_ids, tuple((item[layer_at] for item in weights)))
        return block_data
    group_saved = jax.checkpoint(group_layers)

    def forward(resid, weights):
        resid_blocks = resid.reshape(block_count, SEQ_DEV, LEN, D)

        def advance(carry, item):
            return (carry, group_saved(item[0], item[1], weights))
        _, results = lax.scan(advance, jnp.zeros((), jnp.float32), (resid_blocks, id_blocks))
        return results.reshape(SEQS, LEN, D)
    result, pull_back = jax.vjp(forward, tokens.astype(jnp.float32), params)
    grad_input, grads = pull_back(cotangent.astype(jnp.float32))
    return (result.astype(jnp.bfloat16), grad_input, grads[0], grads[1], grads[2], grads[3], grads[4], grads[5], grads[6], grads[7], grads[8], grads[9], grads[10], grads[11], grads[12], grads[13], grads[14])
```

```python
import functools

import jax
import jax.numpy as jnp
from jax import lax
from jax.experimental import pallas as pl
from jax.experimental.pallas import tpu as pltpu
from jax.sharding import PartitionSpec as P

HD = 64
LAYERS = 2
EPSILON = 1e-05
MESH = pl.DeviceIdType.MESH
F32 = jnp.float32
BF16 = jnp.bfloat16
NEG = -1e30
VEC_ROWS = 24


def nn(a, b):
    return jnp.dot(a, b, preferred_element_type=F32)


def nt(a, b):
    return lax.dot_general(a, b, (((1,), (1,)), ((), ())), preferred_element_type=F32)


def tn(a, b):
    return lax.dot_general(a, b, (((0,), (0,)), ((), ())), preferred_element_type=F32)


def norm_forward(resid, gain, shift):
    center = resid - jnp.mean(resid, axis=-1, keepdims=True)
    spread = jnp.mean(center * center, axis=-1, keepdims=True)
    rstd = lax.rsqrt(spread + EPSILON)
    xhat = center * rstd
    return xhat * gain + shift, xhat, rstd


def norm_backward(grad, xhat, rstd, gain):
    scaled = grad * gain
    first = jnp.mean(scaled, axis=-1, keepdims=True)
    second = jnp.mean(scaled * xhat, axis=-1, keepdims=True)
    return rstd * (scaled - first - xhat * second)


def step_kernel(dims, fused, *refs):
    (
        tok_ref,
        cot_ref,
        idc_ref,
        idr_ref,
        vec_ref,
        wq_ref,
        wk_ref,
        wv_ref,
        wo_ref,
        wi_ref,
        wu_ref,
        out_tok,
        out_grad,
        out_mat,
        out_vec,
        WQ,
        WK,
        WV,
        WO,
        WI,
        WU,
        VB,
        H,
        N1,
        DR,
        DR1,
        TK,
        CO,
        OT,
        OG,
        XH1,
        XH2,
        SD1,
        SD2,
        XB,
        Q,
        K,
        V,
        OB,
        N1B,
        G,
        GP,
        PB,
        DF,
        DA,
        DU,
        DOB,
        DQ,
        DK,
        DV,
        DKF,
        DVF,
        PF,
        SB,
        RB,
        ZS,
        ZR,
        GO,
        GS,
        XR,
        YR,
        Y2,
        wl_sem,
        ws_sem,
        wr_sem,
        rd_s,
        rd_r,
        g8_s,
        g8_r,
        g4_s,
        g4_r,
        rs_s,
        rs_r,
        rz_s,
        rz_r,
        xs_s,
        xs_r,
        z1_s,
        z1_r,
        z2_s,
        z2_r,
        z3_s,
        z3_r,
        om_sem,
    ) = refs
    width, cols, units, half = dims
    seqs, part = tok_ref.shape[0], tok_ref.shape[1]
    rows = 2 * part
    own_rows = 4 * rows
    all_rows = 8 * rows
    s = lax.axis_index("shard")
    c = lax.axis_index("ctx")
    t = lax.axis_index("tp")
    hf = lax.rem(c, 2)
    y = t // 2
    k = lax.rem(t, 2)
    tc = t + 1 - 2 * k
    ty = lax.rem(t + 2, 4)
    zp = c + 1 - 2 * hf
    is_inner = jnp.logical_or(c == 1, c == 2)
    is_outer = jnp.logical_not(is_inner)
    z_in = jnp.where(c == 0, 1, 2)
    z_mid = 3 - c
    z_out = jnp.where(c == 1, 0, 3)

    def rc(src, dst, ssem, rsem, cc, tt, ss=None):
        return pltpu.make_async_remote_copy(
            src_ref=src,
            dst_ref=dst,
            send_sem=ssem,
            recv_sem=rsem,
            device_id=(s if ss is None else ss, cc, tt),
            device_id_type=MESH,
        )

    bar = pltpu.get_barrier_semaphore()
    for dc in range(4):
        for dt in range(4):
            if dc or dt:
                pl.semaphore_signal(
                    bar,
                    1,
                    device_id=(s, lax.rem(c + dc, 4), lax.rem(t + dt, 4)),
                    device_id_type=MESH,
                )
    if fused:
        pl.semaphore_signal(bar, 1, device_id=(1 - s, c, t), device_id_type=MESH)
    pl.semaphore_wait(bar, 16 if fused else 15)

    row_at = pl.multiple_of(s * half, half)

    def weight_views(layer):
        if not fused:
            return [
                (wq_ref.at[layer], WQ.at[layer]),
                (wk_ref.at[layer], WK.at[layer]),
                (wv_ref.at[layer], WV.at[layer]),
                (wo_ref.at[layer], WO.at[layer]),
                (wi_ref.at[layer], WI.at[layer]),
                (wu_ref.at[layer], WU.at[layer]),
            ]
        return [
            (wq_ref.at[layer], WQ.at[layer, pl.ds(row_at, half)]),
            (wk_ref.at[layer], WK.at[layer, pl.ds(row_at, half)]),
            (wv_ref.at[layer], WV.at[layer, pl.ds(row_at, half)]),
            (wo_ref.at[layer], WO.at[layer, :, pl.ds(row_at, half)]),
            (wi_ref.at[layer], WI.at[layer, pl.ds(row_at, half)]),
            (wu_ref.at[layer], WU.at[layer, :, pl.ds(row_at, half)]),
        ]

    def weight_copies(layer, item):
        src, dst = weight_views(layer)[item]
        local = pltpu.make_async_copy(src, dst, wl_sem.at[layer, item])
        remote = None
        if fused:
            remote = rc(src, dst, ws_sem.at[layer, item], wr_sem.at[layer, item], c, t, 1 - s)
        return local, remote

    def weight_wait(layer, item):
        local, remote = weight_copies(layer, item)
        local.wait()
        if fused:
            remote.wait()

    if fused:
        vec_copy = rc(vec_ref, VB.at[s], ws_sem.at[0, 6], wr_sem.at[0, 6], c, t, 1 - s)
        vec_copy.start()
        VB[s] = vec_ref[...]
    else:
        VB[...] = vec_ref[...]

    b_me = c // 2
    spread_t = 2 * hf + y

    def spread_copies(src_ref, dst_ref, which):
        return [
            (
                jnp.logical_and(2 * b + c // 2 == c, spread_t == t),
                rc(
                    src_ref.at[b],
                    dst_ref.at[pl.ds(k * part, part)],
                    rd_s.at[which, b],
                    rd_r.at[which, k],
                    2 * b + c // 2,
                    spread_t,
                ),
            )
            for b in range(2)
        ]

    def spread_start(src_ref, dst_ref, which):
        for b, (mine, copy) in enumerate(spread_copies(src_ref, dst_ref, which)):

            @pl.when(mine)
            def _():
                dst_ref[pl.ds(pl.multiple_of(k * part, part), part), :] = src_ref[b]

            @pl.when(jnp.logical_not(mine))
            def _():
                copy.start()

    def spread_wait(src_ref, dst_ref, which):
        for mine, copy in spread_copies(src_ref, dst_ref, which):

            @pl.when(jnp.logical_not(mine))
            def _():
                copy.wait_send()

        for kk in range(2):
            mine = jnp.logical_and(2 * hf + y == c, 2 * k + kk == t)

            @pl.when(jnp.logical_not(mine))
            def _():
                rc(
                    src_ref.at[0],
                    dst_ref.at[pl.ds(kk * part, part)],
                    rd_s.at[which, 0],
                    rd_r.at[which, kk],
                    c,
                    t,
                ).wait_recv()

    def collect_copies(src_ref, dst_ref, which):
        return [
            (
                jnp.logical_and(2 * hf + y == c, 2 * k + kk == t),
                rc(
                    src_ref.at[pl.ds(kk * part, part)],
                    dst_ref.at[b_me],
                    rd_s.at[which, kk],
                    rd_r.at[which, b_me],
                    2 * hf + y,
                    2 * k + kk,
                ),
            )
            for kk in range(2)
        ]

    def collect_start(src_ref, dst_ref, which):
        for kk, (mine, copy) in enumerate(collect_copies(src_ref, dst_ref, which)):

            @pl.when(mine)
            def _():
                dst_ref[b_me] = src_ref[kk * part : (kk + 1) * part, :]

            @pl.when(jnp.logical_not(mine))
            def _():
                copy.start()

    def collect_wait(src_ref, dst_ref, which):
        for mine, copy in collect_copies(src_ref, dst_ref, which):

            @pl.when(jnp.logical_not(mine))
            def _():
                copy.wait_send()

        for b in range(2):
            mine = jnp.logical_and(2 * b + c // 2 == c, spread_t == t)

            @pl.when(jnp.logical_not(mine))
            def _():
                rc(
                    src_ref.at[pl.ds(0, part)],
                    dst_ref.at[b],
                    rd_s.at[which, 0],
                    rd_r.at[which, b],
                    c,
                    t,
                ).wait_recv()

    spread_start(tok_ref, TK, 0)
    for layer in range(LAYERS):
        for item in range(6):
            local, remote = weight_copies(layer, item)
            local.start()
            if fused:
                remote.start()
    spread_start(cot_ref, CO, 1)

    def gather_copies(buf, ssem, rsem):
        return (
            rc(buf.at[t], buf.at[t], ssem.at[0], rsem.at[0], c, tc),
            rc(buf.at[t], buf.at[t], ssem.at[1], rsem.at[1], c, ty),
            rc(buf.at[ty], buf.at[ty], ssem.at[2], rsem.at[2], c, tc),
        )

    def gather_start(copies):
        copies[1].start()
        copies[0].start()

    def gather_remote(copies):
        copies[1].wait_recv()
        copies[2].start()
        copies[2].wait_recv()

    def gather_finish(copies):
        for copy in copies:
            copy.wait_send()

    def sum_copies(slot, lane):
        return (
            rc(SB.at[lane, 0], RB.at[slot, 0], rs_s.at[slot, 0], rs_r.at[slot, 0], c, tc),
            rc(SB.at[lane, 1], RB.at[slot, 1], rs_s.at[slot, 1], rs_r.at[slot, 1], c, ty),
            rc(SB.at[lane, 2], RB.at[slot, 2], rs_s.at[slot, 2], rs_r.at[slot, 2], c, tc),
        )

    def sum_remote(copies, pf, slot, lane):
        SB[lane, 0] = pf[(1 - y) * 2 + 1 - k].astype(BF16)
        copies[0].start()
        copies[0].wait_recv()
        SB[lane, 1] = (pf[ty] + RB[slot, 0].astype(F32)).astype(BF16)
        copies[1].start()

    def sum_local(copies, pf, slot, lane):
        SB[lane, 2] = pf[tc].astype(BF16)
        copies[2].start()

    def sum_finish(copies, pf, slot, lane):
        copies[2].wait_recv()
        partial = pf[t] + RB[slot, 2].astype(F32)
        copies[1].wait_recv()
        for copy in copies:
            copy.wait_send()
        return partial + RB[slot, 1].astype(F32)

    def full_vec(layer, row):
        return jnp.concatenate([VB[0, layer, row : row + 1], VB[1, layer, row : row + 1]], axis=1)

    def vec_at(layer, row, lanes):
        return VB[y, layer, pl.ds(row, 1)][:, :lanes]

    out_vec[...] = jnp.zeros_like(out_vec)

    def put_vec(layer, row, value):
        out_vec[layer, pl.ds(row, 1), : value.shape[1]] = value

    if fused:
        vec_copy.wait()
    spread_wait(tok_ref, TK, 0)
    H[...] = TK[...].astype(F32)
    lane_low = lax.broadcasted_iota(jnp.int32, (1, 2 * HD), 1) < HD

    def head_cols(value, head):
        if head == 2:
            return value[:, 2 * HD : 3 * HD]
        keep = lane_low if head == 0 else jnp.logical_not(lane_low)
        return jnp.where(keep, value[:, : 2 * HD], jnp.zeros_like(value[:, : 2 * HD]))

    def head_full(value, head):
        return value[:, 2 * HD : 3 * HD] if head == 2 else value[:, : 2 * HD]

    tile = own_rows // 2

    def forward_layer(layer, carry):
        buf = XB.at[layer]
        own = hf * 4
        far = (1 - hf) * 4
        ss, rr = g8_s.at[layer], g8_r.at[layer]
        XB[layer, own + t] = H[...].astype(BF16)
        to_y = rc(buf.at[own + t], buf.at[own + t], ss.at[0], rr.at[0], c, ty)
        to_z = rc(buf.at[own + t], buf.at[own + t], ss.at[1], rr.at[1], zp, t)
        to_c = rc(buf.at[own + t], buf.at[own + t], ss.at[2], rr.at[2], c, tc)
        y_to_c = rc(buf.at[own + ty], buf.at[own + ty], ss.at[3], rr.at[3], c, tc)
        z_to_y = rc(buf.at[far + t], buf.at[far + t], ss.at[4], rr.at[4], c, ty)
        z_to_c = rc(buf.at[far + t], buf.at[far + t], ss.at[5], rr.at[5], c, tc)
        zy_to_c = rc(buf.at[far + ty], buf.at[far + ty], ss.at[6], rr.at[6], c, tc)
        to_y.start()
        to_z.start()
        to_c.start()
        for item in range(3):
            weight_wait(layer, item)

        def project(at, with_q):
            block = XB[layer, pl.ds(at, 2)].reshape(2 * rows, width)
            where = pl.ds(pl.multiple_of(at * rows, 2 * rows), 2 * rows)
            if with_q:
                mine = pl.ds(pl.multiple_of((at - own) * rows, 2 * rows), 2 * rows)
                qb = vec_at(layer, k, cols)
                q_low = (nn(block, WQ[layer]) + qb).astype(BF16)
                Q[layer, mine] = q_low * jnp.asarray(HD**-0.5, BF16)
            K[layer, where] = nn(block, WK[layer]).astype(BF16)
            V[layer, where] = (nn(block, WV[layer]) + vec_at(layer, 2 + k, cols)).astype(BF16)

        to_c.wait_recv()
        project(own + 2 * y, True)
        to_z.wait_recv()
        z_to_y.start()
        z_to_c.start()
        to_y.wait_recv()
        y_to_c.start()
        y_to_c.wait_recv()
        project(own + 2 * (1 - y), True)
        z_to_c.wait_recv()
        project(far + 2 * y, False)
        z_to_y.wait_recv()
        zy_to_c.start()
        zy_to_c.wait_recv()
        project(far + 2 * (1 - y), False)
        for copy in (to_y, to_z, to_c, y_to_c, z_to_y, z_to_c, zy_to_c):
            copy.wait_send()

        def attend(at, inner):
            where = pl.ds(pl.multiple_of(at * tile, tile), tile)
            ids = idc_ref[where][:, :1] == idr_ref[:1]
            q_tile = Q[layer, where]
            mixed = []
            for head in range(3):
                scores = nt(head_cols(q_tile, head), head_full(K[layer], head))
                scores = jnp.where(ids, scores, NEG)
                top = jnp.max(scores, axis=-1, keepdims=True)
                expo = jnp.exp(scores - top)
                low = (expo / jnp.sum(expo, axis=-1, keepdims=True)).astype(BF16)
                PB[layer, head, where] = low
                mixed.append(nn(low, head_full(V[layer], head)))
            OB[layer, where, : 2 * HD] = jnp.where(lane_low, mixed[0], mixed[1]).astype(BF16)
            OB[layer, where, 2 * HD :] = mixed[2].astype(BF16)
            return inner

        lax.fori_loop(0, 2, attend, 0)
        weight_wait(layer, 3)

        def project_out(at):
            where = pl.ds(pl.multiple_of(at * 2 * rows, 2 * rows), 2 * rows)
            PF[pl.ds(at * 2, 2)] = nn(OB[layer, where], WO[layer]).reshape(2, rows, width)

        copies = sum_copies(0, 0)
        project_out(1 - y)
        sum_remote(copies, PF, 0, 0)
        project_out(y)
        sum_local(copies, PF, 0, 0)
        branch = sum_finish(copies, PF, 0, 0) + full_vec(layer, 4)
        normed, xhat, rstd = norm_forward(H[...] + branch, full_vec(layer, 6), full_vec(layer, 7))
        N1[...] = normed
        XH1[layer] = xhat
        SD1[layer] = jnp.broadcast_to(rstd, (rows, 128))

        N1B[layer, t] = normed.astype(BF16)
        moves = gather_copies(N1B.at[layer], g4_s.at[layer, 0], g4_r.at[layer, 0])
        gather_start(moves)
        weight_wait(layer, 4)
        weight_wait(layer, 5)

        def feed(at):
            where = pl.ds(pl.multiple_of(at * 2 * rows, 2 * rows), 2 * rows)
            block = N1B[layer, pl.ds(at * 2, 2)].reshape(2 * rows, width)
            bias = jnp.concatenate([vec_at(layer, 10 + 2 * k, half), vec_at(layer, 11 + 2 * k, half)], axis=1)
            pre = nn(block, WI[layer]) + bias
            phi = 0.5 * (1.0 + lax.erf(pre * (0.5**0.5)))
            low = (pre * phi).astype(BF16)
            G[layer, where] = low
            density = jnp.exp(pre * pre * -0.5) * ((0.5 / jnp.pi) ** 0.5)
            GP[layer, where] = (phi + pre * density).astype(GP.dtype)
            PF[pl.ds(at * 2, 2)] = nn(low, WU[layer]).reshape(2, rows, width)

        copies = sum_copies(1, 0)
        moves[0].wait_recv()
        feed(y)
        sum_local(copies, PF, 1, 0)
        gather_remote(moves)
        feed(1 - y)
        sum_remote(copies, PF, 1, 0)
        gather_finish(moves)
        second = N1[...] + sum_finish(copies, PF, 1, 0) + full_vec(layer, 5)
        result, xhat, rstd = norm_forward(second, full_vec(layer, 8), full_vec(layer, 9))
        XH2[layer] = xhat
        SD2[layer] = jnp.broadcast_to(rstd, (rows, 128))
        H[...] = result
        return carry

    for layer in range(LAYERS):
        forward_layer(layer, 0)

    TK[...] = H[...].astype(BF16)
    collect_start(TK, OT, 2)
    spread_wait(cot_ref, CO, 1)
    H[...] = CO[...].astype(F32)

    first_half = row_at if fused else 0
    other_half = pl.multiple_of((1 - s) * half, half) if fused else half

    def split_grad(a, b_ref_at, unit, step, count):
        for own_side in (True, False):
            at = first_half if own_side else other_half
            value = tn(a, b_ref_at(at)).astype(BF16)
            value = value.reshape(count, cols, half)
            if own_side:
                GO[pl.ds(unit, count)] = value
            elif fused:
                GS[pl.ds(step, count)] = value
            else:
                XR[pl.ds(unit, count)] = value

    def backward_layer(layer):
        base = (LAYERS - 1 - layer) * 12
        grad = H[...]
        xhat = XH2[layer]
        rstd = SD2[layer][:, :1]
        d_second = norm_backward(grad, xhat, rstd, full_vec(layer, 8))
        put_vec(layer, 4, jnp.sum(grad * xhat, axis=0, keepdims=True))
        put_vec(layer, 5, jnp.sum(grad, axis=0, keepdims=True))
        DR[...] = d_second
        DF[t] = d_second.astype(BF16)
        moves = gather_copies(DF, g4_s.at[layer, 1], g4_r.at[layer, 1])
        gather_start(moves)
        copies = sum_copies(2, 0)

        def back_feed(at):
            where = pl.ds(pl.multiple_of(at * 2 * rows, 2 * rows), 2 * rows)
            block = DF[pl.ds(at * 2, 2)].reshape(2 * rows, width)
            d_act = nt(block, WU[layer])
            low = (d_act * GP[layer, where].astype(F32)).astype(BF16)
            DU[where] = low
            PF[pl.ds(at * 2, 2)] = nt(low, WI[layer]).reshape(2, rows, width)

        moves[0].wait_recv()
        back_feed(y)
        sum_local(copies, PF, 2, 0)
        gather_remote(moves)
        back_feed(1 - y)
        sum_remote(copies, PF, 2, 0)
        gather_finish(moves)

        def halves(ref):
            return lambda at: ref[:, :, pl.ds(at, half)].reshape(-1, half)

        split_grad(G[layer], halves(DF), base, 0, 4)
        split_grad(DU[...], halves(N1B.at[layer]), base + 4, 4, 4)
        only = jnp.where(t == 0, 1.0, 0.0)
        put_vec(layer, 0, only * jnp.sum(DF[...].reshape(own_rows, width).astype(F32), axis=0, keepdims=True))
        put_vec(layer, 14 + t, jnp.sum(DU[...].astype(F32), axis=0, keepdims=True))

        d_normed = DR[...] + sum_finish(copies, PF, 2, 0)
        xhat = XH1[layer]
        d_first = norm_backward(d_normed, xhat, SD1[layer][:, :1], full_vec(layer, 6))
        put_vec(layer, 2, jnp.sum(d_normed * xhat, axis=0, keepdims=True))
        put_vec(layer, 3, jnp.sum(d_normed, axis=0, keepdims=True))
        DR1[...] = d_first
        DA[t] = d_first.astype(BF16)
        moves = gather_copies(DA, g4_s.at[layer, 2], g4_r.at[layer, 2])
        gather_start(moves)

        def back_out(at):
            where = pl.ds(pl.multiple_of(at * 2 * rows, 2 * rows), 2 * rows)
            block = DA[pl.ds(at * 2, 2)].reshape(2 * rows, width)
            DOB[where] = nt(block, WO[layer]).astype(BF16)

        moves[0].wait_recv()
        back_out(y)
        gather_remote(moves)
        back_out(1 - y)
        gather_finish(moves)
        split_grad(OB[layer], halves(DA), base + 8, 8, 1)
        put_vec(layer, 1, only * jnp.sum(DA[...].reshape(own_rows, width).astype(F32), axis=0, keepdims=True))

        DKF[...] = jnp.zeros_like(DKF)
        DVF[...] = jnp.zeros_like(DVF)

        def back_attend(at, inner):
            where = pl.ds(pl.multiple_of(at * tile, tile), tile)
            grad_tile = DOB[where]
            q_tile = Q[layer, where]
            product = grad_tile.astype(F32) * OB[layer, where].astype(F32)
            d_query = []
            for head in range(3):
                lanes = slice(2 * HD, 3 * HD) if head == 2 else slice(0, 2 * HD)
                d_mix = head_cols(grad_tile, head)
                d_prob = nt(d_mix, head_full(V[layer], head))
                total = jnp.sum(head_cols(product, head), axis=-1, keepdims=True)
                low = PB[layer, head, where]
                d_score = (low.astype(F32) * (d_prob - total)).astype(BF16)
                d_query.append(nn(d_score, head_full(K[layer], head)))
                DKF[:, lanes] += tn(d_score, head_cols(q_tile, head))
                DVF[:, lanes] += tn(low, d_mix)
            scale = HD**-0.5
            DQ[where, : 2 * HD] = (jnp.where(lane_low, d_query[0], d_query[1]) * scale).astype(BF16)
            DQ[where, 2 * HD :] = (d_query[2] * scale).astype(BF16)
            return inner

        lax.fori_loop(0, 2, back_attend, 0)
        DK[...] = DKF[...].astype(BF16)
        DV[...] = DVF[...].astype(BF16)
        own = hf * 4
        far = (1 - hf) * 4

        def back_in(at, with_q):
            where = pl.ds(pl.multiple_of(at * rows, 2 * rows), 2 * rows)
            total = nt(DK[where], WK[layer]) + nt(DV[where], WV[layer])
            if with_q:
                mine = pl.ds(pl.multiple_of((at - own) * rows, 2 * rows), 2 * rows)
                total = total + nt(DQ[mine], WQ[layer])
            PF[pl.ds(at, 2)] = total.reshape(2, rows, width)

        pf_far = PF.at[pl.ds(far, 4)]
        pf_own = PF.at[pl.ds(own, 4)]
        far_copies = sum_copies(3, 1)
        back_in(far + 2 * (1 - y), False)
        sum_remote(far_copies, pf_far, 3, 1)
        back_in(far + 2 * y, False)
        sum_local(far_copies, pf_far, 3, 1)
        copies = sum_copies(4, 0)
        back_in(own + 2 * (1 - y), True)
        sum_remote(copies, pf_own, 4, 0)
        back_in(own + 2 * y, True)
        sum_local(copies, pf_own, 4, 0)
        ZS[...] = sum_finish(far_copies, pf_far, 3, 1).astype(BF16)
        across = rc(ZS, ZR.at[layer], rz_s.at[layer], rz_r.at[layer], zp, t)
        across.start()

        def block_cols(ref, start, count):
            return lambda at: ref[pl.ds(start, count), :, pl.ds(at, half)].reshape(-1, half)

        xb = XB.at[layer]
        split_grad(DQ[...], block_cols(xb, own, 4), base + 9, 9, 1)
        split_grad(DK[...], block_cols(xb, 0, 8), base + 10, 10, 1)
        split_grad(DV[...], block_cols(xb, 0, 8), base + 11, 11, 1)
        put_vec(layer, 6 + t, jnp.sum(DQ[...].astype(F32), axis=0, keepdims=True))
        put_vec(layer, 10 + t, jnp.sum(DV[...].astype(F32), axis=0, keepdims=True))

        near = sum_finish(copies, pf_own, 4, 0)
        across.wait()
        H[...] = DR1[...] + near + ZR[layer].astype(F32)

    def x_copy(unit, step):
        return rc(GS.at[step], XR.at[unit], xs_s.at[unit], xs_r.at[unit], c, t, 1 - s)

    def z1_copy(unit):
        return rc(GO.at[unit], YR.at[unit], z1_s.at[unit], z1_r.at[unit], z_in, t)

    def z2_copy(unit):
        return rc(GO.at[unit], Y2.at[unit], z2_s.at[unit], z2_r.at[unit], z_mid, t)

    def z3_copy(unit):
        return rc(GO.at[unit], YR.at[unit], z3_s.at[unit], z3_r.at[unit], z_out, t)

    def add_into(unit, other):
        GO[unit] = (GO[unit].astype(F32) + other.astype(F32)).astype(BF16)

    def stage_x(unit, step):
        x_copy(unit, step).start()

    def stage_z1(unit, step):
        copy = x_copy(unit, step)
        copy.wait()
        add_into(unit, XR[unit])

        @pl.when(is_outer)
        def _():
            z1_copy(unit).start()

    def stage_z2(unit):
        @pl.when(is_inner)
        def _():
            z1_copy(unit).wait_recv()
            add_into(unit, YR[unit])
            z2_copy(unit).start()

        @pl.when(is_outer)
        def _():
            z1_copy(unit).wait_send()

    def stage_z3(unit):
        @pl.when(is_inner)
        def _():
            z2_copy(unit).wait()
            add_into(unit, Y2[unit])
            z3_copy(unit).start()

    def stage_out(unit):
        @pl.when(is_inner)
        def _():
            z3_copy(unit).wait_send()
            pltpu.make_async_copy(GO.at[unit], out_mat.at[unit], om_sem.at[unit]).start()

        @pl.when(is_outer)
        def _():
            z3_copy(unit).wait_recv()
            pltpu.make_async_copy(YR.at[unit], out_mat.at[unit], om_sem.at[unit]).start()

    for layer in reversed(range(LAYERS)):
        backward_layer(layer)
        if fused:
            base = (LAYERS - 1 - layer) * 12

            def x_all(i, carry):
                stage_x(base + i, i)
                return carry

            def z1_all(i, carry):
                stage_z1(base + i, i)
                return carry

            lax.fori_loop(0, 12, x_all, 0)
            lax.fori_loop(0, 12, z1_all, 0)

    TK2 = CO
    TK2[...] = H[...].astype(BF16)
    collect_start(TK2, OG, 3)
    total_units = 12 * LAYERS
    if fused:
        for stage in (stage_z2, stage_z3, stage_out):

            def run(i, carry, stage=stage):
                stage(i)
                return carry

            lax.fori_loop(0, total_units, run, 0)

        def drain(i, carry):
            pltpu.make_async_copy(GO.at[i], out_mat.at[i], om_sem.at[i]).wait()
            return carry

        lax.fori_loop(0, total_units, drain, 0)
    else:
        own_out = pltpu.make_async_copy(GO, out_mat.at[0], om_sem.at[0])
        far_out = pltpu.make_async_copy(XR, out_mat.at[1], om_sem.at[1])
        own_out.start()
        far_out.start()
        own_out.wait()
        far_out.wait()
    collect_wait(TK, OT, 2)
    out_tok[...] = OT[...]
    collect_wait(TK2, OG, 3)
    out_grad[...] = OG[...]


def pack_vectors(qb, vb, ob, ub, ib, g1, s1, g2, s2, cols, half):
    def narrow(vec):
        two = vec.astype(F32).reshape(LAYERS, -1, cols)
        return jnp.pad(two, ((0, 0), (0, 0), (0, half - cols)))

    def wide(vec):
        return vec.astype(F32).reshape(LAYERS, -1, half)

    packed = jnp.concatenate(
        [narrow(qb), narrow(vb), wide(ob), wide(ub), wide(g1), wide(s1), wide(g2), wide(s2), wide(ib)], axis=1
    )
    return jnp.pad(packed, ((0, 0), (0, 16 - packed.shape[1]), (0, 0)))


def per_device(
    tokens,
    cotangent,
    segment_ids,
    lengths,
    query_weight,
    key_weight,
    value_weight,
    output_weight,
    inner_weight,
    outer_weight,
    query_bias,
    value_bias,
    output_bias,
    inner_bias,
    outer_bias,
    first_gain,
    first_shift,
    second_gain,
    second_shift,
):
    shards = lax.axis_size("shard")
    assert lax.axis_size("ctx") == 4 and lax.axis_size("tp") == 4 and tokens.shape[0] == 2
    fused = shards == 2
    seqs, part, width = tokens.shape
    cols = query_weight.shape[2]
    units = inner_weight.shape[2]
    half = width // 2
    rows = 2 * part
    own_rows, all_rows = 4 * rows, 8 * rows
    assert cols == 3 * HD and segment_ids.shape[1] == all_rows and units == width == 4 * cols

    c = lax.axis_index("ctx")
    positions = lax.broadcasted_iota(jnp.int32, segment_ids.shape, 1)
    key_ids = jnp.where(positions < lengths[:, None], segment_ids, -1)
    seq_ids = lax.dynamic_index_in_dim(key_ids, c // 2, 0, keepdims=False)
    row_ids = jnp.broadcast_to(seq_ids[None, :], (8, all_rows))
    own_ids = lax.dynamic_slice_in_dim(seq_ids, lax.rem(c, 2) * own_rows, own_rows)
    col_ids = jnp.broadcast_to(own_ids[:, None], (own_rows, 128))

    mats = (query_weight, key_weight, value_weight, output_weight, inner_weight, outer_weight)
    vecs = (query_bias, value_bias, output_bias, outer_bias, inner_bias, first_gain, first_shift, second_gain, second_shift)
    if fused:
        vec_in = pack_vectors(*vecs, cols, half)
    else:
        mats = tuple(
            lax.all_gather(mat, "shard", axis=axis, tiled=True) for mat, axis in zip(mats, (1, 1, 1, 2, 1, 2))
        )
        full = [lax.all_gather(vec, "shard", axis=1, tiled=True) for vec in vecs]
        vec_in = jnp.stack(
            [
                pack_vectors(*[vec.reshape(LAYERS, 2, -1)[:, side] for vec in full], cols, half)
                for side in range(2)
            ]
        )

    n_units = 12 * LAYERS
    out_shape = [
        jax.ShapeDtypeStruct((2, part, width), BF16),
        jax.ShapeDtypeStruct((2, part, width), BF16),
        jax.ShapeDtypeStruct((n_units, cols, half) if fused else (2, n_units, cols, half), BF16),
        jax.ShapeDtypeStruct((LAYERS, VEC_ROWS, width), F32),
    ]
    vm = pltpu.VMEM
    dma = pltpu.SemaphoreType.DMA
    scratch = [
        vm((LAYERS, width, cols), BF16),
        vm((LAYERS, width, cols), BF16),
        vm((LAYERS, width, cols), BF16),
        vm((LAYERS, cols, width), BF16),
        vm((LAYERS, width, units), BF16),
        vm((LAYERS, units, width), BF16),
        vm((2, LAYERS, 16, half), F32),
        vm((rows, width), F32),
        vm((rows, width), F32),
        vm((rows, width), F32),
        vm((rows, width), F32),
        vm((rows, width), BF16),
        vm((rows, width), BF16),
        vm((2, part, width), BF16),
        vm((2, part, width), BF16),
        vm((LAYERS, rows, width), F32),
        vm((LAYERS, rows, width), F32),
        vm((LAYERS, rows, 128), F32),
        vm((LAYERS, rows, 128), F32),
        vm((LAYERS, 8, rows, width), BF16),
        vm((LAYERS, own_rows, cols), BF16),
        vm((LAYERS, all_rows, cols), BF16),
        vm((LAYERS, all_rows, cols), BF16),
        vm((LAYERS, own_rows, cols), BF16),
        vm((LAYERS, 4, rows, width), BF16),
        vm((LAYERS, own_rows, units), BF16),
        vm((LAYERS, own_rows, units), BF16),
        vm((LAYERS, 3, own_rows, all_rows), BF16),
        vm((4, rows, width), BF16),
        vm((4, rows, width), BF16),
        vm((own_rows, units), BF16),
        vm((own_rows, cols), BF16),
        vm((own_rows, cols), BF16),
        vm((all_rows, cols), BF16),
        vm((all_rows, cols), BF16),
        vm((all_rows, cols), F32),
        vm((all_rows, cols), F32),
        vm((8, rows, width), F32),
        vm((2, 3, rows, width), BF16),
        vm((5, 3, rows, width), BF16),
        vm((rows, width), BF16),
        vm((LAYERS, rows, width), BF16),
        vm((n_units, cols, half), BF16),
        vm((12, cols, half), BF16),
        vm((n_units, cols, half), BF16),
        vm((n_units, cols, half), BF16),
        vm((n_units, cols, half), BF16),
        dma((LAYERS, 7)),
        dma((LAYERS, 7)),
        dma((LAYERS, 7)),
        dma((4, 2)),
        dma((4, 2)),
        dma((LAYERS, 7)),
        dma((LAYERS, 7)),
        dma((LAYERS, 3, 3)),
        dma((LAYERS, 3, 3)),
        dma((5, 3)),
        dma((5, 3)),
        dma((LAYERS,)),
        dma((LAYERS,)),
        dma((n_units,)),
        dma((n_units,)),
        dma((n_units,)),
        dma((n_units,)),
        dma((n_units,)),
        dma((n_units,)),
        dma((n_units,)),
        dma((n_units,)),
        dma((n_units,)),
    ]
    vmem = pl.BlockSpec(memory_space=pltpu.VMEM)
    hbm = pl.BlockSpec(memory_space=pl.ANY)
    layer_out, grad_tokens, grad_mats, grad_vecs = pl.pallas_call(
        functools.partial(step_kernel, (width, cols, units, half), fused),
        out_shape=out_shape,
        in_specs=[vmem] * 5 + [hbm] * 6,
        out_specs=[vmem, vmem, hbm, vmem],
        scratch_shapes=scratch,
        compiler_params=pltpu.CompilerParams(
            collective_id=0, has_side_effects=True, vmem_limit_bytes=67043328
        ),
        name="encoder_step",
    )(tokens, cotangent, col_ids, row_ids, vec_in, *mats)

    if not fused:
        both = jnp.concatenate([grad_mats[0], grad_mats[1]], axis=-1)
        both = lax.psum_scatter(both, "shard", scatter_dimension=2, tiled=True)
        grad_mats = lax.psum(both, "ctx")
    keep = grad_mats.shape[-1]
    units_of = grad_mats.reshape(LAYERS, 12, cols, keep)[::-1]

    def flip(block):
        return jnp.swapaxes(block, 1, 2).astype(F32)

    grad_outer = units_of[:, 0:4].reshape(LAYERS, units, keep).astype(F32)
    grad_inner = flip(units_of[:, 4:8].reshape(LAYERS, units, keep))
    grad_output = units_of[:, 8].astype(F32)
    grad_query, grad_key, grad_value = (flip(units_of[:, 9 + at]) for at in range(3))

    total = lax.psum(grad_vecs, ("shard", "ctx", "tp"))
    at = lax.axis_index("shard")

    def owned(vec):
        count = vec.shape[1] // shards
        return lax.dynamic_slice_in_dim(vec, at * count, count, 1)

    vec_query = owned(total[:, 6:10, :cols].reshape(LAYERS, -1))
    vec_value = owned(total[:, 10:14, :cols].reshape(LAYERS, -1))
    vec_inner = owned(total[:, 14:18].reshape(LAYERS, -1))
    vec_outer, vec_output, gain_one, shift_one, gain_two, shift_two = (owned(total[:, row]) for row in range(6))
    return (
        layer_out,
        grad_tokens.astype(F32),
        grad_query,
        grad_key,
        grad_value,
        grad_output,
        grad_inner,
        grad_outer,
        vec_query,
        vec_value,
        vec_output,
        vec_inner,
        vec_outer,
        gain_one,
        shift_one,
        gain_two,
        shift_two,
    )


def solution(mesh):
    rows = P("shard", ("ctx", "tp"), None)
    down = P(None, "shard", "tp")
    across = P(None, "tp", "shard")
    vector = P(None, "shard")
    mats = (down, down, down, across, down, across)
    return jax.shard_map(
        per_device,
        mesh=mesh,
        in_specs=(rows, rows, P("shard", None), P("shard")) + mats + (vector,) * 9,
        out_specs=(rows, rows) + mats + (vector,) * 9,
        check_vma=False,
    )
```

```python
import functools

import jax
import jax.numpy as jnp
from jax import lax
from jax.experimental import pallas as pl
from jax.experimental.pallas import tpu as pltpu
from jax.sharding import PartitionSpec as P

HD = 64
LAYERS = 2
EPSILON = 1e-05
MESH = pl.DeviceIdType.MESH
F32 = jnp.float32
BF16 = jnp.bfloat16
NEG = -1e30
VEC_ROWS = 24
LAGS = (4, 6, 8, 10)


def nn(a, b):
    return jnp.dot(a, b, preferred_element_type=F32)


def nt(a, b):
    return lax.dot_general(a, b, (((1,), (1,)), ((), ())), preferred_element_type=F32)


def tn(a, b):
    return lax.dot_general(a, b, (((0,), (0,)), ((), ())), preferred_element_type=F32)


def norm_forward(resid, gain, shift):
    center = resid - jnp.mean(resid, axis=-1, keepdims=True)
    spread = jnp.mean(center * center, axis=-1, keepdims=True)
    rstd = lax.rsqrt(spread + EPSILON)
    xhat = center * rstd
    return xhat * gain + shift, xhat, rstd


def norm_backward(grad, xhat, rstd, gain):
    scaled = grad * gain
    first = jnp.mean(scaled, axis=-1, keepdims=True)
    second = jnp.mean(scaled * xhat, axis=-1, keepdims=True)
    return rstd * (scaled - first - xhat * second)


def step_kernel(dims, fused, *refs):
    (
        tok_ref,
        cot_ref,
        seg_ref,
        vec_refs,
        len_ref,
        wq_ref,
        wk_ref,
        wv_ref,
        wo_ref,
        wi_ref,
        wu_ref,
        out_tok,
        out_grad,
        out_mat,
        out_vec,
        WQ,
        WO,
        WI,
        WU,
        VB,
        IDC,
        IDR,
        H,
        N1,
        DR,
        DR1,
        TK,
        CO,
        OT,
        OG,
        XH1,
        XH2,
        SD1,
        SD2,
        XB,
        Q,
        K,
        V,
        OB,
        N1B,
        G,
        GP,
        PB,
        DF,
        DA,
        DU,
        DOB,
        DQ,
        DK,
        DV,
        DKF,
        DVF,
        PF,
        SB,
        RB,
        ZS,
        ZR,
        GO,
        GS,
        XR,
        YR,
        Y2,
        OV,
        VR,
        wl_sem,
        ws_sem,
        wr_sem,
        wz_s,
        wz_r,
        v_s,
        v_r,
        rd_s,
        rd_r,
        g8_s,
        g8_r,
        g4_s,
        g4_r,
        rs_s,
        rs_r,
        rz_s,
        rz_r,
        xs_s,
        xs_r,
        z1_s,
        z1_r,
        z2_s,
        z2_r,
        z3_s,
        z3_r,
        om_sem,
    ) = refs[:3] + (refs[3:12],) + refs[12:]
    width, cols, units, half = dims
    seqs, part = tok_ref.shape[0], tok_ref.shape[1]
    rows = 2 * part
    own_rows = 4 * rows
    all_rows = 8 * rows
    s = lax.axis_index("shard")
    c = lax.axis_index("ctx")
    t = lax.axis_index("tp")
    hf = lax.rem(c, 2)
    y = t // 2
    k = lax.rem(t, 2)
    tc = t + 1 - 2 * k
    ty = lax.rem(t + 2, 4)
    zp = c + 1 - 2 * hf
    is_inner = jnp.logical_or(c == 1, c == 2)
    is_outer = jnp.logical_not(is_inner)
    z_in = jnp.where(c == 0, 1, 2)
    z_mid = 3 - c
    z_out = jnp.where(c == 1, 0, 3)

    def rc(src, dst, ssem, rsem, cc, tt, ss=None):
        return pltpu.make_async_remote_copy(
            src_ref=src,
            dst_ref=dst,
            send_sem=ssem,
            recv_sem=rsem,
            device_id=(s if ss is None else ss, cc, tt),
            device_id_type=MESH,
        )

    bar = pltpu.get_barrier_semaphore()
    for dc in range(4):
        for dt in range(4):
            if dc or dt:
                pl.semaphore_signal(
                    bar,
                    1,
                    device_id=(s, lax.rem(c + dc, 4), lax.rem(t + dt, 4)),
                    device_id_type=MESH,
                )
    if fused:
        pl.semaphore_signal(bar, 1, device_id=(1 - s, c, t), device_id_type=MESH)
    pl.semaphore_wait(bar, 16 if fused else 15)

    def unit_view(layer, item, side):
        at = pl.multiple_of(side * half, half)
        lanes = pl.ds(at, half)
        if item < 3:
            return WQ.at[layer, pl.ds(item * cols, cols), lanes]
        if item == 3:
            return WO.at[layer, :, lanes]
        if item < 8:
            return WI.at[layer, pl.ds(at + (item - 4) * (half // 4), half // 4)]
        return WU.at[layer, pl.ds((item - 8) * cols, cols), lanes]

    def unit_arg(layer, item):
        if item < 4:
            return (wq_ref, wk_ref, wv_ref, wo_ref)[item].at[layer]
        if item < 8:
            return wi_ref.at[layer, pl.ds((item - 4) * (half // 4), half // 4)]
        return wu_ref.at[layer, pl.ds((item - 8) * cols, cols)]

    def local_copy(layer, item):
        lanes = pl.ds(pl.multiple_of(s * half, half), half) if fused else pl.ds(0, width)
        if item < 3:
            src, dst = (wq_ref, wk_ref, wv_ref)[item], WQ.at[layer, pl.ds(item * cols, cols), lanes]
        elif item == 3:
            src, dst = wo_ref, WO.at[layer, :, lanes]
        elif item == 4:
            src, dst = wi_ref, WI.at[layer, lanes]
        else:
            src, dst = wu_ref, WU.at[layer, :, lanes]
        return pltpu.make_async_copy(src.at[layer], dst, wl_sem.at[layer, item])

    def over_x(layer, item):
        return rc(
            unit_arg(layer, item),
            unit_view(layer, item, s),
            ws_sem.at[layer, item],
            wr_sem.at[layer, item],
            c,
            t,
            1 - s,
        )

    def over_z(layer, item):
        view = unit_view(layer, item, 1 - s)
        return rc(view, view, wz_s.at[layer, item], wz_r.at[layer, item], zp, t)

    def direct(layer, item):
        return jnp.logical_and(layer == 0, item < 4)

    def mine_over_x(layer, item):
        return jnp.logical_or(direct(layer, item), hf == item % 2)

    def fetch_start(layer, item):
        @pl.when(mine_over_x(layer, item))
        def _():
            over_x(layer, item).start()

    def fetch_pass(layer, items):
        if fused:
            for item in items:

                @pl.when(hf == item % 2)
                def _():
                    over_x(layer, item).wait_recv()
                    over_z(layer, item).start()

    def fetch_wait(layer, items):
        for item in items:
            local_copy(layer, {0: 0, 1: 1, 2: 2, 3: 3, 4: 4, 8: 5}[item]).wait() if item in (0, 1, 2, 3, 4, 8) else None
            if fused:

                @pl.when(direct(layer, item))
                def _():
                    over_x(layer, item).wait_recv()

                @pl.when(jnp.logical_not(mine_over_x(layer, item)))
                def _():
                    over_z(layer, item).wait_recv()

    def fetch_drain(layer):
        for item in range(12):

            @pl.when(mine_over_x(layer, item))
            def _():
                over_x(layer, item).wait_send()

            @pl.when(jnp.logical_and(hf == item % 2, jnp.logical_not(direct(layer, item))))
            def _():
                over_z(layer, item).wait_send()

    def fill_vectors(side, at):
        for layer in range(LAYERS):
            for place, ref in ((0, vec_refs[0]), (2, vec_refs[1])):
                value = ref[...].astype(F32)[layer : layer + 1, at : at + half]
                VB[side, layer, place : place + 1, :cols] = value[:, :cols]
                VB[side, layer, place + 1 : place + 2, :cols] = value[:, cols:]
            for place, ref in zip((4, 5, 6, 7, 8, 9), vec_refs[2:4] + vec_refs[5:9]):
                VB[side, layer, place : place + 1] = ref[...].astype(F32)[layer : layer + 1, at : at + half]
            value = vec_refs[4][...].astype(F32)[layer : layer + 1, 4 * at : 4 * at + 4 * half]
            for j in range(4):
                VB[side, layer, 10 + j : 11 + j] = value[:, j * half : (j + 1) * half]

    if fused:
        fill_vectors(s, 0)
        vec_copy = rc(VB.at[s], VB.at[s], ws_sem.at[0, 12], wr_sem.at[0, 12], c, t, 1 - s)
        vec_copy.start()
    else:
        fill_vectors(0, 0)
        fill_vectors(1, half)

    b_me = c // 2
    spread_t = 2 * hf + y

    def spread_copies(src_ref, dst_ref, which):
        return [
            (
                jnp.logical_and(2 * b + c // 2 == c, spread_t == t),
                rc(
                    src_ref.at[b],
                    dst_ref.at[pl.ds(k * part, part)],
                    rd_s.at[which, b],
                    rd_r.at[which, k],
                    2 * b + c // 2,
                    spread_t,
                ),
            )
            for b in range(2)
        ]

    def spread_start(src_ref, dst_ref, which):
        for b, (mine, copy) in enumerate(spread_copies(src_ref, dst_ref, which)):

            @pl.when(mine)
            def _():
                dst_ref[pl.ds(pl.multiple_of(k * part, part), part), :] = src_ref[b]

            @pl.when(jnp.logical_not(mine))
            def _():
                copy.start()

    def spread_wait(src_ref, dst_ref, which):
        for mine, copy in spread_copies(src_ref, dst_ref, which):

            @pl.when(jnp.logical_not(mine))
            def _():
                copy.wait_send()

        for kk in range(2):
            mine = jnp.logical_and(2 * hf + y == c, 2 * k + kk == t)

            @pl.when(jnp.logical_not(mine))
            def _():
                rc(
                    src_ref.at[0],
                    dst_ref.at[pl.ds(kk * part, part)],
                    rd_s.at[which, 0],
                    rd_r.at[which, kk],
                    c,
                    t,
                ).wait_recv()

    def collect_copies(src_ref, dst_ref, which):
        return [
            (
                jnp.logical_and(2 * hf + y == c, 2 * k + kk == t),
                rc(
                    src_ref.at[pl.ds(kk * part, part)],
                    dst_ref.at[b_me],
                    rd_s.at[which, kk],
                    rd_r.at[which, b_me],
                    2 * hf + y,
                    2 * k + kk,
                ),
            )
            for kk in range(2)
        ]

    def collect_start(src_ref, dst_ref, which):
        for kk, (mine, copy) in enumerate(collect_copies(src_ref, dst_ref, which)):

            @pl.when(mine)
            def _():
                dst_ref[b_me] = src_ref[kk * part : (kk + 1) * part, :]

            @pl.when(jnp.logical_not(mine))
            def _():
                copy.start()

    def collect_wait(src_ref, dst_ref, which):
        for mine, copy in collect_copies(src_ref, dst_ref, which):

            @pl.when(jnp.logical_not(mine))
            def _():
                copy.wait_send()

        for b in range(2):
            mine = jnp.logical_and(2 * b + c // 2 == c, spread_t == t)

            @pl.when(jnp.logical_not(mine))
            def _():
                rc(
                    src_ref.at[pl.ds(0, part)],
                    dst_ref.at[b],
                    rd_s.at[which, 0],
                    rd_r.at[which, b],
                    c,
                    t,
                ).wait_recv()

    spread_start(tok_ref, TK, 0)
    for layer in range(LAYERS):
        if fused:
            for item in range(12):
                fetch_start(layer, item)
        for item in range(6):
            local_copy(layer, item).start()
    spread_start(cot_ref, CO, 1)

    ids = seg_ref[pl.ds(b_me, 1)]
    places = lax.broadcasted_iota(jnp.int32, ids.shape, 1)
    ids = jnp.where(places < len_ref[b_me], ids, -1).astype(F32)
    IDR[...] = jnp.broadcast_to(ids, IDR.shape)
    own_ids = jnp.where(hf == 0, ids[:, :own_rows], ids[:, own_rows:])
    IDC[...] = jnp.broadcast_to(own_ids, (128, own_rows)).T

    def gather_copies(buf, ssem, rsem):
        return (
            rc(buf.at[t], buf.at[t], ssem.at[0], rsem.at[0], c, tc),
            rc(buf.at[t], buf.at[t], ssem.at[1], rsem.at[1], c, ty),
            rc(buf.at[ty], buf.at[ty], ssem.at[2], rsem.at[2], c, tc),
        )

    def gather_start(copies):
        copies[1].start()
        copies[0].start()

    def gather_remote(copies):
        copies[1].wait_recv()
        copies[2].start()
        copies[2].wait_recv()

    def gather_finish(copies):
        for copy in copies:
            copy.wait_send()

    def sum_copies(slot, lane):
        return (
            rc(SB.at[lane, 0], RB.at[slot, 0], rs_s.at[slot, 0], rs_r.at[slot, 0], c, tc),
            rc(SB.at[lane, 1], RB.at[slot, 1], rs_s.at[slot, 1], rs_r.at[slot, 1], c, ty),
            rc(SB.at[lane, 2], RB.at[slot, 2], rs_s.at[slot, 2], rs_r.at[slot, 2], c, tc),
        )

    def sum_remote(copies, pf, slot, lane):
        SB[lane, 0] = pf[(1 - y) * 2 + 1 - k].astype(BF16)
        copies[0].start()
        copies[0].wait_recv()
        SB[lane, 1] = (pf[ty] + RB[slot, 0].astype(F32)).astype(BF16)
        copies[1].start()

    def sum_local(copies, pf, slot, lane):
        SB[lane, 2] = pf[tc].astype(BF16)
        copies[2].start()

    def sum_finish(copies, pf, slot, lane):
        copies[2].wait_recv()
        partial = pf[t] + RB[slot, 2].astype(F32)
        copies[1].wait_recv()
        for copy in copies:
            copy.wait_send()
        return partial + RB[slot, 1].astype(F32)

    def full_vec(layer, row):
        return jnp.concatenate([VB[0, layer, row : row + 1], VB[1, layer, row : row + 1]], axis=1)

    def vec_at(layer, row, lanes):
        return VB[y, layer, pl.ds(row, 1)][:, :lanes]

    OV[...] = jnp.zeros_like(OV)

    def put_vec(layer, row, value):
        OV[layer, pl.ds(row, 1), : value.shape[1]] = value

    if fused:
        vec_copy.wait()
    spread_wait(tok_ref, TK, 0)
    H[...] = TK[...].astype(F32)
    lane_low = lax.broadcasted_iota(jnp.int32, (1, 2 * HD), 1) < HD

    def head_cols(value, head):
        if head == 2:
            return value[:, 2 * HD : 3 * HD]
        keep = lane_low if head == 0 else jnp.logical_not(lane_low)
        return jnp.where(keep, value[:, : 2 * HD], jnp.zeros_like(value[:, : 2 * HD]))

    def head_full(value, head):
        return value[:, 2 * HD : 3 * HD] if head == 2 else value[:, : 2 * HD]

    tile = own_rows // 2

    def forward_layer(layer, carry):
        buf = XB.at[layer]
        own = hf * 4
        far = (1 - hf) * 4
        ss, rr = g8_s.at[layer], g8_r.at[layer]
        XB[layer, own + t] = H[...].astype(BF16)
        to_y = rc(buf.at[own + t], buf.at[own + t], ss.at[0], rr.at[0], c, ty)
        to_z = rc(buf.at[own + t], buf.at[own + t], ss.at[1], rr.at[1], zp, t)
        to_c = rc(buf.at[own + t], buf.at[own + t], ss.at[2], rr.at[2], c, tc)
        y_to_c = rc(buf.at[own + ty], buf.at[own + ty], ss.at[3], rr.at[3], c, tc)
        z_to_y = rc(buf.at[far + t], buf.at[far + t], ss.at[4], rr.at[4], c, ty)
        z_to_c = rc(buf.at[far + t], buf.at[far + t], ss.at[5], rr.at[5], c, tc)
        zy_to_c = rc(buf.at[far + ty], buf.at[far + ty], ss.at[6], rr.at[6], c, tc)
        to_y.start()
        to_z.start()
        to_c.start()
        fetch_wait(layer, (0, 1, 2))

        def project(at, with_q):
            block = XB[layer, pl.ds(at, 2)].reshape(2 * rows, width)
            where = pl.ds(pl.multiple_of(at * rows, 2 * rows), 2 * rows)
            if with_q:
                mine = pl.ds(pl.multiple_of((at - own) * rows, 2 * rows), 2 * rows)
                qb = vec_at(layer, k, cols)
                q_low = (nt(block, WQ[layer, :cols]) + qb).astype(BF16)
                Q[layer, mine] = q_low * jnp.asarray(HD**-0.5, BF16)
            K[layer, where] = nt(block, WQ[layer, cols : 2 * cols]).astype(BF16)
            V[layer, where] = (nt(block, WQ[layer, 2 * cols :]) + vec_at(layer, 2 + k, cols)).astype(BF16)

        to_c.wait_recv()
        project(own + 2 * y, True)
        to_z.wait_recv()
        z_to_y.start()
        z_to_c.start()
        to_y.wait_recv()
        y_to_c.start()
        y_to_c.wait_recv()
        project(own + 2 * (1 - y), True)
        z_to_c.wait_recv()
        project(far + 2 * y, False)
        z_to_y.wait_recv()
        zy_to_c.start()
        zy_to_c.wait_recv()
        project(far + 2 * (1 - y), False)
        for copy in (to_y, to_z, to_c, y_to_c, z_to_y, z_to_c, zy_to_c):
            copy.wait_send()

        def attend(at, inner):
            where = pl.ds(pl.multiple_of(at * tile, tile), tile)
            ids = IDC[where][:, :1] == IDR[:1]
            q_tile = Q[layer, where]
            mixed = []
            for head in range(3):
                scores = nt(head_cols(q_tile, head), head_full(K[layer], head))
                scores = jnp.where(ids, scores, NEG)
                top = jnp.max(scores, axis=-1, keepdims=True)
                expo = jnp.exp(scores - top)
                low = (expo / jnp.sum(expo, axis=-1, keepdims=True)).astype(BF16)
                PB[layer, head, where] = low
                mixed.append(nn(low, head_full(V[layer], head)))
            OB[layer, where, : 2 * HD] = jnp.where(lane_low, mixed[0], mixed[1]).astype(BF16)
            OB[layer, where, 2 * HD :] = mixed[2].astype(BF16)
            return inner

        lax.fori_loop(0, 2, attend, 0)
        fetch_wait(layer, (3,))

        def project_out(at):
            where = pl.ds(pl.multiple_of(at * 2 * rows, 2 * rows), 2 * rows)
            PF[pl.ds(at * 2, 2)] = nn(OB[layer, where], WO[layer]).reshape(2, rows, width)

        copies = sum_copies(0, 0)
        project_out(1 - y)
        sum_remote(copies, PF, 0, 0)
        project_out(y)
        sum_local(copies, PF, 0, 0)
        fetch_pass(layer, (4, 5, 6, 7))
        branch = sum_finish(copies, PF, 0, 0) + full_vec(layer, 4)
        normed, xhat, rstd = norm_forward(H[...] + branch, full_vec(layer, 6), full_vec(layer, 7))
        N1[...] = normed
        XH1[layer] = xhat
        SD1[layer] = jnp.broadcast_to(rstd, (rows, 128))

        N1B[layer, t] = normed.astype(BF16)
        moves = gather_copies(N1B.at[layer], g4_s.at[layer, 0], g4_r.at[layer, 0])
        gather_start(moves)
        fetch_pass(layer, (8, 9, 10, 11))
        fetch_wait(layer, (4, 5, 6, 7))

        def feed(at):
            where = pl.ds(pl.multiple_of(at * 2 * rows, 2 * rows), 2 * rows)
            block = N1B[layer, pl.ds(at * 2, 2)].reshape(2 * rows, width)
            bias = jnp.concatenate([vec_at(layer, 10 + 2 * k, half), vec_at(layer, 11 + 2 * k, half)], axis=1)
            pre = nn(block, WI[layer]) + bias
            phi = 0.5 * (1.0 + lax.erf(pre * (0.5**0.5)))
            low = (pre * phi).astype(BF16)
            G[layer, where] = low
            density = jnp.exp(pre * pre * -0.5) * ((0.5 / jnp.pi) ** 0.5)
            GP[layer, where] = (phi + pre * density).astype(GP.dtype)
            PF[pl.ds(at * 2, 2)] = nn(low, WU[layer]).reshape(2, rows, width)

        copies = sum_copies(1, 0)
        moves[0].wait_recv()
        fetch_wait(layer, (8, 9, 10, 11))
        feed(y)
        sum_local(copies, PF, 1, 0)
        gather_remote(moves)
        feed(1 - y)
        sum_remote(copies, PF, 1, 0)
        gather_finish(moves)

        @pl.when(layer == 0)
        def _():
            fetch_pass(1, (0, 1, 2, 3))

        second = N1[...] + sum_finish(copies, PF, 1, 0) + full_vec(layer, 5)
        result, xhat, rstd = norm_forward(second, full_vec(layer, 8), full_vec(layer, 9))
        XH2[layer] = xhat
        SD2[layer] = jnp.broadcast_to(rstd, (rows, 128))
        H[...] = result
        return carry

    lax.fori_loop(0, LAYERS, forward_layer, 0)

    TK[...] = H[...].astype(BF16)
    collect_start(TK, OT, 2)
    spread_wait(cot_ref, CO, 1)
    H[...] = CO[...].astype(F32)

    total_units = 12 * LAYERS

    def x_copy(unit):
        return rc(GS.at[lax.rem(unit, 12)], XR.at[unit], xs_s.at[unit], xs_r.at[unit], c, t, 1 - s)

    def z1_copy(unit):
        return rc(GO.at[unit], YR.at[unit], z1_s.at[unit], z1_r.at[unit], z_in, t)

    def z2_copy(unit):
        return rc(GO.at[unit], Y2.at[unit], z2_s.at[unit], z2_r.at[unit], z_mid, t)

    def z3_copy(unit):
        return rc(GO.at[unit], YR.at[unit], z3_s.at[unit], z3_r.at[unit], z_out, t)

    def add_into(unit, other):
        GO[unit] = (GO[unit].astype(F32) + other.astype(F32)).astype(BF16)

    def stage_z1(unit):
        x_copy(unit).wait()
        add_into(unit, XR[unit])

        @pl.when(is_outer)
        def _():
            z1_copy(unit).start()

    def stage_z2(unit):
        @pl.when(is_inner)
        def _():
            z1_copy(unit).wait_recv()
            add_into(unit, YR[unit])
            z2_copy(unit).start()

        @pl.when(is_outer)
        def _():
            z1_copy(unit).wait_send()

    def stage_z3(unit):
        @pl.when(is_inner)
        def _():
            z2_copy(unit).wait()
            add_into(unit, Y2[unit])
            z3_copy(unit).start()

    def stage_out(unit):
        @pl.when(is_inner)
        def _():
            z3_copy(unit).wait_send()
            pltpu.make_async_copy(GO.at[unit], out_mat.at[unit], om_sem.at[unit]).start()

        @pl.when(is_outer)
        def _():
            z3_copy(unit).wait_recv()
            pltpu.make_async_copy(YR.at[unit], out_mat.at[unit], om_sem.at[unit]).start()

    stages = ((stage_out, LAGS[3]), (stage_z3, LAGS[2]), (stage_z2, LAGS[1]), (stage_z1, LAGS[0]))

    def advance(tick):
        for stage, lag in stages:
            unit = tick - lag

            @pl.when(jnp.logical_and(unit >= 0, unit < total_units))
            def _(stage=stage, unit=unit):
                stage(unit)

    def vec_step(layer, at):
        partner = (
            (s, c, tc),
            (s, c, ty),
            (1 - s, c, t),
            (s, zp, t),
            (s, lax.rem(c + 2, 4), t),
        )[at]
        return pltpu.make_async_remote_copy(
            src_ref=OV.at[layer],
            dst_ref=VR.at[layer, at],
            send_sem=v_s.at[layer, at],
            recv_sem=v_r.at[layer, at],
            device_id=partner,
            device_id_type=MESH,
        )

    def vec_move(layer, at):
        if fused:
            if at > 0:
                vec_step(layer, at - 1).wait()
                OV[layer] += VR[layer, at - 1]
            if at < 5:
                vec_step(layer, at).start()

    def side_of(own_side):
        if fused:
            return pl.multiple_of((s if own_side else 1 - s) * half, half)
        return 0 if own_side else half

    def put_units(own_side, base, step, count, value):
        value = value.astype(BF16).reshape(count, cols, half)
        if own_side:
            GO[pl.ds(base + step, count)] = value
        elif fused:
            GS[pl.ds(step, count)] = value
        else:
            XR[pl.ds(base + step, count)] = value

    def send_units(base, step, count):
        if fused:
            for i in range(step, step + count):
                x_copy(base + i).start()

    def split_grad(a, b_ref_at, base, step, count):
        for own_side in (False, True):
            put_units(own_side, base, step, count, tn(a, b_ref_at(side_of(own_side))))
            if not own_side:
                send_units(base, step, count)

    def backward_layer(turn, carry):
        layer = LAYERS - 1 - turn
        base = turn * 12

        def tick(*places):
            if fused:
                for i in places:
                    advance(base + i)

        def late_vec(at):
            @pl.when(turn > 0)
            def _():
                vec_move(LAYERS - 1, at)

        grad = H[...]
        xhat = XH2[layer]
        rstd = SD2[layer][:, :1]
        d_second = norm_backward(grad, xhat, rstd, full_vec(layer, 8))
        put_vec(layer, 4, jnp.sum(grad * xhat, axis=0, keepdims=True))
        put_vec(layer, 5, jnp.sum(grad, axis=0, keepdims=True))
        DR[...] = d_second
        DF[t] = d_second.astype(BF16)
        moves = gather_copies(DF, g4_s.at[layer, 1], g4_r.at[layer, 1])
        gather_start(moves)
        copies = sum_copies(2, 0)

        def back_feed(at):
            where = pl.ds(pl.multiple_of(at * 2 * rows, 2 * rows), 2 * rows)
            block = DF[pl.ds(at * 2, 2)].reshape(2 * rows, width)
            d_act = nt(block, WU[layer])
            low = (d_act * GP[layer, where].astype(F32)).astype(BF16)
            DU[where] = low
            PF[pl.ds(at * 2, 2)] = nt(low, WI[layer]).reshape(2, rows, width)

        moves[0].wait_recv()
        back_feed(y)
        sum_local(copies, PF, 2, 0)
        tick(0, 1)
        late_vec(0)
        gather_remote(moves)
        back_feed(1 - y)
        sum_remote(copies, PF, 2, 0)
        gather_finish(moves)

        def halves(ref):
            return lambda at: ref[:, :, pl.ds(at, half)].reshape(-1, half)

        split_grad(G[layer], halves(DF), base, 0, 4)
        tick(2)
        for own_side in (False, True):
            left = N1B[layer, :, :, pl.ds(side_of(own_side), half)].reshape(own_rows, half)
            for at in range(2):
                put_units(own_side, base, 4 + 2 * at, 2, tn(left, DU[:, at * half : (at + 1) * half]))
            if not own_side:
                send_units(base, 4, 4)
        tick(3)
        late_vec(1)
        only = jnp.where(t == 0, 1.0, 0.0)
        put_vec(layer, 0, only * jnp.sum(DF[...].reshape(own_rows, width).astype(F32), axis=0, keepdims=True))
        put_vec(layer, 14 + t, jnp.sum(DU[...].astype(F32), axis=0, keepdims=True))

        d_normed = DR[...] + sum_finish(copies, PF, 2, 0)
        xhat = XH1[layer]
        d_first = norm_backward(d_normed, xhat, SD1[layer][:, :1], full_vec(layer, 6))
        put_vec(layer, 2, jnp.sum(d_normed * xhat, axis=0, keepdims=True))
        put_vec(layer, 3, jnp.sum(d_normed, axis=0, keepdims=True))
        DR1[...] = d_first
        DA[t] = d_first.astype(BF16)
        moves = gather_copies(DA, g4_s.at[layer, 2], g4_r.at[layer, 2])
        gather_start(moves)

        def back_out(at):
            where = pl.ds(pl.multiple_of(at * 2 * rows, 2 * rows), 2 * rows)
            block = DA[pl.ds(at * 2, 2)].reshape(2 * rows, width)
            DOB[where] = nt(block, WO[layer]).astype(BF16)

        moves[0].wait_recv()
        back_out(y)
        tick(4, 5)
        late_vec(2)
        gather_remote(moves)
        back_out(1 - y)
        gather_finish(moves)
        split_grad(OB[layer], halves(DA), base, 8, 1)
        put_vec(layer, 1, only * jnp.sum(DA[...].reshape(own_rows, width).astype(F32), axis=0, keepdims=True))

        DKF[...] = jnp.zeros_like(DKF)
        DVF[...] = jnp.zeros_like(DVF)

        def back_attend(at, inner):
            where = pl.ds(pl.multiple_of(at * tile, tile), tile)
            grad_tile = DOB[where]
            q_tile = Q[layer, where]
            product = grad_tile.astype(F32) * OB[layer, where].astype(F32)
            d_query = []
            for head in range(3):
                lanes = slice(2 * HD, 3 * HD) if head == 2 else slice(0, 2 * HD)
                d_mix = head_cols(grad_tile, head)
                d_prob = nt(d_mix, head_full(V[layer], head))
                total = jnp.sum(head_cols(product, head), axis=-1, keepdims=True)
                low = PB[layer, head, where]
                d_score = (low.astype(F32) * (d_prob - total)).astype(BF16)
                d_query.append(nn(d_score, head_full(K[layer], head)))
                DKF[:, lanes] += tn(d_score, head_cols(q_tile, head))
                DVF[:, lanes] += tn(low, d_mix)
            scale = HD**-0.5
            DQ[where, : 2 * HD] = (jnp.where(lane_low, d_query[0], d_query[1]) * scale).astype(BF16)
            DQ[where, 2 * HD :] = (d_query[2] * scale).astype(BF16)
            return inner

        tick(6)
        lax.fori_loop(0, 2, back_attend, 0)
        tick(7, 8)
        late_vec(3)
        DK[...] = DKF[...].astype(BF16)
        DV[...] = DVF[...].astype(BF16)
        own = hf * 4
        far = (1 - hf) * 4

        def back_in(at, with_q):
            where = pl.ds(pl.multiple_of(at * rows, 2 * rows), 2 * rows)
            total = nn(DK[where], WQ[layer, cols : 2 * cols]) + nn(DV[where], WQ[layer, 2 * cols :])
            if with_q:
                mine = pl.ds(pl.multiple_of((at - own) * rows, 2 * rows), 2 * rows)
                total = total + nn(DQ[mine], WQ[layer, :cols])
            PF[pl.ds(at, 2)] = total.reshape(2, rows, width)

        pf_far = PF.at[pl.ds(far, 4)]
        pf_own = PF.at[pl.ds(own, 4)]
        far_copies = sum_copies(3, 1)
        back_in(far + 2 * (1 - y), False)
        sum_remote(far_copies, pf_far, 3, 1)
        back_in(far + 2 * y, False)
        sum_local(far_copies, pf_far, 3, 1)
        copies = sum_copies(4, 0)
        back_in(own + 2 * (1 - y), True)
        sum_remote(copies, pf_own, 4, 0)
        back_in(own + 2 * y, True)
        sum_local(copies, pf_own, 4, 0)
        ZS[...] = sum_finish(far_copies, pf_far, 3, 1).astype(BF16)
        across = rc(ZS, ZR.at[layer], rz_s.at[layer], rz_r.at[layer], zp, t)
        across.start()
        tick(9)
        late_vec(4)

        def block_cols(ref, start, count):
            return lambda at: ref[pl.ds(start, count), :, pl.ds(at, half)].reshape(-1, half)

        xb = XB.at[layer]
        split_grad(DQ[...], block_cols(xb, own, 4), base, 9, 1)
        split_grad(DK[...], block_cols(xb, 0, 8), base, 10, 1)
        split_grad(DV[...], block_cols(xb, 0, 8), base, 11, 1)
        tick(10)
        put_vec(layer, 6 + t, jnp.sum(DQ[...].astype(F32), axis=0, keepdims=True))
        put_vec(layer, 10 + t, jnp.sum(DV[...].astype(F32), axis=0, keepdims=True))

        near = sum_finish(copies, pf_own, 4, 0)
        tick(11)
        late_vec(5)
        across.wait()
        H[...] = DR1[...] + near + ZR[layer].astype(F32)
        return carry

    lax.fori_loop(0, LAYERS, backward_layer, 0)
    CO[...] = H[...].astype(BF16)
    collect_start(CO, OG, 3)
    vec_move(0, 0)
    if fused:
        more = LAGS[3]
        spots = [0, more // 5, 2 * more // 5, 3 * more // 5, 4 * more // 5]
        for i in range(more):
            if i in spots[1:]:
                vec_move(0, spots.index(i))
            advance(total_units + i)
        vec_move(0, 5)

        def drain(i, carry):
            pltpu.make_async_copy(GO.at[i], out_mat.at[i], om_sem.at[i]).wait()
            return carry

        lax.fori_loop(0, total_units, drain, 0)
        for layer in range(LAYERS):
            fetch_drain(layer)
    else:
        own_out = pltpu.make_async_copy(GO, out_mat.at[0], om_sem.at[0])
        far_out = pltpu.make_async_copy(XR, out_mat.at[1], om_sem.at[1])
        own_out.start()
        far_out.start()
        own_out.wait()
        far_out.wait()
    out_vec[...] = OV[...]
    collect_wait(TK, OT, 2)
    out_tok[...] = OT[...]
    collect_wait(CO, OG, 3)
    out_grad[...] = OG[...]


def finish_kernel(dims, *refs):
    tok_ref, grad_ref, mat_ref, vec_ref = refs[:4]
    out_tok, out_grad, out_q, out_k, out_v, out_o, out_i, out_u = refs[4:12]
    vec_q, vec_v, vec_o, vec_i, vec_u, gain_1, shift_1, gain_2, shift_2 = refs[12:]
    width, cols, units, half = dims
    layer = pl.program_id(0)
    s = lax.axis_index("shard")

    @pl.when(layer == 0)
    def _():
        out_tok[...] = tok_ref[...]
        out_grad[...] = grad_ref[...].astype(F32)

    for i in range(4):
        out_u[0, i * cols : (i + 1) * cols, :] = mat_ref[i].astype(F32)
        r, cc = i % 2, i // 2
        out_i[0, r * cols : (r + 1) * cols, cc * half : (cc + 1) * half] = mat_ref[4 + i].astype(F32)
    out_o[0] = mat_ref[8].astype(F32)
    out_q[0] = mat_ref[9].astype(F32)
    out_k[0] = mat_ref[10].astype(F32)
    out_v[0] = mat_ref[11].astype(F32)
    line = pl.ds(layer, 1)
    at = pl.ds(pl.multiple_of(s * half, half), half)
    for row, ref in ((0, vec_u), (1, vec_o), (2, gain_1), (3, shift_1), (4, gain_2), (5, shift_2)):
        ref[line, :] = vec_ref[0, row : row + 1, at]
    for row, ref in ((6, vec_q), (10, vec_v)):
        first = vec_ref[0, pl.ds(row + 2 * s, 1), :cols]
        second = vec_ref[0, pl.ds(row + 1 + 2 * s, 1), :cols]
        ref[line, :] = jnp.concatenate([first, second], axis=1)
    vec_i[line, :width] = vec_ref[0, pl.ds(14 + 2 * s, 1)]
    vec_i[line, width:] = vec_ref[0, pl.ds(15 + 2 * s, 1)]


def per_device(
    tokens,
    cotangent,
    segment_ids,
    lengths,
    query_weight,
    key_weight,
    value_weight,
    output_weight,
    inner_weight,
    outer_weight,
    query_bias,
    value_bias,
    output_bias,
    inner_bias,
    outer_bias,
    first_gain,
    first_shift,
    second_gain,
    second_shift,
):
    shards = lax.axis_size("shard")
    assert lax.axis_size("ctx") == 4 and lax.axis_size("tp") == 4 and tokens.shape[0] == 2
    fused = shards == 2
    seqs, part, width = tokens.shape
    cols = query_weight.shape[2]
    units = inner_weight.shape[2]
    half = width // 2
    rows = 2 * part
    own_rows, all_rows = 4 * rows, 8 * rows
    assert cols == 3 * HD and segment_ids.shape[1] == all_rows and units == width == 4 * cols

    def turned(mat):
        return jnp.swapaxes(mat, 1, 2)

    mats = (
        turned(query_weight),
        turned(key_weight),
        turned(value_weight),
        output_weight,
        inner_weight,
        outer_weight,
    )
    vecs = (query_bias, value_bias, output_bias, outer_bias, inner_bias, first_gain, first_shift, second_gain, second_shift)
    if not fused:
        mats = tuple(
            lax.all_gather(mat, "shard", axis=axis, tiled=True) for mat, axis in zip(mats, (2, 2, 2, 2, 1, 2))
        )
        vecs = tuple(lax.all_gather(vec, "shard", axis=1, tiled=True) for vec in vecs)

    n_units = 12 * LAYERS
    out_shape = [
        jax.ShapeDtypeStruct((2, part, width), BF16),
        jax.ShapeDtypeStruct((2, part, width), BF16),
        jax.ShapeDtypeStruct((n_units, cols, half) if fused else (2, n_units, cols, half), BF16),
        jax.ShapeDtypeStruct((LAYERS, VEC_ROWS, width), F32),
    ]
    vm = pltpu.VMEM
    dma = pltpu.SemaphoreType.DMA
    scratch = [
        vm((LAYERS, 3 * cols, width), BF16),
        vm((LAYERS, cols, width), BF16),
        vm((LAYERS, width, units), BF16),
        vm((LAYERS, units, width), BF16),
        vm((2, LAYERS, 16, half), F32),
        vm((own_rows, 128), F32),
        vm((8, all_rows), F32),
        vm((rows, width), F32),
        vm((rows, width), F32),
        vm((rows, width), F32),
        vm((rows, width), F32),
        vm((rows, width), BF16),
        vm((rows, width), BF16),
        vm((2, part, width), BF16),
        vm((2, part, width), BF16),
        vm((LAYERS, rows, width), F32),
        vm((LAYERS, rows, width), F32),
        vm((LAYERS, rows, 128), F32),
        vm((LAYERS, rows, 128), F32),
        vm((LAYERS, 8, rows, width), BF16),
        vm((LAYERS, own_rows, cols), BF16),
        vm((LAYERS, all_rows, cols), BF16),
        vm((LAYERS, all_rows, cols), BF16),
        vm((LAYERS, own_rows, cols), BF16),
        vm((LAYERS, 4, rows, width), BF16),
        vm((LAYERS, own_rows, units), BF16),
        vm((LAYERS, own_rows, units), BF16),
        vm((LAYERS, 3, own_rows, all_rows), BF16),
        vm((4, rows, width), BF16),
        vm((4, rows, width), BF16),
        vm((own_rows, units), BF16),
        vm((own_rows, cols), BF16),
        vm((own_rows, cols), BF16),
        vm((all_rows, cols), BF16),
        vm((all_rows, cols), BF16),
        vm((all_rows, cols), F32),
        vm((all_rows, cols), F32),
        vm((8, rows, width), F32),
        vm((2, 3, rows, width), BF16),
        vm((5, 3, rows, width), BF16),
        vm((rows, width), BF16),
        vm((LAYERS, rows, width), BF16),
        vm((n_units, cols, half), BF16),
        vm((12, cols, half), BF16),
        vm((n_units, cols, half), BF16),
        vm((n_units, cols, half), BF16),
        vm((n_units, cols, half), BF16),
        vm((LAYERS, VEC_ROWS, width), F32),
        vm((LAYERS, 5, VEC_ROWS, width), F32),
        dma((LAYERS, 6)),
        dma((LAYERS, 13)),
        dma((LAYERS, 13)),
        dma((LAYERS, 12)),
        dma((LAYERS, 12)),
        dma((LAYERS, 5)),
        dma((LAYERS, 5)),
        dma((4, 2)),
        dma((4, 2)),
        dma((LAYERS, 7)),
        dma((LAYERS, 7)),
        dma((LAYERS, 3, 3)),
        dma((LAYERS, 3, 3)),
        dma((5, 3)),
        dma((5, 3)),
        dma((LAYERS,)),
        dma((LAYERS,)),
        dma((n_units,)),
        dma((n_units,)),
        dma((n_units,)),
        dma((n_units,)),
        dma((n_units,)),
        dma((n_units,)),
        dma((n_units,)),
        dma((n_units,)),
        dma((n_units,)),
    ]
    vmem = pl.BlockSpec(memory_space=pltpu.VMEM)
    hbm = pl.BlockSpec(memory_space=pl.ANY)
    layer_out, grad_tokens, grad_mats, grad_vecs = pl.pallas_call(
        functools.partial(step_kernel, (width, cols, units, half), fused),
        out_shape=out_shape,
        in_specs=[vmem] * 12 + [pl.BlockSpec(memory_space=pltpu.SMEM)] + [hbm] * 6,
        out_specs=[vmem, vmem, hbm, vmem],
        scratch_shapes=scratch,
        compiler_params=pltpu.CompilerParams(
            collective_id=0, has_side_effects=True, vmem_limit_bytes=67043328
        ),
        name="encoder_step",
    )(tokens, cotangent, segment_ids, *vecs, lengths, *mats)

    if fused:
        dims = (width, cols, units, half)
        layer_block = lambda *shape: pl.BlockSpec((1,) + shape, lambda i: (i,) + (0,) * len(shape))
        whole = lambda *shape: pl.BlockSpec(shape, lambda i: (0,) * len(shape))
        mat_shapes = [(cols, half)] * 4 + [(half, units), (units, half)]
        vec_lens = (half, half, half, 4 * half, half, half, half, half, half)
        outs = pl.pallas_call(
            functools.partial(finish_kernel, dims),
            grid=(LAYERS,),
            out_shape=[
                jax.ShapeDtypeStruct((2, part, width), BF16),
                jax.ShapeDtypeStruct((2, part, width), F32),
            ]
            + [jax.ShapeDtypeStruct((LAYERS,) + shape, F32) for shape in mat_shapes]
            + [jax.ShapeDtypeStruct((LAYERS, count), F32) for count in vec_lens],
            in_specs=[
                whole(2, part, width),
                whole(2, part, width),
                pl.BlockSpec((12, cols, half), lambda i: (LAYERS - 1 - i, 0, 0)),
                layer_block(VEC_ROWS, width),
            ],
            out_specs=[whole(2, part, width), whole(2, part, width)]
            + [layer_block(*shape) for shape in mat_shapes]
            + [whole(LAYERS, count) for count in vec_lens],
            name="write_out",
        )(layer_out, grad_tokens, grad_mats, grad_vecs)
        return tuple(outs[:2]) + tuple(turned(mat) for mat in outs[2:5]) + tuple(outs[5:])

    mats = grad_mats.reshape(2, LAYERS, 12, cols, half)[:, ::-1]
    wide = jnp.concatenate([mats[0], mats[1]], axis=-1)
    wide = jnp.concatenate([wide[:, :4], wide[:, 8:]], axis=1)
    wide = lax.psum(lax.psum_scatter(wide, "shard", scatter_dimension=3, tiled=True), "ctx").astype(F32)
    inner = mats[:, :, 4:8].reshape(2, LAYERS, 2, 2, cols, half)
    inner = jnp.transpose(inner, (1, 0, 3, 4, 2, 5)).reshape(LAYERS, width, units)
    inner = lax.psum(lax.psum_scatter(inner, "shard", scatter_dimension=1, tiled=True), "ctx").astype(F32)
    grad_outer = wide[:, :4].reshape(LAYERS, units, -1)
    grad_output = wide[:, 4]
    grad_query, grad_key, grad_value = (turned(wide[:, 5 + at]) for at in range(3))

    total = lax.psum(grad_vecs, ("shard", "ctx", "tp"))
    at = lax.axis_index("shard")

    def owned(vec):
        count = vec.shape[1] // shards
        return lax.dynamic_slice_in_dim(vec, at * count, count, 1)

    vec_query = owned(total[:, 6:10, :cols].reshape(LAYERS, -1))
    vec_value = owned(total[:, 10:14, :cols].reshape(LAYERS, -1))
    vec_inner = owned(total[:, 14:18].reshape(LAYERS, -1))
    vec_outer, vec_output, gain_one, shift_one, gain_two, shift_two = (owned(total[:, row]) for row in range(6))
    return (
        layer_out,
        grad_tokens.astype(F32),
        grad_query,
        grad_key,
        grad_value,
        grad_output,
        inner,
        grad_outer,
        vec_query,
        vec_value,
        vec_output,
        vec_inner,
        vec_outer,
        gain_one,
        shift_one,
        gain_two,
        shift_two,
    )


def solution(mesh):
    rows = P("shard", ("ctx", "tp"), None)
    down = P(None, "shard", "tp")
    across = P(None, "tp", "shard")
    vector = P(None, "shard")
    mats = (down, down, down, across, down, across)
    return jax.shard_map(
        per_device,
        mesh=mesh,
        in_specs=(rows, rows, P("shard", None), P("shard")) + mats + (vector,) * 9,
        out_specs=(rows, rows) + mats + (vector,) * 9,
        check_vma=False,
    )
```

```python
import functools

import jax
import jax.numpy as jnp
from jax import lax
from jax.experimental import pallas as pl
from jax.experimental.pallas import tpu as pltpu
from jax.sharding import PartitionSpec as P

HD = 64
LAYERS = 2
EPSILON = 1e-05
MESH = pl.DeviceIdType.MESH
F32 = jnp.float32
BF16 = jnp.bfloat16
NEG = -1e30
VEC_ROWS = 24
PIECES = 2
LAGS = (4, 6, 8, 10)
VEC_TICKS = (1, 2, 5, 7)


def nn(a, b):
    return jnp.dot(a, b, preferred_element_type=F32)


def nt(a, b):
    return lax.dot_general(a, b, (((1,), (1,)), ((), ())), preferred_element_type=F32)


def tn(a, b):
    return lax.dot_general(a, b, (((0,), (0,)), ((), ())), preferred_element_type=F32)


def norm_forward(resid, gain, shift):
    center = resid - jnp.mean(resid, axis=-1, keepdims=True)
    spread = jnp.mean(center * center, axis=-1, keepdims=True)
    rstd = lax.rsqrt(spread + EPSILON)
    xhat = center * rstd
    return xhat * gain + shift, xhat, rstd


def norm_backward(grad, xhat, rstd, gain):
    scaled = grad * gain
    first = jnp.mean(scaled, axis=-1, keepdims=True)
    second = jnp.mean(scaled * xhat, axis=-1, keepdims=True)
    return rstd * (scaled - first - xhat * second)


def step_kernel(dims, fused, *refs):
    (
        tok_ref,
        cot_ref,
        seg_ref,
        vec_refs,
        len_ref,
        wq_ref,
        wk_ref,
        wv_ref,
        wo_ref,
        wi_ref,
        wu_ref,
        out_tok,
        out_grad,
        out_mat,
        out_vec,
        WQ,
        WO,
        WI,
        WU,
        VB,
        IDC,
        IDR,
        H,
        N1,
        DR,
        DR1,
        TK,
        CO,
        OT,
        OG,
        XH1,
        XH2,
        SD1,
        SD2,
        XB,
        Q,
        K,
        V,
        OB,
        N1B,
        G,
        GP,
        PB,
        DF,
        DA,
        DU,
        DOB,
        DQ,
        DK,
        DV,
        DKF,
        DVF,
        PF,
        SB,
        RB,
        ZS,
        ZR,
        GO,
        GS,
        XR,
        YR,
        Y2,
        OV,
        VR,
        wl_sem,
        ws_sem,
        wr_sem,
        wz_s,
        wz_r,
        v_s,
        v_r,
        rd_s,
        rd_r,
        g8_s,
        g8_r,
        g4_s,
        g4_r,
        rs_s,
        rs_r,
        rz_s,
        rz_r,
        xs_s,
        xs_r,
        z1_s,
        z1_r,
        z2_s,
        z2_r,
        z3_s,
        z3_r,
        om_sem,
    ) = refs[:3] + (refs[3:12],) + refs[12:]
    width, cols, units, half = dims
    seqs, part = tok_ref.shape[0], tok_ref.shape[1]
    rows = 2 * part
    own_rows = 4 * rows
    all_rows = 8 * rows
    tall = rows // PIECES
    s = lax.axis_index("shard")
    c = lax.axis_index("ctx")
    t = lax.axis_index("tp")
    hf = lax.rem(c, 2)
    y = t // 2
    k = lax.rem(t, 2)
    tc = t + 1 - 2 * k
    ty = lax.rem(t + 2, 4)
    zp = c + 1 - 2 * hf
    is_inner = jnp.logical_or(c == 1, c == 2)
    is_outer = jnp.logical_not(is_inner)
    z_in = jnp.where(c == 0, 1, 2)
    z_mid = 3 - c
    z_out = jnp.where(c == 1, 0, 3)

    def rc(src, dst, ssem, rsem, cc, tt, ss=None):
        return pltpu.make_async_remote_copy(
            src_ref=src,
            dst_ref=dst,
            send_sem=ssem,
            recv_sem=rsem,
            device_id=(s if ss is None else ss, cc, tt),
            device_id_type=MESH,
        )

    bar = pltpu.get_barrier_semaphore()
    for dc in range(4):
        for dt in range(4):
            if dc or dt:
                pl.semaphore_signal(
                    bar,
                    1,
                    device_id=(s, lax.rem(c + dc, 4), lax.rem(t + dt, 4)),
                    device_id_type=MESH,
                )
    if fused:
        pl.semaphore_signal(bar, 1, device_id=(1 - s, c, t), device_id_type=MESH)
    pl.semaphore_wait(bar, 16 if fused else 15)

    def unit_view(layer, item, side):
        at = pl.multiple_of(side * half, half)
        lanes = pl.ds(at, half)
        if item < 3:
            return WQ.at[layer, pl.ds(item * cols, cols), lanes]
        if item == 3:
            return WO.at[layer, :, lanes]
        if item < 8:
            return WI.at[layer, pl.ds(at + (item - 4) * (half // 4), half // 4)]
        return WU.at[layer, pl.ds((item - 8) * cols, cols), lanes]

    def unit_arg(layer, item):
        if item < 4:
            return (wq_ref, wk_ref, wv_ref, wo_ref)[item].at[layer]
        if item < 8:
            return wi_ref.at[layer, pl.ds((item - 4) * (half // 4), half // 4)]
        return wu_ref.at[layer, pl.ds((item - 8) * cols, cols)]

    def local_copy(layer, item):
        lanes = pl.ds(pl.multiple_of(s * half, half), half) if fused else pl.ds(0, width)
        if item < 3:
            src, dst = (wq_ref, wk_ref, wv_ref)[item], WQ.at[layer, pl.ds(item * cols, cols), lanes]
        elif item == 3:
            src, dst = wo_ref, WO.at[layer, :, lanes]
        elif item == 4:
            src, dst = wi_ref, WI.at[layer, lanes]
        else:
            src, dst = wu_ref, WU.at[layer, :, lanes]
        return pltpu.make_async_copy(src.at[layer], dst, wl_sem.at[layer, item])

    def over_x(layer, item):
        return rc(
            unit_arg(layer, item),
            unit_view(layer, item, s),
            ws_sem.at[layer, item],
            wr_sem.at[layer, item],
            c,
            t,
            1 - s,
        )

    def over_z(layer, item):
        view = unit_view(layer, item, 1 - s)
        return rc(view, view, wz_s.at[layer, item], wz_r.at[layer, item], zp, t)

    def direct(layer, item):
        return jnp.logical_and(layer == 0, item < 4)

    def mine_over_x(layer, item):
        return jnp.logical_or(direct(layer, item), hf == item % 2)

    def fetch_start(layer, item):
        @pl.when(mine_over_x(layer, item))
        def _():
            over_x(layer, item).start()

    def fetch_pass(layer, items):
        if fused:
            for item in items:

                @pl.when(hf == item % 2)
                def _():
                    over_x(layer, item).wait_recv()
                    over_z(layer, item).start()

    def fetch_wait(layer, items):
        for item in items:
            local_copy(layer, {0: 0, 1: 1, 2: 2, 3: 3, 4: 4, 8: 5}[item]).wait() if item in (0, 1, 2, 3, 4, 8) else None
            if fused:

                @pl.when(direct(layer, item))
                def _():
                    over_x(layer, item).wait_recv()

                @pl.when(jnp.logical_not(mine_over_x(layer, item)))
                def _():
                    over_z(layer, item).wait_recv()

    def fetch_drain(layer):
        for item in range(12):

            @pl.when(mine_over_x(layer, item))
            def _():
                over_x(layer, item).wait_send()

            @pl.when(jnp.logical_and(hf == item % 2, jnp.logical_not(direct(layer, item))))
            def _():
                over_z(layer, item).wait_send()

    def fill_vectors(side, at):
        for layer in range(LAYERS):
            for place, ref in ((0, vec_refs[0]), (2, vec_refs[1])):
                value = ref[...].astype(F32)[layer : layer + 1, at : at + half]
                VB[side, layer, place : place + 1, :cols] = value[:, :cols]
                VB[side, layer, place + 1 : place + 2, :cols] = value[:, cols:]
            for place, ref in zip((4, 5, 6, 7, 8, 9), vec_refs[2:4] + vec_refs[5:9]):
                VB[side, layer, place : place + 1] = ref[...].astype(F32)[layer : layer + 1, at : at + half]
            value = vec_refs[4][...].astype(F32)[layer : layer + 1, 4 * at : 4 * at + 4 * half]
            for j in range(4):
                VB[side, layer, 10 + j : 11 + j] = value[:, j * half : (j + 1) * half]

    if fused:
        fill_vectors(s, 0)
        vec_copy = rc(VB.at[s], VB.at[s], ws_sem.at[0, 12], wr_sem.at[0, 12], c, t, 1 - s)
        vec_copy.start()
    else:
        fill_vectors(0, 0)
        fill_vectors(1, half)

    b_me = c // 2
    spread_t = 2 * hf + y

    def spread_copies(src_ref, dst_ref, which):
        return [
            (
                jnp.logical_and(2 * b + c // 2 == c, spread_t == t),
                rc(
                    src_ref.at[b],
                    dst_ref.at[pl.ds(k * part, part)],
                    rd_s.at[which, b],
                    rd_r.at[which, k],
                    2 * b + c // 2,
                    spread_t,
                ),
            )
            for b in range(2)
        ]

    def spread_start(src_ref, dst_ref, which):
        for b, (mine, copy) in enumerate(spread_copies(src_ref, dst_ref, which)):

            @pl.when(mine)
            def _():
                dst_ref[pl.ds(pl.multiple_of(k * part, part), part), :] = src_ref[b]

            @pl.when(jnp.logical_not(mine))
            def _():
                copy.start()

    def spread_wait(src_ref, dst_ref, which):
        for mine, copy in spread_copies(src_ref, dst_ref, which):

            @pl.when(jnp.logical_not(mine))
            def _():
                copy.wait_send()

        for kk in range(2):
            mine = jnp.logical_and(2 * hf + y == c, 2 * k + kk == t)

            @pl.when(jnp.logical_not(mine))
            def _():
                rc(
                    src_ref.at[0],
                    dst_ref.at[pl.ds(kk * part, part)],
                    rd_s.at[which, 0],
                    rd_r.at[which, kk],
                    c,
                    t,
                ).wait_recv()

    def collect_copies(src_ref, dst_ref, which):
        return [
            (
                jnp.logical_and(2 * hf + y == c, 2 * k + kk == t),
                rc(
                    src_ref.at[pl.ds(kk * part, part)],
                    dst_ref.at[b_me],
                    rd_s.at[which, kk],
                    rd_r.at[which, b_me],
                    2 * hf + y,
                    2 * k + kk,
                ),
            )
            for kk in range(2)
        ]

    def collect_start(src_ref, dst_ref, which):
        for kk, (mine, copy) in enumerate(collect_copies(src_ref, dst_ref, which)):

            @pl.when(mine)
            def _():
                dst_ref[b_me] = src_ref[kk * part : (kk + 1) * part, :]

            @pl.when(jnp.logical_not(mine))
            def _():
                copy.start()

    def collect_wait(src_ref, dst_ref, which):
        for mine, copy in collect_copies(src_ref, dst_ref, which):

            @pl.when(jnp.logical_not(mine))
            def _():
                copy.wait_send()

        for b in range(2):
            mine = jnp.logical_and(2 * b + c // 2 == c, spread_t == t)

            @pl.when(jnp.logical_not(mine))
            def _():
                rc(
                    src_ref.at[pl.ds(0, part)],
                    dst_ref.at[b],
                    rd_s.at[which, 0],
                    rd_r.at[which, b],
                    c,
                    t,
                ).wait_recv()

    spread_start(tok_ref, TK, 0)
    for layer in range(LAYERS):
        if fused:
            for item in range(12):
                fetch_start(layer, item)
        for item in range(6):
            local_copy(layer, item).start()
    spread_start(cot_ref, CO, 1)

    ids = seg_ref[pl.ds(b_me, 1)]
    places = lax.broadcasted_iota(jnp.int32, ids.shape, 1)
    ids = jnp.where(places < len_ref[b_me], ids, -1).astype(F32)
    IDR[...] = jnp.broadcast_to(ids, IDR.shape)
    own_ids = jnp.where(hf == 0, ids[:, :own_rows], ids[:, own_rows:])
    IDC[...] = jnp.broadcast_to(own_ids, (128, own_rows)).T

    def piece(ch):
        return slice(ch * tall, (ch + 1) * tall)

    def gather_copies(buf, ssem, rsem):
        def move(slot, ch, at, tt):
            view = buf.at[slot, pl.ds(ch * tall, tall)]
            return rc(view, view, ssem.at[3 * ch + at], rsem.at[3 * ch + at], c, tt)

        return [(move(t, ch, 0, tc), move(t, ch, 1, ty), move(ty, ch, 2, tc)) for ch in range(PIECES)]

    def gather_start(copies, ch):
        copies[ch][1].start()
        copies[ch][0].start()

    def gather_near(copies):
        for to_c, _, _ in copies:
            to_c.wait_recv()

    def gather_remote(copies):
        for _, to_y, y_to_c in copies:
            to_y.wait_recv()
            y_to_c.start()
        for _, _, y_to_c in copies:
            y_to_c.wait_recv()

    def gather_finish(copies):
        for moves in copies:
            for copy in moves:
                copy.wait_send()

    def sum_copies(slot, lane):
        def move(at, ch, tt):
            where = pl.ds(ch * tall, tall)
            sem = PIECES * at + ch
            return rc(SB.at[lane, at, where], RB.at[slot, at, where], rs_s.at[slot, sem], rs_r.at[slot, sem], c, tt)

        pairs = [(move(0, ch, tc), move(1, ch, ty)) for ch in range(PIECES)]
        last = 2 * PIECES
        return pairs, rc(SB.at[lane, 2], RB.at[slot, 2], rs_s.at[slot, last], rs_r.at[slot, last], c, tc)

    def sum_remote(copies, pf, slot, lane):
        for ch, (to_c, _) in enumerate(copies[0]):
            SB[lane, 0, piece(ch)] = pf[(1 - y) * 2 + 1 - k, piece(ch)].astype(BF16)
            to_c.start()
        for ch, (to_c, to_y) in enumerate(copies[0]):
            to_c.wait_recv()
            SB[lane, 1, piece(ch)] = (pf[ty, piece(ch)] + RB[slot, 0, piece(ch)].astype(F32)).astype(BF16)
            to_y.start()

    def sum_local(copies, pf, slot, lane):
        SB[lane, 2] = pf[tc].astype(BF16)
        copies[1].start()

    def sum_finish(copies, pf, slot, lane, ch):
        pairs, near = copies
        if ch == 0:
            near.wait_recv()
        partial = pf[t, piece(ch)] + RB[slot, 2, piece(ch)].astype(F32)
        pairs[ch][1].wait_recv()
        if ch == PIECES - 1:
            for to_c, to_y in pairs:
                to_c.wait_send()
                to_y.wait_send()
            near.wait_send()
        return partial + RB[slot, 1, piece(ch)].astype(F32)

    def full_vec(layer, row):
        return jnp.concatenate([VB[0, layer, row : row + 1], VB[1, layer, row : row + 1]], axis=1)

    def vec_at(layer, row, lanes):
        return VB[y, layer, pl.ds(row, 1)][:, :lanes]

    OV[...] = jnp.zeros_like(OV)

    def put_vec(layer, row, value):
        OV[layer, pl.ds(row, 1), : value.shape[1]] = value

    if fused:
        vec_copy.wait()
    spread_wait(tok_ref, TK, 0)
    own = hf * 4
    far = (1 - hf) * 4

    def input_copies(layer):
        buf = XB.at[layer]

        def move(slot, ch, at, cc, tt):
            view = buf.at[slot, pl.ds(ch * tall, tall)]
            return rc(view, view, g8_s.at[layer, 7 * ch + at], g8_r.at[layer, 7 * ch + at], cc, tt)

        return [
            (
                move(own + t, ch, 0, c, ty),
                move(own + t, ch, 1, zp, t),
                move(own + t, ch, 2, c, tc),
                move(own + ty, ch, 3, c, tc),
                move(far + t, ch, 4, c, ty),
                move(far + t, ch, 5, c, tc),
                move(far + ty, ch, 6, c, tc),
            )
            for ch in range(PIECES)
        ]

    def input_start(layer, ch):
        for copy in input_copies(layer)[ch][:3]:
            copy.start()

    H[...] = TK[...].astype(F32)
    XB[0, own + t] = TK[...]
    for ch in range(PIECES):
        input_start(0, ch)
    lane_low = lax.broadcasted_iota(jnp.int32, (1, 2 * HD), 1) < HD

    def head_cols(value, head):
        if head == 2:
            return value[:, 2 * HD : 3 * HD]
        keep = lane_low if head == 0 else jnp.logical_not(lane_low)
        return jnp.where(keep, value[:, : 2 * HD], jnp.zeros_like(value[:, : 2 * HD]))

    def head_full(value, head):
        return value[:, 2 * HD : 3 * HD] if head == 2 else value[:, : 2 * HD]

    tile = own_rows // 2

    def forward_layer(layer, carry):
        arrivals = input_copies(layer)
        fetch_wait(layer, (0, 1, 2))

        def project(at, with_q):
            block = XB[layer, pl.ds(at, 2)].reshape(2 * rows, width)
            where = pl.ds(pl.multiple_of(at * rows, 2 * rows), 2 * rows)
            if with_q:
                mine = pl.ds(pl.multiple_of((at - own) * rows, 2 * rows), 2 * rows)
                qb = vec_at(layer, k, cols)
                q_low = (nt(block, WQ[layer, :cols]) + qb).astype(BF16)
                Q[layer, mine] = q_low * jnp.asarray(HD**-0.5, BF16)
            K[layer, where] = nt(block, WQ[layer, cols : 2 * cols]).astype(BF16)
            V[layer, where] = (nt(block, WQ[layer, 2 * cols :]) + vec_at(layer, 2 + k, cols)).astype(BF16)

        for moves in arrivals:
            moves[2].wait_recv()
        project(own + 2 * y, True)
        for moves in arrivals:
            moves[1].wait_recv()
            moves[4].start()
            moves[5].start()
            moves[0].wait_recv()
            moves[3].start()
        for moves in arrivals:
            moves[3].wait_recv()
        project(own + 2 * (1 - y), True)
        for moves in arrivals:
            moves[5].wait_recv()
        project(far + 2 * y, False)
        for moves in arrivals:
            moves[4].wait_recv()
            moves[6].start()
        for moves in arrivals:
            moves[6].wait_recv()
        project(far + 2 * (1 - y), False)
        for moves in arrivals:
            for copy in moves:
                copy.wait_send()
        fetch_pass(layer, (4, 5))

        def attend(at, inner):
            where = pl.ds(pl.multiple_of(at * tile, tile), tile)
            ids = IDC[where][:, :1] == IDR[:1]
            q_tile = Q[layer, where]
            mixed = []
            for head in range(3):
                scores = nt(head_cols(q_tile, head), head_full(K[layer], head))
                scores = jnp.where(ids, scores, NEG)
                top = jnp.max(scores, axis=-1, keepdims=True)
                expo = jnp.exp(scores - top)
                low = (expo / jnp.sum(expo, axis=-1, keepdims=True)).astype(BF16)
                PB[layer, head, where] = low
                mixed.append(nn(low, head_full(V[layer], head)))
            OB[layer, where, : 2 * HD] = jnp.where(lane_low, mixed[0], mixed[1]).astype(BF16)
            OB[layer, where, 2 * HD :] = mixed[2].astype(BF16)
            return inner

        lax.fori_loop(0, 2, attend, 0)
        fetch_wait(layer, (3,))
        fetch_pass(layer, (6, 7))

        def project_out(at):
            where = pl.ds(pl.multiple_of(at * 2 * rows, 2 * rows), 2 * rows)
            PF[pl.ds(at * 2, 2)] = nn(OB[layer, where], WO[layer]).reshape(2, rows, width)

        copies = sum_copies(0, 0)
        project_out(1 - y)
        sum_remote(copies, PF, 0, 0)
        project_out(y)
        sum_local(copies, PF, 0, 0)
        fetch_pass(layer, (8, 9))
        moves = gather_copies(N1B.at[layer], g4_s.at[layer, 0], g4_r.at[layer, 0])
        for ch in range(PIECES):
            branch = sum_finish(copies, PF, 0, 0, ch) + full_vec(layer, 4)
            resid = H[piece(ch)] + branch
            normed, xhat, rstd = norm_forward(resid, full_vec(layer, 6), full_vec(layer, 7))
            N1B[layer, t, piece(ch)] = normed.astype(BF16)
            gather_start(moves, ch)
            N1[piece(ch)] = normed
            XH1[layer, piece(ch)] = xhat
            SD1[layer, piece(ch)] = jnp.broadcast_to(rstd, (tall, 128))
        fetch_pass(layer, (10, 11))
        fetch_wait(layer, (4, 5, 6, 7))

        def feed(at):
            where = pl.ds(pl.multiple_of(at * 2 * rows, 2 * rows), 2 * rows)
            block = N1B[layer, pl.ds(at * 2, 2)].reshape(2 * rows, width)
            bias = jnp.concatenate([vec_at(layer, 10 + 2 * k, half), vec_at(layer, 11 + 2 * k, half)], axis=1)
            pre = nn(block, WI[layer]) + bias
            phi = 0.5 * (1.0 + lax.erf(pre * (0.5**0.5)))
            low = (pre * phi).astype(BF16)
            G[layer, where] = low
            density = jnp.exp(pre * pre * -0.5) * ((0.5 / jnp.pi) ** 0.5)
            GP[layer, where] = (phi + pre * density).astype(GP.dtype)
            PF[pl.ds(at * 2, 2)] = nn(low, WU[layer]).reshape(2, rows, width)

        copies = sum_copies(1, 0)
        gather_near(moves)
        fetch_wait(layer, (8, 9, 10, 11))
        feed(y)
        sum_local(copies, PF, 1, 0)

        @pl.when(layer == 0)
        def _():
            fetch_pass(1, (0, 1, 2, 3))

        gather_remote(moves)
        feed(1 - y)
        sum_remote(copies, PF, 1, 0)
        gather_finish(moves)
        following = jnp.minimum(layer + 1, LAYERS - 1)
        for ch in range(PIECES):
            second = N1[piece(ch)] + sum_finish(copies, PF, 1, 0, ch) + full_vec(layer, 5)
            result, xhat, rstd = norm_forward(second, full_vec(layer, 8), full_vec(layer, 9))
            low = result.astype(BF16)
            TK[piece(ch)] = low

            @pl.when(layer + 1 < LAYERS)
            def _():
                XB[following, own + t, piece(ch)] = low
                input_start(following, ch)

            XH2[layer, piece(ch)] = xhat
            SD2[layer, piece(ch)] = jnp.broadcast_to(rstd, (tall, 128))
            H[piece(ch)] = result
        return carry

    lax.fori_loop(0, LAYERS, forward_layer, 0)

    collect_start(TK, OT, 2)
    spread_wait(cot_ref, CO, 1)

    total_units = 12 * LAYERS

    def x_copy(unit):
        return rc(GS.at[lax.rem(unit, 12)], XR.at[unit], xs_s.at[unit], xs_r.at[unit], c, t, 1 - s)

    def z1_copy(unit):
        return rc(GO.at[unit], YR.at[unit], z1_s.at[unit], z1_r.at[unit], z_in, t)

    def z2_copy(unit):
        return rc(GO.at[unit], Y2.at[unit], z2_s.at[unit], z2_r.at[unit], z_mid, t)

    def z3_copy(unit):
        return rc(GO.at[unit], YR.at[unit], z3_s.at[unit], z3_r.at[unit], z_out, t)

    def add_into(unit, other):
        GO[unit] = (GO[unit].astype(F32) + other.astype(F32)).astype(BF16)

    def stage_z1(unit):
        x_copy(unit).wait()
        add_into(unit, XR[unit])

        @pl.when(is_outer)
        def _():
            z1_copy(unit).start()

    def stage_z2(unit):
        @pl.when(is_inner)
        def _():
            z1_copy(unit).wait_recv()
            add_into(unit, YR[unit])
            z2_copy(unit).start()

        @pl.when(is_outer)
        def _():
            z1_copy(unit).wait_send()

    def stage_z3(unit):
        @pl.when(is_inner)
        def _():
            z2_copy(unit).wait()
            add_into(unit, Y2[unit])
            z3_copy(unit).start()

    def stage_out(unit):
        @pl.when(is_inner)
        def _():
            z3_copy(unit).wait_send()
            pltpu.make_async_copy(GO.at[unit], out_mat.at[unit], om_sem.at[unit]).start()

        @pl.when(is_outer)
        def _():
            z3_copy(unit).wait_recv()
            pltpu.make_async_copy(YR.at[unit], out_mat.at[unit], om_sem.at[unit]).start()

    stages = ((stage_out, LAGS[3]), (stage_z3, LAGS[2]), (stage_z2, LAGS[1]), (stage_z1, LAGS[0]))

    def advance(tick):
        for stage, lag in stages:
            unit = tick - lag

            @pl.when(jnp.logical_and(unit >= 0, unit < total_units))
            def _(stage=stage, unit=unit):
                stage(unit)

    def vec_step(at):
        partner = (
            (s, c, tc),
            (s, c, ty),
            (1 - s, c, t),
            (s, zp, t),
            (s, lax.rem(c + 2, 4), t),
        )[at]
        return pltpu.make_async_remote_copy(
            src_ref=OV,
            dst_ref=VR.at[at],
            send_sem=v_s.at[at],
            recv_sem=v_r.at[at],
            device_id=partner,
            device_id_type=MESH,
        )

    def vec_move(at):
        if fused:
            if at > 0:
                vec_step(at - 1).wait()
                OV[...] += VR[at - 1]
            if at < 5:
                vec_step(at).start()

    def side_of(own_side):
        if fused:
            return pl.multiple_of((s if own_side else 1 - s) * half, half)
        return 0 if own_side else half

    def put_units(own_side, base, step, count, value):
        value = value.astype(BF16).reshape(count, cols, half)
        if own_side:
            GO[pl.ds(base + step, count)] = value
        elif fused:
            GS[pl.ds(step, count)] = value
        else:
            XR[pl.ds(base + step, count)] = value

    def send_units(base, step, count):
        if fused:
            for i in range(step, step + count):
                x_copy(base + i).start()

    def split_grad(a, b_ref_at, base, step, count):
        for own_side in (False, True):
            put_units(own_side, base, step, count, tn(a, b_ref_at(side_of(own_side))))
            if not own_side:
                send_units(base, step, count)

    def across(layer, ch):
        where = pl.ds(ch * tall, tall)
        return rc(ZS.at[where], ZR.at[layer, where], rz_s.at[layer, ch], rz_r.at[layer, ch], zp, t)

    def layer_grad(layer, ch):
        near = sum_finish(sum_copies(4, 0), PF.at[pl.ds(own, 4)], 4, 0, ch)
        across(layer, ch).wait()
        return DR1[piece(ch)] + near + ZR[layer, piece(ch)].astype(F32)

    def backward_layer(turn, carry):
        layer = LAYERS - 1 - turn
        base = turn * 12

        def tick(*places):
            if fused:
                for i in places:
                    advance(base + i)

        moves = gather_copies(DF, g4_s.at[layer, 1], g4_r.at[layer, 1])
        above = jnp.minimum(layer + 1, LAYERS - 1)
        for ch in range(PIECES):

            @pl.when(turn == 0)
            def _():
                H[piece(ch)] = CO[piece(ch)].astype(F32)

            @pl.when(turn > 0)
            def _():
                H[piece(ch)] = layer_grad(above, ch)

            rstd = SD2[layer, piece(ch)][:, :1]
            d_second = norm_backward(H[piece(ch)], XH2[layer, piece(ch)], rstd, full_vec(layer, 8))
            DF[t, piece(ch)] = d_second.astype(BF16)
            gather_start(moves, ch)
            DR[piece(ch)] = d_second
        put_vec(layer, 4, jnp.sum(H[...] * XH2[layer], axis=0, keepdims=True))
        put_vec(layer, 5, jnp.sum(H[...], axis=0, keepdims=True))
        copies = sum_copies(2, 0)

        def back_feed(at):
            where = pl.ds(pl.multiple_of(at * 2 * rows, 2 * rows), 2 * rows)
            block = DF[pl.ds(at * 2, 2)].reshape(2 * rows, width)
            d_act = nt(block, WU[layer])
            low = (d_act * GP[layer, where].astype(F32)).astype(BF16)
            DU[where] = low
            PF[pl.ds(at * 2, 2)] = nt(low, WI[layer]).reshape(2, rows, width)

        gather_near(moves)
        back_feed(y)
        sum_local(copies, PF, 2, 0)
        tick(0, 1)
        gather_remote(moves)
        back_feed(1 - y)
        sum_remote(copies, PF, 2, 0)
        gather_finish(moves)

        def halves(ref):
            return lambda at: ref[:, :, pl.ds(at, half)].reshape(-1, half)

        split_grad(G[layer], halves(DF), base, 0, 4)
        tick(2)
        for own_side in (False, True):
            left = N1B[layer, :, :, pl.ds(side_of(own_side), half)].reshape(own_rows, half)
            for at in range(2):
                put_units(own_side, base, 4 + 2 * at, 2, tn(left, DU[:, at * half : (at + 1) * half]))
            if not own_side:
                send_units(base, 4, 4)
        tick(3)
        only = jnp.where(t == 0, 1.0, 0.0)
        put_vec(layer, 0, only * jnp.sum(DF[...].reshape(own_rows, width).astype(F32), axis=0, keepdims=True))
        put_vec(layer, 14 + t, jnp.sum(DU[...].astype(F32), axis=0, keepdims=True))

        moves = gather_copies(DA, g4_s.at[layer, 2], g4_r.at[layer, 2])
        for ch in range(PIECES):
            d_normed = DR[piece(ch)] + sum_finish(copies, PF, 2, 0, ch)
            rstd = SD1[layer, piece(ch)][:, :1]
            d_first = norm_backward(d_normed, XH1[layer, piece(ch)], rstd, full_vec(layer, 6))
            DA[t, piece(ch)] = d_first.astype(BF16)
            gather_start(moves, ch)
            DR1[piece(ch)] = d_first
            DR[piece(ch)] = d_normed
        put_vec(layer, 2, jnp.sum(DR[...] * XH1[layer], axis=0, keepdims=True))
        put_vec(layer, 3, jnp.sum(DR[...], axis=0, keepdims=True))

        def back_out(at):
            where = pl.ds(pl.multiple_of(at * 2 * rows, 2 * rows), 2 * rows)
            block = DA[pl.ds(at * 2, 2)].reshape(2 * rows, width)
            DOB[where] = nt(block, WO[layer]).astype(BF16)

        gather_near(moves)
        back_out(y)
        tick(4, 5)
        gather_remote(moves)
        back_out(1 - y)
        gather_finish(moves)
        split_grad(OB[layer], halves(DA), base, 8, 1)
        put_vec(layer, 1, only * jnp.sum(DA[...].reshape(own_rows, width).astype(F32), axis=0, keepdims=True))

        DKF[...] = jnp.zeros_like(DKF)
        DVF[...] = jnp.zeros_like(DVF)

        def back_attend(at, inner):
            where = pl.ds(pl.multiple_of(at * tile, tile), tile)
            grad_tile = DOB[where]
            q_tile = Q[layer, where]
            product = grad_tile.astype(F32) * OB[layer, where].astype(F32)
            d_query = []
            for head in range(3):
                lanes = slice(2 * HD, 3 * HD) if head == 2 else slice(0, 2 * HD)
                d_mix = head_cols(grad_tile, head)
                d_prob = nt(d_mix, head_full(V[layer], head))
                total = jnp.sum(head_cols(product, head), axis=-1, keepdims=True)
                low = PB[layer, head, where]
                d_score = (low.astype(F32) * (d_prob - total)).astype(BF16)
                d_query.append(nn(d_score, head_full(K[layer], head)))
                DKF[:, lanes] += tn(d_score, head_cols(q_tile, head))
                DVF[:, lanes] += tn(low, d_mix)
            scale = HD**-0.5
            DQ[where, : 2 * HD] = (jnp.where(lane_low, d_query[0], d_query[1]) * scale).astype(BF16)
            DQ[where, 2 * HD :] = (d_query[2] * scale).astype(BF16)
            return inner

        tick(6)
        lax.fori_loop(0, 2, back_attend, 0)
        tick(7)
        DK[...] = DKF[...].astype(BF16)
        DV[...] = DVF[...].astype(BF16)

        def back_in(at, with_q):
            where = pl.ds(pl.multiple_of(at * rows, 2 * rows), 2 * rows)
            total = nn(DK[where], WQ[layer, cols : 2 * cols]) + nn(DV[where], WQ[layer, 2 * cols :])
            if with_q:
                mine = pl.ds(pl.multiple_of((at - own) * rows, 2 * rows), 2 * rows)
                total = total + nn(DQ[mine], WQ[layer, :cols])
            PF[pl.ds(at, 2)] = total.reshape(2, rows, width)

        pf_far = PF.at[pl.ds(far, 4)]
        pf_own = PF.at[pl.ds(own, 4)]
        far_copies = sum_copies(3, 1)
        back_in(far + 2 * (1 - y), False)
        sum_remote(far_copies, pf_far, 3, 1)
        back_in(far + 2 * y, False)
        sum_local(far_copies, pf_far, 3, 1)
        copies = sum_copies(4, 0)
        back_in(own + 2 * (1 - y), True)
        sum_remote(copies, pf_own, 4, 0)
        back_in(own + 2 * y, True)
        sum_local(copies, pf_own, 4, 0)
        for ch in range(PIECES):
            ZS[piece(ch)] = sum_finish(far_copies, pf_far, 3, 1, ch).astype(BF16)
            across(layer, ch).start()
        tick(8, 9)

        def block_cols(ref, start, count):
            return lambda at: ref[pl.ds(start, count), :, pl.ds(at, half)].reshape(-1, half)

        xb = XB.at[layer]
        split_grad(DQ[...], block_cols(xb, own, 4), base, 9, 1)
        split_grad(DK[...], block_cols(xb, 0, 8), base, 10, 1)
        split_grad(DV[...], block_cols(xb, 0, 8), base, 11, 1)
        tick(10)
        put_vec(layer, 6 + t, jnp.sum(DQ[...].astype(F32), axis=0, keepdims=True))
        put_vec(layer, 10 + t, jnp.sum(DV[...].astype(F32), axis=0, keepdims=True))

        tick(11)
        return carry

    lax.fori_loop(0, LAYERS, backward_layer, 0)
    for ch in range(PIECES):
        CO[piece(ch)] = layer_grad(0, ch).astype(BF16)
    collect_start(CO, OG, 3)
    vec_move(0)
    if fused:
        more = LAGS[3]
        for i in range(more):
            if i in VEC_TICKS:
                vec_move(1 + VEC_TICKS.index(i))
            advance(total_units + i)
        vec_move(5)

        def drain(i, carry):
            pltpu.make_async_copy(GO.at[i], out_mat.at[i], om_sem.at[i]).wait()
            return carry

        lax.fori_loop(0, total_units, drain, 0)
        for layer in range(LAYERS):
            fetch_drain(layer)
    else:
        own_out = pltpu.make_async_copy(GO, out_mat.at[0], om_sem.at[0])
        far_out = pltpu.make_async_copy(XR, out_mat.at[1], om_sem.at[1])
        own_out.start()
        far_out.start()
        own_out.wait()
        far_out.wait()
    out_vec[...] = OV[...]
    collect_wait(TK, OT, 2)
    out_tok[...] = OT[...]
    collect_wait(CO, OG, 3)
    out_grad[...] = OG[...]


def finish_kernel(dims, *refs):
    tok_ref, grad_ref, mat_ref, vec_ref = refs[:4]
    out_tok, out_grad, out_q, out_k, out_v, out_o, out_i, out_u = refs[4:12]
    vec_q, vec_v, vec_o, vec_i, vec_u, gain_1, shift_1, gain_2, shift_2 = refs[12:]
    width, cols, units, half = dims
    layer = pl.program_id(0)
    s = lax.axis_index("shard")

    @pl.when(layer == 0)
    def _():
        out_tok[...] = tok_ref[...]
        out_grad[...] = grad_ref[...].astype(F32)

    for i in range(4):
        out_u[0, i * cols : (i + 1) * cols, :] = mat_ref[i].astype(F32)
        r, cc = i % 2, i // 2
        out_i[0, r * cols : (r + 1) * cols, cc * half : (cc + 1) * half] = mat_ref[4 + i].astype(F32)
    out_o[0] = mat_ref[8].astype(F32)
    out_q[0] = mat_ref[9].astype(F32)
    out_k[0] = mat_ref[10].astype(F32)
    out_v[0] = mat_ref[11].astype(F32)
    line = pl.ds(layer, 1)
    at = pl.ds(pl.multiple_of(s * half, half), half)
    for row, ref in ((0, vec_u), (1, vec_o), (2, gain_1), (3, shift_1), (4, gain_2), (5, shift_2)):
        ref[line, :] = vec_ref[0, row : row + 1, at]
    for row, ref in ((6, vec_q), (10, vec_v)):
        first = vec_ref[0, pl.ds(row + 2 * s, 1), :cols]
        second = vec_ref[0, pl.ds(row + 1 + 2 * s, 1), :cols]
        ref[line, :] = jnp.concatenate([first, second], axis=1)
    vec_i[line, :width] = vec_ref[0, pl.ds(14 + 2 * s, 1)]
    vec_i[line, width:] = vec_ref[0, pl.ds(15 + 2 * s, 1)]


def per_device(
    tokens,
    cotangent,
    segment_ids,
    lengths,
    query_weight,
    key_weight,
    value_weight,
    output_weight,
    inner_weight,
    outer_weight,
    query_bias,
    value_bias,
    output_bias,
    inner_bias,
    outer_bias,
    first_gain,
    first_shift,
    second_gain,
    second_shift,
):
    shards = lax.axis_size("shard")
    assert lax.axis_size("ctx") == 4 and lax.axis_size("tp") == 4 and tokens.shape[0] == 2
    fused = shards == 2
    seqs, part, width = tokens.shape
    cols = query_weight.shape[2]
    units = inner_weight.shape[2]
    half = width // 2
    rows = 2 * part
    own_rows, all_rows = 4 * rows, 8 * rows
    assert cols == 3 * HD and segment_ids.shape[1] == all_rows and units == width == 4 * cols

    def turned(mat):
        return jnp.swapaxes(mat, 1, 2)

    mats = (
        turned(query_weight),
        turned(key_weight),
        turned(value_weight),
        output_weight,
        inner_weight,
        outer_weight,
    )
    vecs = (query_bias, value_bias, output_bias, outer_bias, inner_bias, first_gain, first_shift, second_gain, second_shift)
    if not fused:
        mats = tuple(
            lax.all_gather(mat, "shard", axis=axis, tiled=True) for mat, axis in zip(mats, (2, 2, 2, 2, 1, 2))
        )
        vecs = tuple(lax.all_gather(vec, "shard", axis=1, tiled=True) for vec in vecs)

    n_units = 12 * LAYERS
    out_shape = [
        jax.ShapeDtypeStruct((2, part, width), BF16),
        jax.ShapeDtypeStruct((2, part, width), BF16),
        jax.ShapeDtypeStruct((n_units, cols, half) if fused else (2, n_units, cols, half), BF16),
        jax.ShapeDtypeStruct((LAYERS, VEC_ROWS, width), F32),
    ]
    vm = pltpu.VMEM
    dma = pltpu.SemaphoreType.DMA
    scratch = [
        vm((LAYERS, 3 * cols, width), BF16),
        vm((LAYERS, cols, width), BF16),
        vm((LAYERS, width, units), BF16),
        vm((LAYERS, units, width), BF16),
        vm((2, LAYERS, 16, half), F32),
        vm((own_rows, 128), F32),
        vm((8, all_rows), F32),
        vm((rows, width), F32),
        vm((rows, width), F32),
        vm((rows, width), F32),
        vm((rows, width), F32),
        vm((rows, width), BF16),
        vm((rows, width), BF16),
        vm((2, part, width), BF16),
        vm((2, part, width), BF16),
        vm((LAYERS, rows, width), F32),
        vm((LAYERS, rows, width), F32),
        vm((LAYERS, rows, 128), F32),
        vm((LAYERS, rows, 128), F32),
        vm((LAYERS, 8, rows, width), BF16),
        vm((LAYERS, own_rows, cols), BF16),
        vm((LAYERS, all_rows, cols), BF16),
        vm((LAYERS, all_rows, cols), BF16),
        vm((LAYERS, own_rows, cols), BF16),
        vm((LAYERS, 4, rows, width), BF16),
        vm((LAYERS, own_rows, units), BF16),
        vm((LAYERS, own_rows, units), BF16),
        vm((LAYERS, 3, own_rows, all_rows), BF16),
        vm((4, rows, width), BF16),
        vm((4, rows, width), BF16),
        vm((own_rows, units), BF16),
        vm((own_rows, cols), BF16),
        vm((own_rows, cols), BF16),
        vm((all_rows, cols), BF16),
        vm((all_rows, cols), BF16),
        vm((all_rows, cols), F32),
        vm((all_rows, cols), F32),
        vm((8, rows, width), F32),
        vm((2, 3, rows, width), BF16),
        vm((5, 3, rows, width), BF16),
        vm((rows, width), BF16),
        vm((LAYERS, rows, width), BF16),
        vm((n_units, cols, half), BF16),
        vm((12, cols, half), BF16),
        vm((n_units, cols, half), BF16),
        vm((n_units, cols, half), BF16),
        vm((n_units, cols, half), BF16),
        vm((LAYERS, VEC_ROWS, width), F32),
        vm((5, LAYERS, VEC_ROWS, width), F32),
        dma((LAYERS, 6)),
        dma((LAYERS, 13)),
        dma((LAYERS, 13)),
        dma((LAYERS, 12)),
        dma((LAYERS, 12)),
        dma((5,)),
        dma((5,)),
        dma((4, 2)),
        dma((4, 2)),
        dma((LAYERS, 7 * PIECES)),
        dma((LAYERS, 7 * PIECES)),
        dma((LAYERS, 3, 3 * PIECES)),
        dma((LAYERS, 3, 3 * PIECES)),
        dma((5, 2 * PIECES + 1)),
        dma((5, 2 * PIECES + 1)),
        dma((LAYERS, PIECES)),
        dma((LAYERS, PIECES)),
        dma((n_units,)),
        dma((n_units,)),
        dma((n_units,)),
        dma((n_units,)),
        dma((n_units,)),
        dma((n_units,)),
        dma((n_units,)),
        dma((n_units,)),
        dma((n_units,)),
    ]
    vmem = pl.BlockSpec(memory_space=pltpu.VMEM)
    hbm = pl.BlockSpec(memory_space=pl.ANY)
    layer_out, grad_tokens, grad_mats, grad_vecs = pl.pallas_call(
        functools.partial(step_kernel, (width, cols, units, half), fused),
        out_shape=out_shape,
        in_specs=[vmem] * 12 + [pl.BlockSpec(memory_space=pltpu.SMEM)] + [hbm] * 6,
        out_specs=[vmem, vmem, hbm, vmem],
        scratch_shapes=scratch,
        compiler_params=pltpu.CompilerParams(
            collective_id=0, has_side_effects=True, vmem_limit_bytes=67043328
        ),
        name="encoder_step",
    )(tokens, cotangent, segment_ids, *vecs, lengths, *mats)

    if fused:
        dims = (width, cols, units, half)
        layer_block = lambda *shape: pl.BlockSpec((1,) + shape, lambda i: (i,) + (0,) * len(shape))
        whole = lambda *shape: pl.BlockSpec(shape, lambda i: (0,) * len(shape))
        mat_shapes = [(cols, half)] * 4 + [(half, units), (units, half)]
        vec_lens = (half, half, half, 4 * half, half, half, half, half, half)
        outs = pl.pallas_call(
            functools.partial(finish_kernel, dims),
            grid=(LAYERS,),
            out_shape=[
                jax.ShapeDtypeStruct((2, part, width), BF16),
                jax.ShapeDtypeStruct((2, part, width), F32),
            ]
            + [jax.ShapeDtypeStruct((LAYERS,) + shape, F32) for shape in mat_shapes]
            + [jax.ShapeDtypeStruct((LAYERS, count), F32) for count in vec_lens],
            in_specs=[
                whole(2, part, width),
                whole(2, part, width),
                pl.BlockSpec((12, cols, half), lambda i: (LAYERS - 1 - i, 0, 0)),
                layer_block(VEC_ROWS, width),
            ],
            out_specs=[whole(2, part, width), whole(2, part, width)]
            + [layer_block(*shape) for shape in mat_shapes]
            + [whole(LAYERS, count) for count in vec_lens],
            name="write_out",
        )(layer_out, grad_tokens, grad_mats, grad_vecs)
        return tuple(outs[:2]) + tuple(turned(mat) for mat in outs[2:5]) + tuple(outs[5:])

    mats = grad_mats.reshape(2, LAYERS, 12, cols, half)[:, ::-1]
    wide = jnp.concatenate([mats[0], mats[1]], axis=-1)
    wide = jnp.concatenate([wide[:, :4], wide[:, 8:]], axis=1)
    wide = lax.psum(lax.psum_scatter(wide, "shard", scatter_dimension=3, tiled=True), "ctx").astype(F32)
    inner = mats[:, :, 4:8].reshape(2, LAYERS, 2, 2, cols, half)
    inner = jnp.transpose(inner, (1, 0, 3, 4, 2, 5)).reshape(LAYERS, width, units)
    inner = lax.psum(lax.psum_scatter(inner, "shard", scatter_dimension=1, tiled=True), "ctx").astype(F32)
    grad_outer = wide[:, :4].reshape(LAYERS, units, -1)
    grad_output = wide[:, 4]
    grad_query, grad_key, grad_value = (turned(wide[:, 5 + at]) for at in range(3))

    total = lax.psum(grad_vecs, ("shard", "ctx", "tp"))
    at = lax.axis_index("shard")

    def owned(vec):
        count = vec.shape[1] // shards
        return lax.dynamic_slice_in_dim(vec, at * count, count, 1)

    vec_query = owned(total[:, 6:10, :cols].reshape(LAYERS, -1))
    vec_value = owned(total[:, 10:14, :cols].reshape(LAYERS, -1))
    vec_inner = owned(total[:, 14:18].reshape(LAYERS, -1))
    vec_outer, vec_output, gain_one, shift_one, gain_two, shift_two = (owned(total[:, row]) for row in range(6))
    return (
        layer_out,
        grad_tokens.astype(F32),
        grad_query,
        grad_key,
        grad_value,
        grad_output,
        inner,
        grad_outer,
        vec_query,
        vec_value,
        vec_output,
        vec_inner,
        vec_outer,
        gain_one,
        shift_one,
        gain_two,
        shift_two,
    )


def solution(mesh):
    rows = P("shard", ("ctx", "tp"), None)
    down = P(None, "shard", "tp")
    across = P(None, "tp", "shard")
    vector = P(None, "shard")
    mats = (down, down, down, across, down, across)
    return jax.shard_map(
        per_device,
        mesh=mesh,
        in_specs=(rows, rows, P("shard", None), P("shard")) + mats + (vector,) * 9,
        out_specs=(rows, rows) + mats + (vector,) * 9,
        check_vma=False,
    )
```

```python
import functools

import jax
import jax.numpy as jnp
from jax import lax
from jax.experimental import pallas as pl
from jax.experimental.pallas import tpu as pltpu
from jax.sharding import PartitionSpec as P

HD = 64
LAYERS = 2
EPSILON = 1e-05
MESH = pl.DeviceIdType.MESH
F32 = jnp.float32
BF16 = jnp.bfloat16
NEG = -1e30
VEC_ROWS = 32
PIECES = 4
RING = 8
LAGS = (4, 6, 8, 10)
VEC_TICKS = (0, 1, 4, 6, 8, 9)


def nn(a, b):
    return jnp.dot(a, b, preferred_element_type=F32)


def nt(a, b):
    return lax.dot_general(a, b, (((1,), (1,)), ((), ())), preferred_element_type=F32)


def tn(a, b):
    return lax.dot_general(a, b, (((0,), (0,)), ((), ())), preferred_element_type=F32)


def norm_forward(resid, gain, shift):
    center = resid - jnp.mean(resid, axis=-1, keepdims=True)
    spread = jnp.mean(center * center, axis=-1, keepdims=True)
    rstd = lax.rsqrt(spread + EPSILON)
    xhat = center * rstd
    return xhat * gain + shift, xhat, rstd


def norm_backward(grad, xhat, rstd, gain):
    scaled = grad * gain
    first = jnp.mean(scaled, axis=-1, keepdims=True)
    second = jnp.mean(scaled * xhat, axis=-1, keepdims=True)
    return rstd * (scaled - first - xhat * second)


def step_kernel(dims, fused, *refs):
    (
        tok_ref,
        cot_ref,
        seg_ref,
        vec_refs,
        len_ref,
        wq_ref,
        wk_ref,
        wv_ref,
        wo_ref,
        wi_ref,
        wu_ref,
        out_tok,
        out_grad,
        out_mat,
        out_vec,
        WQ,
        WO,
        WI,
        WU,
        VB,
        IDC,
        IDR,
        H,
        N1,
        DR,
        DR1,
        TK,
        CO,
        OT,
        OG,
        XH1,
        XH2,
        SD1,
        SD2,
        XB,
        Q,
        K,
        V,
        OB,
        N1B,
        G,
        GP,
        PB,
        DF,
        DA,
        DU,
        DOB,
        DQ,
        DK,
        DV,
        DKF,
        DVF,
        PF,
        SB,
        RB,
        ZS,
        ZR,
        GO,
        GS,
        XR,
        YR,
        Y2,
        OV,
        VR,
        VQ,
        OW,
        wl_sem,
        ws_sem,
        wr_sem,
        wz_s,
        wz_r,
        v_s,
        v_r,
        rd_s,
        rd_r,
        g8_s,
        g8_r,
        g4_s,
        g4_r,
        rs_s,
        rs_r,
        rz_s,
        rz_r,
        xs_s,
        xs_r,
        z1_s,
        z1_r,
        z2_s,
        z2_r,
        z3_s,
        z3_r,
        om_sem,
    ) = refs[:3] + (refs[3:12],) + refs[12:]
    width, cols, units, half = dims
    seqs, part = tok_ref.shape[0], tok_ref.shape[1]
    rows = 2 * part
    own_rows = 4 * rows
    all_rows = 8 * rows
    tall = rows // PIECES
    s = lax.axis_index("shard")
    c = lax.axis_index("ctx")
    t = lax.axis_index("tp")
    hf = lax.rem(c, 2)
    y = t // 2
    k = lax.rem(t, 2)
    tc = t + 1 - 2 * k
    ty = lax.rem(t + 2, 4)
    zp = c + 1 - 2 * hf
    is_inner = jnp.logical_or(c == 1, c == 2)
    is_outer = jnp.logical_not(is_inner)
    z_in = jnp.where(c == 0, 1, 2)
    z_mid = 3 - c
    z_out = jnp.where(c == 1, 0, 3)

    def rc(src, dst, ssem, rsem, cc, tt, ss=None):
        return pltpu.make_async_remote_copy(
            src_ref=src,
            dst_ref=dst,
            send_sem=ssem,
            recv_sem=rsem,
            device_id=(s if ss is None else ss, cc, tt),
            device_id_type=MESH,
        )

    bar = pltpu.get_barrier_semaphore()
    for dc in range(4):
        for dt in range(4):
            if dc or dt:
                pl.semaphore_signal(
                    bar,
                    1,
                    device_id=(s, lax.rem(c + dc, 4), lax.rem(t + dt, 4)),
                    device_id_type=MESH,
                )
    if fused:
        pl.semaphore_signal(bar, 1, device_id=(1 - s, c, t), device_id_type=MESH)

    def unit_view(layer, item, side):
        at = pl.multiple_of(side * half, half)
        lanes = pl.ds(at, half)
        if item < 3:
            return WQ.at[layer, pl.ds(item * cols, cols), lanes]
        if item == 3:
            return WO.at[layer, :, lanes]
        if item < 8:
            return WI.at[layer, pl.ds(at + (item - 4) * (half // 4), half // 4)]
        return WU.at[layer, pl.ds((item - 8) * cols, cols), lanes]

    def unit_arg(layer, item):
        if item < 4:
            return (wq_ref, wk_ref, wv_ref, wo_ref)[item].at[layer]
        if item < 8:
            return wi_ref.at[layer, pl.ds((item - 4) * (half // 4), half // 4)]
        return wu_ref.at[layer, pl.ds((item - 8) * cols, cols)]

    def local_copy(layer, item):
        lanes = pl.ds(pl.multiple_of(s * half, half), half) if fused else pl.ds(0, width)
        if item < 3:
            src, dst = (wq_ref, wk_ref, wv_ref)[item], WQ.at[layer, pl.ds(item * cols, cols), lanes]
        elif item == 3:
            src, dst = wo_ref, WO.at[layer, :, lanes]
        elif item == 4:
            src, dst = wi_ref, WI.at[layer, lanes]
        else:
            src, dst = wu_ref, WU.at[layer, :, lanes]
        return pltpu.make_async_copy(src.at[layer], dst, wl_sem.at[layer, item])

    def over_x(layer, item):
        return rc(
            unit_arg(layer, item),
            unit_view(layer, item, s),
            ws_sem.at[layer, item if item < 4 else 2 + item // 2],
            wr_sem.at[layer, item if item < 4 else 2 + item // 2],
            c,
            t,
            1 - s,
        )

    def over_z(layer, item):
        view = unit_view(layer, item, 1 - s)
        return rc(view, view, wz_s.at[layer, item // 2], wz_r.at[layer, item // 2], zp, t)

    def direct(layer, item):
        return jnp.logical_and(layer == 0, item < 4)

    def mine_over_x(layer, item):
        return jnp.logical_or(direct(layer, item), hf == item % 2)

    def fetch_start(layer, item):
        @pl.when(mine_over_x(layer, item))
        def _():
            over_x(layer, item).start()

    def fetch_pass(layer, items):
        if fused:
            for item in items:

                @pl.when(hf == item % 2)
                def _():
                    over_x(layer, item).wait_recv()
                    over_z(layer, item).start()

    def fetch_wait(layer, items):
        for item in items:
            local_copy(layer, {0: 0, 1: 1, 2: 2, 3: 3, 4: 4, 8: 5}[item]).wait() if item in (0, 1, 2, 3, 4, 8) else None
            if fused:

                @pl.when(direct(layer, item))
                def _():
                    over_x(layer, item).wait_recv()

                @pl.when(jnp.logical_not(mine_over_x(layer, item)))
                def _():
                    over_z(layer, item).wait_recv()

    def fetch_drain(layer):
        for item in range(12):

            @pl.when(mine_over_x(layer, item))
            def _():
                over_x(layer, item).wait_send()

            @pl.when(jnp.logical_and(hf == item % 2, jnp.logical_not(direct(layer, item))))
            def _():
                over_z(layer, item).wait_send()

    def fill_vectors(side, at):
        for layer in range(LAYERS):
            for place, ref in ((0, vec_refs[0]), (2, vec_refs[1])):
                value = ref[...].astype(F32)[layer : layer + 1, at : at + half]
                VB[side, layer, place : place + 1, :cols] = value[:, :cols]
                VB[side, layer, place + 1 : place + 2, :cols] = value[:, cols:]
            for place, ref in zip((4, 5, 6, 7, 8, 9), vec_refs[2:4] + vec_refs[5:9]):
                VB[side, layer, place : place + 1] = ref[...].astype(F32)[layer : layer + 1, at : at + half]
            value = vec_refs[4][...].astype(F32)[layer : layer + 1, 4 * at : 4 * at + 4 * half]
            for j in range(4):
                VB[side, layer, 10 + j : 11 + j] = value[:, j * half : (j + 1) * half]

    for layer in range(LAYERS):
        for item in range(6):
            local_copy(layer, item).start()
    if fused:
        fill_vectors(s, 0)
    else:
        fill_vectors(0, 0)
        fill_vectors(1, half)
    b_me = c // 2
    ids = seg_ref[pl.ds(b_me, 1)]
    places = lax.broadcasted_iota(jnp.int32, ids.shape, 1)
    ids = jnp.where(places < len_ref[b_me], ids, -1).astype(F32)
    IDR[...] = jnp.broadcast_to(ids, IDR.shape)
    own_ids = jnp.where(hf == 0, ids[:, :own_rows], ids[:, own_rows:])
    IDC[...] = jnp.broadcast_to(own_ids, (128, own_rows)).T
    OV[...] = jnp.zeros_like(OV)
    pl.semaphore_wait(bar, 16 if fused else 15)

    spread_t = 2 * hf + y

    def spread_copies(src_ref, dst_ref, which):
        return [
            (
                jnp.logical_and(2 * b + c // 2 == c, spread_t == t),
                rc(
                    src_ref.at[b],
                    dst_ref.at[pl.ds(k * part, part)],
                    rd_s.at[which, b],
                    rd_r.at[which, k],
                    2 * b + c // 2,
                    spread_t,
                ),
            )
            for b in range(2)
        ]

    def spread_start(src_ref, dst_ref, which):
        for b, (mine, copy) in enumerate(spread_copies(src_ref, dst_ref, which)):

            @pl.when(mine)
            def _():
                dst_ref[pl.ds(pl.multiple_of(k * part, part), part), :] = src_ref[b]

            @pl.when(jnp.logical_not(mine))
            def _():
                copy.start()

    def spread_wait(src_ref, dst_ref, which):
        for mine, copy in spread_copies(src_ref, dst_ref, which):

            @pl.when(jnp.logical_not(mine))
            def _():
                copy.wait_send()

        for kk in range(2):
            mine = jnp.logical_and(2 * hf + y == c, 2 * k + kk == t)

            @pl.when(jnp.logical_not(mine))
            def _():
                rc(
                    src_ref.at[0],
                    dst_ref.at[pl.ds(kk * part, part)],
                    rd_s.at[which, 0],
                    rd_r.at[which, kk],
                    c,
                    t,
                ).wait_recv()

    def collect_copies(src_ref, dst_ref, which):
        return [
            (
                jnp.logical_and(2 * hf + y == c, 2 * k + kk == t),
                rc(
                    src_ref.at[pl.ds(kk * part, part)],
                    dst_ref.at[b_me],
                    rd_s.at[which, kk],
                    rd_r.at[which, b_me],
                    2 * hf + y,
                    2 * k + kk,
                ),
            )
            for kk in range(2)
        ]

    def collect_start(src_ref, dst_ref, which):
        for kk, (mine, copy) in enumerate(collect_copies(src_ref, dst_ref, which)):

            @pl.when(mine)
            def _():
                dst_ref[b_me] = src_ref[kk * part : (kk + 1) * part, :]

            @pl.when(jnp.logical_not(mine))
            def _():
                copy.start()

    def collect_wait(src_ref, dst_ref, which):
        for mine, copy in collect_copies(src_ref, dst_ref, which):

            @pl.when(jnp.logical_not(mine))
            def _():
                copy.wait_send()

        for b in range(2):
            mine = jnp.logical_and(2 * b + c // 2 == c, spread_t == t)

            @pl.when(jnp.logical_not(mine))
            def _():
                rc(
                    src_ref.at[pl.ds(0, part)],
                    dst_ref.at[b],
                    rd_s.at[which, 0],
                    rd_r.at[which, b],
                    c,
                    t,
                ).wait_recv()

    spread_start(tok_ref, TK, 0)
    if fused:
        vec_copy = rc(VB.at[s], VB.at[s], ws_sem.at[0, 8], wr_sem.at[0, 8], c, t, 1 - s)
        vec_copy.start()
        for layer in range(LAYERS):
            for item in range(12):
                fetch_start(layer, item)
    spread_start(cot_ref, CO, 1)

    def piece(ch):
        return slice(ch * tall, (ch + 1) * tall)

    def gather_copies(buf):
        def move(slot, ch, at, tt):
            view = buf.at[slot, pl.ds(ch * tall, tall)]
            return rc(view, view, g4_s.at[3 * ch + at], g4_r.at[3 * ch + at], c, tt)

        return [(move(t, ch, 0, tc), move(t, ch, 1, ty), move(ty, ch, 2, tc)) for ch in range(PIECES)]

    def gather_start(copies, ch):
        copies[ch][1].start()
        copies[ch][0].start()

    def gather_near(copies):
        for to_c, _, _ in copies:
            to_c.wait_recv()

    def gather_remote(copies):
        for _, to_y, y_to_c in copies:
            to_y.wait_recv()
            y_to_c.start()
        for _, _, y_to_c in copies:
            y_to_c.wait_recv()

    def gather_finish(copies):
        for moves in copies:
            for copy in moves:
                copy.wait_send()

    def sum_copies(slot, lane):
        def move(at, ch, tt):
            where = pl.ds(ch * tall, tall)
            sem = PIECES * at + ch
            return rc(SB.at[lane, at, where], RB.at[slot, at, where], rs_s.at[lane, sem], rs_r.at[lane, sem], c, tt)

        pairs = [(move(0, ch, tc), move(1, ch, ty)) for ch in range(PIECES)]
        last = 2 * PIECES
        return pairs, rc(SB.at[lane, 2], RB.at[slot, 2], rs_s.at[lane, last], rs_r.at[lane, last], c, tc)

    def sum_remote(copies, pf, slot, lane):
        for ch, (to_c, _) in enumerate(copies[0]):
            SB[lane, 0, piece(ch)] = pf[(1 - y) * 2 + 1 - k, piece(ch)].astype(BF16)
            to_c.start()
        for ch, (to_c, to_y) in enumerate(copies[0]):
            to_c.wait_recv()
            SB[lane, 1, piece(ch)] = (pf[ty, piece(ch)] + RB[slot, 0, piece(ch)].astype(F32)).astype(BF16)
            to_y.start()

    def sum_local(copies, pf, slot, lane):
        SB[lane, 2] = pf[tc].astype(BF16)
        copies[1].start()

    def sum_finish(copies, pf, slot, lane, ch):
        pairs, near = copies
        if ch == 0:
            near.wait_recv()
        partial = pf[t, piece(ch)] + RB[slot, 2, piece(ch)].astype(F32)
        pairs[ch][1].wait_recv()
        if ch == PIECES - 1:
            for to_c, to_y in pairs:
                to_c.wait_send()
                to_y.wait_send()
            near.wait_send()
        return partial + RB[slot, 1, piece(ch)].astype(F32)

    def full_vec(layer, row):
        return jnp.concatenate([VB[0, layer, row : row + 1], VB[1, layer, row : row + 1]], axis=1)

    def vec_at(layer, row, lanes):
        return VB[y, layer, pl.ds(row, 1)][:, :lanes]

    def put_vec(layer, row, value):
        OV[layer, pl.ds(row, 1), : value.shape[1]] = value

    if fused:
        vec_copy.wait()
    spread_wait(tok_ref, TK, 0)
    own = hf * 4
    far = (1 - hf) * 4

    def input_copies(layer):
        buf = XB.at[layer]

        def move(slot, ch, at, cc, tt):
            view = buf.at[slot, pl.ds(ch * tall, tall)]
            return rc(view, view, g8_s.at[layer, 7 * ch + at], g8_r.at[layer, 7 * ch + at], cc, tt)

        return [
            (
                move(own + t, ch, 0, c, ty),
                move(own + t, ch, 1, zp, t),
                move(own + t, ch, 2, c, tc),
                move(own + ty, ch, 3, c, tc),
                move(far + t, ch, 4, c, ty),
                move(far + t, ch, 5, c, tc),
                move(far + ty, ch, 6, c, tc),
            )
            for ch in range(PIECES)
        ]

    def input_start(layer, ch):
        for copy in input_copies(layer)[ch][:3]:
            copy.start()

    H[...] = TK[...].astype(F32)
    XB[0, own + t] = TK[...]
    for ch in range(PIECES):
        input_start(0, ch)
    lane_low = lax.broadcasted_iota(jnp.int32, (1, 2 * HD), 1) < HD

    def head_cols(value, head):
        if head == 2:
            return value[:, 2 * HD : 3 * HD]
        keep = lane_low if head == 0 else jnp.logical_not(lane_low)
        return jnp.where(keep, value[:, : 2 * HD], jnp.zeros_like(value[:, : 2 * HD]))

    def head_full(value, head):
        return value[:, 2 * HD : 3 * HD] if head == 2 else value[:, : 2 * HD]

    tile = own_rows // 2

    def forward_layer(layer, carry):
        arrivals = input_copies(layer)
        fetch_wait(layer, (0, 1, 2))

        def project(at, with_q):
            block = XB[layer, pl.ds(at, 2)].reshape(2 * rows, width)
            where = pl.ds(pl.multiple_of(at * rows, 2 * rows), 2 * rows)
            if with_q:
                mine = pl.ds(pl.multiple_of((at - own) * rows, 2 * rows), 2 * rows)
                qb = vec_at(layer, k, cols)
                q_low = (nt(block, WQ[layer, :cols]) + qb).astype(BF16)
                Q[layer, mine] = q_low * jnp.asarray(HD**-0.5, BF16)
            K[layer, where] = nt(block, WQ[layer, cols : 2 * cols]).astype(BF16)
            V[layer, where] = (nt(block, WQ[layer, 2 * cols :]) + vec_at(layer, 2 + k, cols)).astype(BF16)

        for moves in arrivals:
            moves[2].wait_recv()
        project(own + 2 * y, True)
        for moves in arrivals:
            moves[1].wait_recv()
            moves[4].start()
            moves[5].start()
            moves[0].wait_recv()
            moves[3].start()
        for moves in arrivals:
            moves[3].wait_recv()
        project(own + 2 * (1 - y), True)
        for moves in arrivals:
            moves[5].wait_recv()
        project(far + 2 * y, False)
        for moves in arrivals:
            moves[4].wait_recv()
            moves[6].start()
        for moves in arrivals:
            moves[6].wait_recv()
        project(far + 2 * (1 - y), False)
        for moves in arrivals:
            for copy in moves:
                copy.wait_send()
        fetch_pass(layer, (4, 5))

        def attend(at, inner):
            where = pl.ds(pl.multiple_of(at * tile, tile), tile)
            ids = IDC[where][:, :1] == IDR[:1]
            q_tile = Q[layer, where]
            mixed = []
            for head in range(3):
                scores = nt(head_cols(q_tile, head), head_full(K[layer], head))
                scores = jnp.where(ids, scores, NEG)
                top = jnp.max(scores, axis=-1, keepdims=True)
                expo = jnp.exp(scores - top)
                low = (expo / jnp.sum(expo, axis=-1, keepdims=True)).astype(BF16)
                PB[layer, head, where] = low
                mixed.append(nn(low, head_full(V[layer], head)))
            OB[layer, where, : 2 * HD] = jnp.where(lane_low, mixed[0], mixed[1]).astype(BF16)
            OB[layer, where, 2 * HD :] = mixed[2].astype(BF16)
            return inner

        lax.fori_loop(0, 2, attend, 0)
        fetch_wait(layer, (3,))
        fetch_pass(layer, (6, 7))

        def project_out(at):
            where = pl.ds(pl.multiple_of(at * 2 * rows, 2 * rows), 2 * rows)
            PF[pl.ds(at * 2, 2)] = nn(OB[layer, where], WO[layer]).reshape(2, rows, width)

        copies = sum_copies(0, 0)
        project_out(1 - y)
        sum_remote(copies, PF, 0, 0)
        project_out(y)
        sum_local(copies, PF, 0, 0)
        fetch_pass(layer, (8, 9))
        moves = gather_copies(N1B.at[layer])
        for ch in range(PIECES):
            branch = sum_finish(copies, PF, 0, 0, ch) + full_vec(layer, 4)
            resid = H[piece(ch)] + branch
            normed, xhat, rstd = norm_forward(resid, full_vec(layer, 6), full_vec(layer, 7))
            N1B[layer, t, piece(ch)] = normed.astype(BF16)
            gather_start(moves, ch)
            N1[piece(ch)] = normed
            XH1[layer, piece(ch)] = xhat
            SD1[layer, piece(ch)] = jnp.broadcast_to(rstd, (tall, 128))
        fetch_pass(layer, (10, 11))
        fetch_wait(layer, (4, 5, 6, 7))

        def feed(at):
            where = pl.ds(pl.multiple_of(at * 2 * rows, 2 * rows), 2 * rows)
            block = N1B[layer, pl.ds(at * 2, 2)].reshape(2 * rows, width)
            bias = jnp.concatenate([vec_at(layer, 10 + 2 * k, half), vec_at(layer, 11 + 2 * k, half)], axis=1)
            pre = nn(block, WI[layer]) + bias
            phi = 0.5 * (1.0 + lax.erf(pre * (0.5**0.5)))
            low = (pre * phi).astype(BF16)
            G[layer, where] = low
            density = jnp.exp(pre * pre * -0.5) * ((0.5 / jnp.pi) ** 0.5)
            GP[layer, where] = (phi + pre * density).astype(GP.dtype)
            PF[pl.ds(at * 2, 2)] = nn(low, WU[layer]).reshape(2, rows, width)

        copies = sum_copies(1, 0)
        gather_near(moves)
        fetch_wait(layer, (8, 9, 10, 11))
        feed(y)
        sum_local(copies, PF, 1, 0)

        @pl.when(layer == 0)
        def _():
            fetch_pass(1, (0, 1, 2, 3))

        gather_remote(moves)
        feed(1 - y)
        sum_remote(copies, PF, 1, 0)
        gather_finish(moves)
        following = jnp.minimum(layer + 1, LAYERS - 1)
        for ch in range(PIECES):
            second = N1[piece(ch)] + sum_finish(copies, PF, 1, 0, ch) + full_vec(layer, 5)
            result, xhat, rstd = norm_forward(second, full_vec(layer, 8), full_vec(layer, 9))
            low = result.astype(BF16)
            TK[piece(ch)] = low

            @pl.when(layer + 1 < LAYERS)
            def _():
                XB[following, own + t, piece(ch)] = low
                input_start(following, ch)

            XH2[layer, piece(ch)] = xhat
            SD2[layer, piece(ch)] = jnp.broadcast_to(rstd, (tall, 128))
            H[piece(ch)] = result
        return carry

    lax.fori_loop(0, LAYERS, forward_layer, 0)

    spread_wait(cot_ref, CO, 1)

    total_units = 12 * LAYERS

    def x_copy(unit):
        return rc(GS.at[lax.rem(unit, 12)], XR.at[unit], xs_s.at[lax.rem(unit, 12)], xs_r.at[unit], c, t, 1 - s)

    def z1_copy(unit):
        return rc(GO.at[unit], YR.at[unit], z1_s.at[lax.rem(unit, RING)], z1_r.at[lax.rem(unit, RING)], z_in, t)

    def z2_copy(unit):
        return rc(GO.at[unit], Y2.at[unit], z2_s.at[lax.rem(unit, RING)], z2_r.at[lax.rem(unit, RING)], z_mid, t)

    def z3_copy(unit):
        return rc(GO.at[unit], YR.at[unit], z3_s.at[lax.rem(unit, RING)], z3_r.at[lax.rem(unit, RING)], z_out, t)

    def add_into(unit, other):
        GO[unit] = (GO[unit].astype(F32) + other.astype(F32)).astype(BF16)

    def stage_z1(unit):
        x_copy(unit).wait()
        add_into(unit, XR[unit])

        @pl.when(is_outer)
        def _():
            z1_copy(unit).start()

    def stage_z2(unit):
        @pl.when(is_inner)
        def _():
            z1_copy(unit).wait_recv()
            add_into(unit, YR[unit])
            z2_copy(unit).start()

        @pl.when(is_outer)
        def _():
            z1_copy(unit).wait_send()

    def stage_z3(unit):
        @pl.when(is_inner)
        def _():
            z2_copy(unit).wait()
            add_into(unit, Y2[unit])
            z3_copy(unit).start()

    def out_copy(src, unit):
        return pltpu.make_async_copy(src.at[unit], out_mat.at[unit], om_sem.at[lax.rem(unit, RING)])

    def stage_out(unit):
        @pl.when(unit >= RING)
        def _():
            out_copy(GO, unit - RING).wait()

        @pl.when(is_inner)
        def _():
            z3_copy(unit).wait_send()
            out_copy(GO, unit).start()

        @pl.when(is_outer)
        def _():
            z3_copy(unit).wait_recv()
            out_copy(YR, unit).start()

    stages = ((stage_out, LAGS[3]), (stage_z3, LAGS[2]), (stage_z2, LAGS[1]), (stage_z1, LAGS[0]))

    def advance(tick):
        for stage, lag in stages:
            unit = tick - lag

            @pl.when(jnp.logical_and(unit >= 0, unit < total_units))
            def _(stage=stage, unit=unit):
                stage(unit)

    def vec_step(at):
        partner = (
            (s, c, tc),
            (s, c, ty),
            (1 - s, c, t),
            (s, zp, t),
            (s, lax.rem(c + 2, 4), t),
            (s, c, tc),
            (s, c, ty),
        )[at]
        if at < 2:
            src, dst = OV, VR.at[at]
        elif at < 5:
            src, dst = OW.at[:, vec_rows(t)], VQ.at[at - 2]
        elif at == 5:
            src = dst = OW.at[:, vec_rows(t)]
        else:
            src = dst = OW.at[:, pl.ds(pl.multiple_of(y * (VEC_ROWS // 2), VEC_ROWS // 2), VEC_ROWS // 2)]
        return pltpu.make_async_remote_copy(
            src_ref=src,
            dst_ref=dst,
            send_sem=v_s.at[at],
            recv_sem=v_r.at[at],
            device_id=partner,
            device_id_type=MESH,
        )

    def vec_rows(place):
        count = VEC_ROWS // 4
        return pl.ds(pl.multiple_of(place * count, count), count)

    def vec_move(at):
        if fused:
            if at > 0:
                vec_step(at - 1).wait()
                if at == 1:
                    OV[...] += VR[0]
                elif at == 2:
                    OW[:, vec_rows(t)] = OV[:, vec_rows(t)] + VR[1, :, vec_rows(t)]
                elif at <= 5:
                    OW[:, vec_rows(t)] += VQ[at - 3]
            if at < 7:
                vec_step(at).start()

    def side_of(own_side):
        if fused:
            return pl.multiple_of((s if own_side else 1 - s) * half, half)
        return 0 if own_side else half

    def put_units(own_side, base, step, count, value):
        value = value.astype(BF16).reshape(count, cols, half)
        if own_side:
            GO[pl.ds(base + step, count)] = value
        elif fused:
            GS[pl.ds(step, count)] = value
        else:
            XR[pl.ds(base + step, count)] = value

    def send_units(base, step, count):
        if fused:
            for i in range(step, step + count):
                x_copy(base + i).start()

    def split_grad(a, b_ref_at, base, step, count):
        for own_side in (False, True):
            put_units(own_side, base, step, count, tn(a, b_ref_at(side_of(own_side))))
            if not own_side:
                send_units(base, step, count)

    def across(layer, ch):
        where = pl.ds(ch * tall, tall)
        return rc(ZS.at[where], ZR.at[layer, where], rz_s.at[layer, ch], rz_r.at[layer, ch], zp, t)

    def layer_grad(layer, ch):
        near = sum_finish(sum_copies(4, 0), PF.at[pl.ds(own, 4)], 4, 0, ch)
        across(layer, ch).wait()
        return DR1[piece(ch)] + near + ZR[layer, piece(ch)].astype(F32)

    def backward_layer(turn, carry):
        layer = LAYERS - 1 - turn
        base = turn * 12

        def tick(*places):
            if fused:
                for i in places:
                    advance(base + i)

        moves = gather_copies(DF)
        above = jnp.minimum(layer + 1, LAYERS - 1)
        for ch in range(PIECES):

            @pl.when(turn == 0)
            def _():
                H[piece(ch)] = CO[piece(ch)].astype(F32)

            @pl.when(turn > 0)
            def _():
                H[piece(ch)] = layer_grad(above, ch)

            rstd = SD2[layer, piece(ch)][:, :1]
            d_second = norm_backward(H[piece(ch)], XH2[layer, piece(ch)], rstd, full_vec(layer, 8))
            DF[t, piece(ch)] = d_second.astype(BF16)
            gather_start(moves, ch)
            DR[piece(ch)] = d_second

        @pl.when(turn == 0)
        def _():
            collect_start(TK, OT, 2)

        put_vec(layer, 4, jnp.sum(H[...] * XH2[layer], axis=0, keepdims=True))
        put_vec(layer, 5, jnp.sum(H[...], axis=0, keepdims=True))
        copies = sum_copies(2, 0)

        def back_feed(at):
            where = pl.ds(pl.multiple_of(at * 2 * rows, 2 * rows), 2 * rows)
            block = DF[pl.ds(at * 2, 2)].reshape(2 * rows, width)
            d_act = nt(block, WU[layer])
            low = (d_act * GP[layer, where].astype(F32)).astype(BF16)
            DU[where] = low
            PF[pl.ds(at * 2, 2)] = nt(low, WI[layer]).reshape(2, rows, width)

        gather_near(moves)
        back_feed(y)
        sum_local(copies, PF, 2, 0)
        tick(0, 1)
        gather_remote(moves)
        back_feed(1 - y)
        sum_remote(copies, PF, 2, 0)
        gather_finish(moves)

        def halves(ref):
            return lambda at: ref[:, :, pl.ds(at, half)].reshape(-1, half)

        split_grad(G[layer], halves(DF), base, 0, 4)
        tick(2)
        for own_side in (False, True):
            left = N1B[layer, :, :, pl.ds(side_of(own_side), half)].reshape(own_rows, half)
            for at in range(2):
                put_units(own_side, base, 4 + 2 * at, 2, tn(left, DU[:, at * half : (at + 1) * half]))
            if not own_side:
                send_units(base, 4, 4)
        tick(3)
        only = jnp.where(t == 0, 1.0, 0.0)
        put_vec(layer, 0, only * jnp.sum(DF[...].reshape(own_rows, width).astype(F32), axis=0, keepdims=True))
        put_vec(layer, 14 + t, jnp.sum(DU[...].astype(F32), axis=0, keepdims=True))

        moves = gather_copies(DA)
        for ch in range(PIECES):
            d_normed = DR[piece(ch)] + sum_finish(copies, PF, 2, 0, ch)
            rstd = SD1[layer, piece(ch)][:, :1]
            d_first = norm_backward(d_normed, XH1[layer, piece(ch)], rstd, full_vec(layer, 6))
            DA[t, piece(ch)] = d_first.astype(BF16)
            gather_start(moves, ch)
            DR1[piece(ch)] = d_first
            DR[piece(ch)] = d_normed
        put_vec(layer, 2, jnp.sum(DR[...] * XH1[layer], axis=0, keepdims=True))
        put_vec(layer, 3, jnp.sum(DR[...], axis=0, keepdims=True))

        def back_out(at):
            where = pl.ds(pl.multiple_of(at * 2 * rows, 2 * rows), 2 * rows)
            block = DA[pl.ds(at * 2, 2)].reshape(2 * rows, width)
            DOB[where] = nt(block, WO[layer]).astype(BF16)

        gather_near(moves)
        back_out(y)
        tick(4, 5)
        gather_remote(moves)
        back_out(1 - y)
        gather_finish(moves)
        split_grad(OB[layer], halves(DA), base, 8, 1)
        put_vec(layer, 1, only * jnp.sum(DA[...].reshape(own_rows, width).astype(F32), axis=0, keepdims=True))

        DKF[...] = jnp.zeros_like(DKF)
        DVF[...] = jnp.zeros_like(DVF)

        def back_attend(at, inner):
            where = pl.ds(pl.multiple_of(at * tile, tile), tile)
            grad_tile = DOB[where]
            q_tile = Q[layer, where]
            product = grad_tile.astype(F32) * OB[layer, where].astype(F32)
            d_query = []
            for head in range(3):
                lanes = slice(2 * HD, 3 * HD) if head == 2 else slice(0, 2 * HD)
                d_mix = head_cols(grad_tile, head)
                d_prob = nt(d_mix, head_full(V[layer], head))
                total = jnp.sum(head_cols(product, head), axis=-1, keepdims=True)
                low = PB[layer, head, where]
                d_score = (low.astype(F32) * (d_prob - total)).astype(BF16)
                d_query.append(nn(d_score, head_full(K[layer], head)))
                DKF[:, lanes] += tn(d_score, head_cols(q_tile, head))
                DVF[:, lanes] += tn(low, d_mix)
            scale = HD**-0.5
            DQ[where, : 2 * HD] = (jnp.where(lane_low, d_query[0], d_query[1]) * scale).astype(BF16)
            DQ[where, 2 * HD :] = (d_query[2] * scale).astype(BF16)
            return inner

        tick(6)
        lax.fori_loop(0, 2, back_attend, 0)
        tick(7)
        DK[...] = DKF[...].astype(BF16)
        DV[...] = DVF[...].astype(BF16)

        def back_in(at, with_q):
            where = pl.ds(pl.multiple_of(at * rows, 2 * rows), 2 * rows)
            total = nn(DK[where], WQ[layer, cols : 2 * cols]) + nn(DV[where], WQ[layer, 2 * cols :])
            if with_q:
                mine = pl.ds(pl.multiple_of((at - own) * rows, 2 * rows), 2 * rows)
                total = total + nn(DQ[mine], WQ[layer, :cols])
            PF[pl.ds(at, 2)] = total.reshape(2, rows, width)

        pf_far = PF.at[pl.ds(far, 4)]
        pf_own = PF.at[pl.ds(own, 4)]
        far_copies = sum_copies(3, 1)
        back_in(far + 2 * (1 - y), False)
        sum_remote(far_copies, pf_far, 3, 1)
        back_in(far + 2 * y, False)
        sum_local(far_copies, pf_far, 3, 1)
        copies = sum_copies(4, 0)
        back_in(own + 2 * (1 - y), True)
        sum_remote(copies, pf_own, 4, 0)
        back_in(own + 2 * y, True)
        sum_local(copies, pf_own, 4, 0)
        for ch in range(PIECES):
            ZS[piece(ch)] = sum_finish(far_copies, pf_far, 3, 1, ch).astype(BF16)
            across(layer, ch).start()
        tick(8, 9)

        def block_cols(ref, start, count):
            return lambda at: ref[pl.ds(start, count), :, pl.ds(at, half)].reshape(-1, half)

        xb = XB.at[layer]
        split_grad(DQ[...], block_cols(xb, own, 4), base, 9, 1)
        split_grad(DK[...], block_cols(xb, 0, 8), base, 10, 1)
        split_grad(DV[...], block_cols(xb, 0, 8), base, 11, 1)
        tick(10)
        put_vec(layer, 6 + t, jnp.sum(DQ[...].astype(F32), axis=0, keepdims=True))
        put_vec(layer, 10 + t, jnp.sum(DV[...].astype(F32), axis=0, keepdims=True))

        tick(11)
        return carry

    lax.fori_loop(0, LAYERS, backward_layer, 0)
    for ch in range(PIECES):
        CO[piece(ch)] = layer_grad(0, ch).astype(BF16)
    collect_start(CO, OG, 3)
    vec_move(0)
    if fused:
        more = LAGS[3]
        for i in range(more):
            if i in VEC_TICKS:
                vec_move(1 + VEC_TICKS.index(i))
            advance(total_units + i)
        vec_move(7)

        def drain(i, carry):
            out_copy(GO, i).wait()
            return carry

        lax.fori_loop(total_units - RING, total_units, drain, 0)
        for layer in range(LAYERS):
            fetch_drain(layer)
    else:
        own_out = pltpu.make_async_copy(GO, out_mat.at[0], om_sem.at[0])
        far_out = pltpu.make_async_copy(XR, out_mat.at[1], om_sem.at[1])
        own_out.start()
        far_out.start()
        own_out.wait()
        far_out.wait()
    out_vec[...] = (OW if fused else OV)[...]
    collect_wait(TK, OT, 2)
    out_tok[...] = OT[...]
    collect_wait(CO, OG, 3)
    out_grad[...] = OG[...]


def finish_kernel(dims, *refs):
    tok_ref, grad_ref, mat_ref, vec_ref = refs[:4]
    out_tok, out_grad, out_q, out_k, out_v, out_o, out_i, out_u = refs[4:12]
    vec_q, vec_v, vec_o, vec_i, vec_u, gain_1, shift_1, gain_2, shift_2 = refs[12:]
    width, cols, units, half = dims
    layer = pl.program_id(0)
    s = lax.axis_index("shard")

    @pl.when(layer == 0)
    def _():
        out_tok[...] = tok_ref[...]
        out_grad[...] = grad_ref[...].astype(F32)

    for i in range(4):
        out_u[0, i * cols : (i + 1) * cols, :] = mat_ref[i].astype(F32)
        r, cc = i % 2, i // 2
        out_i[0, r * cols : (r + 1) * cols, cc * half : (cc + 1) * half] = mat_ref[4 + i].astype(F32)
    out_o[0] = mat_ref[8].astype(F32)
    out_q[0] = mat_ref[9].astype(F32)
    out_k[0] = mat_ref[10].astype(F32)
    out_v[0] = mat_ref[11].astype(F32)
    line = pl.ds(layer, 1)
    at = pl.ds(pl.multiple_of(s * half, half), half)
    for row, ref in ((0, vec_u), (1, vec_o), (2, gain_1), (3, shift_1), (4, gain_2), (5, shift_2)):
        ref[line, :] = vec_ref[0, row : row + 1, at]
    for row, ref in ((6, vec_q), (10, vec_v)):
        first = vec_ref[0, pl.ds(row + 2 * s, 1), :cols]
        second = vec_ref[0, pl.ds(row + 1 + 2 * s, 1), :cols]
        ref[line, :] = jnp.concatenate([first, second], axis=1)
    vec_i[line, :width] = vec_ref[0, pl.ds(14 + 2 * s, 1)]
    vec_i[line, width:] = vec_ref[0, pl.ds(15 + 2 * s, 1)]


def per_device(
    tokens,
    cotangent,
    segment_ids,
    lengths,
    query_weight,
    key_weight,
    value_weight,
    output_weight,
    inner_weight,
    outer_weight,
    query_bias,
    value_bias,
    output_bias,
    inner_bias,
    outer_bias,
    first_gain,
    first_shift,
    second_gain,
    second_shift,
):
    shards = lax.axis_size("shard")
    assert lax.axis_size("ctx") == 4 and lax.axis_size("tp") == 4 and tokens.shape[0] == 2
    fused = shards == 2
    seqs, part, width = tokens.shape
    cols = query_weight.shape[2]
    units = inner_weight.shape[2]
    half = width // 2
    rows = 2 * part
    own_rows, all_rows = 4 * rows, 8 * rows
    assert cols == 3 * HD and segment_ids.shape[1] == all_rows and units == width == 4 * cols

    def turned(mat):
        return jnp.swapaxes(mat, 1, 2)

    mats = (
        turned(query_weight),
        turned(key_weight),
        turned(value_weight),
        output_weight,
        inner_weight,
        outer_weight,
    )
    vecs = (query_bias, value_bias, output_bias, outer_bias, inner_bias, first_gain, first_shift, second_gain, second_shift)
    if not fused:
        mats = tuple(
            lax.all_gather(mat, "shard", axis=axis, tiled=True) for mat, axis in zip(mats, (2, 2, 2, 2, 1, 2))
        )
        vecs = tuple(lax.all_gather(vec, "shard", axis=1, tiled=True) for vec in vecs)

    n_units = 12 * LAYERS
    out_shape = [
        jax.ShapeDtypeStruct((2, part, width), BF16),
        jax.ShapeDtypeStruct((2, part, width), BF16),
        jax.ShapeDtypeStruct((n_units, cols, half) if fused else (2, n_units, cols, half), BF16),
        jax.ShapeDtypeStruct((LAYERS, VEC_ROWS, width), F32),
    ]
    vm = pltpu.VMEM
    dma = pltpu.SemaphoreType.DMA
    scratch = [
        vm((LAYERS, 3 * cols, width), BF16),
        vm((LAYERS, cols, width), BF16),
        vm((LAYERS, width, units), BF16),
        vm((LAYERS, units, width), BF16),
        vm((2, LAYERS, 16, half), F32),
        vm((own_rows, 128), F32),
        vm((8, all_rows), F32),
        vm((rows, width), F32),
        vm((rows, width), F32),
        vm((rows, width), F32),
        vm((rows, width), F32),
        vm((rows, width), BF16),
        vm((rows, width), BF16),
        vm((2, part, width), BF16),
        vm((2, part, width), BF16),
        vm((LAYERS, rows, width), F32),
        vm((LAYERS, rows, width), F32),
        vm((LAYERS, rows, 128), F32),
        vm((LAYERS, rows, 128), F32),
        vm((LAYERS, 8, rows, width), BF16),
        vm((LAYERS, own_rows, cols), BF16),
        vm((LAYERS, all_rows, cols), BF16),
        vm((LAYERS, all_rows, cols), BF16),
        vm((LAYERS, own_rows, cols), BF16),
        vm((LAYERS, 4, rows, width), BF16),
        vm((LAYERS, own_rows, units), BF16),
        vm((LAYERS, own_rows, units), BF16),
        vm((LAYERS, 3, own_rows, all_rows), BF16),
        vm((4, rows, width), BF16),
        vm((4, rows, width), BF16),
        vm((own_rows, units), BF16),
        vm((own_rows, cols), BF16),
        vm((own_rows, cols), BF16),
        vm((all_rows, cols), BF16),
        vm((all_rows, cols), BF16),
        vm((all_rows, cols), F32),
        vm((all_rows, cols), F32),
        vm((8, rows, width), F32),
        vm((2, 3, rows, width), BF16),
        vm((5, 3, rows, width), BF16),
        vm((rows, width), BF16),
        vm((LAYERS, rows, width), BF16),
        vm((n_units, cols, half), BF16),
        vm((12, cols, half), BF16),
        vm((n_units, cols, half), BF16),
        vm((n_units, cols, half), BF16),
        vm((n_units, cols, half), BF16),
        vm((LAYERS, VEC_ROWS, width), F32),
        vm((2, LAYERS, VEC_ROWS, width), F32),
        vm((3, LAYERS, VEC_ROWS // 4, width), F32),
        vm((LAYERS, VEC_ROWS, width), F32),
        dma((LAYERS, 6)),
        dma((LAYERS, 9)),
        dma((LAYERS, 9)),
        dma((LAYERS, 6)),
        dma((LAYERS, 6)),
        dma((7,)),
        dma((7,)),
        dma((4, 2)),
        dma((4, 2)),
        dma((LAYERS, 7 * PIECES)),
        dma((LAYERS, 7 * PIECES)),
        dma((3 * PIECES,)),
        dma((3 * PIECES,)),
        dma((2, 2 * PIECES + 1)),
        dma((2, 2 * PIECES + 1)),
        dma((LAYERS, PIECES)),
        dma((LAYERS, PIECES)),
        dma((12,)),
        dma((n_units,)),
        dma((RING,)),
        dma((RING,)),
        dma((RING,)),
        dma((RING,)),
        dma((RING,)),
        dma((RING,)),
        dma((RING,)),
    ]
    vmem = pl.BlockSpec(memory_space=pltpu.VMEM)
    hbm = pl.BlockSpec(memory_space=pl.ANY)
    layer_out, grad_tokens, grad_mats, grad_vecs = pl.pallas_call(
        functools.partial(step_kernel, (width, cols, units, half), fused),
        out_shape=out_shape,
        in_specs=[vmem] * 12 + [pl.BlockSpec(memory_space=pltpu.SMEM)] + [hbm] * 6,
        out_specs=[vmem, vmem, hbm, vmem],
        scratch_shapes=scratch,
        compiler_params=pltpu.CompilerParams(
            collective_id=0, has_side_effects=True, vmem_limit_bytes=67043328
        ),
        name="encoder_step",
    )(tokens, cotangent, segment_ids, *vecs, lengths, *mats)

    if fused:
        dims = (width, cols, units, half)
        layer_block = lambda *shape: pl.BlockSpec((1,) + shape, lambda i: (i,) + (0,) * len(shape))
        whole = lambda *shape: pl.BlockSpec(shape, lambda i: (0,) * len(shape))
        mat_shapes = [(cols, half)] * 4 + [(half, units), (units, half)]
        vec_lens = (half, half, half, 4 * half, half, half, half, half, half)
        outs = pl.pallas_call(
            functools.partial(finish_kernel, dims),
            grid=(LAYERS,),
            out_shape=[
                jax.ShapeDtypeStruct((2, part, width), BF16),
                jax.ShapeDtypeStruct((2, part, width), F32),
            ]
            + [jax.ShapeDtypeStruct((LAYERS,) + shape, F32) for shape in mat_shapes]
            + [jax.ShapeDtypeStruct((LAYERS, count), F32) for count in vec_lens],
            in_specs=[
                whole(2, part, width),
                whole(2, part, width),
                pl.BlockSpec((12, cols, half), lambda i: (LAYERS - 1 - i, 0, 0)),
                layer_block(VEC_ROWS, width),
            ],
            out_specs=[whole(2, part, width), whole(2, part, width)]
            + [layer_block(*shape) for shape in mat_shapes]
            + [whole(LAYERS, count) for count in vec_lens],
            name="write_out",
        )(layer_out, grad_tokens, grad_mats, grad_vecs)
        return tuple(outs[:2]) + tuple(turned(mat) for mat in outs[2:5]) + tuple(outs[5:])

    mats = grad_mats.reshape(2, LAYERS, 12, cols, half)[:, ::-1]
    wide = jnp.concatenate([mats[0], mats[1]], axis=-1)
    wide = jnp.concatenate([wide[:, :4], wide[:, 8:]], axis=1)
    wide = lax.psum(lax.psum_scatter(wide, "shard", scatter_dimension=3, tiled=True), "ctx").astype(F32)
    inner = mats[:, :, 4:8].reshape(2, LAYERS, 2, 2, cols, half)
    inner = jnp.transpose(inner, (1, 0, 3, 4, 2, 5)).reshape(LAYERS, width, units)
    inner = lax.psum(lax.psum_scatter(inner, "shard", scatter_dimension=1, tiled=True), "ctx").astype(F32)
    grad_outer = wide[:, :4].reshape(LAYERS, units, -1)
    grad_output = wide[:, 4]
    grad_query, grad_key, grad_value = (turned(wide[:, 5 + at]) for at in range(3))

    total = lax.psum(grad_vecs, ("shard", "ctx", "tp"))
    at = lax.axis_index("shard")

    def owned(vec):
        count = vec.shape[1] // shards
        return lax.dynamic_slice_in_dim(vec, at * count, count, 1)

    vec_query = owned(total[:, 6:10, :cols].reshape(LAYERS, -1))
    vec_value = owned(total[:, 10:14, :cols].reshape(LAYERS, -1))
    vec_inner = owned(total[:, 14:18].reshape(LAYERS, -1))
    vec_outer, vec_output, gain_one, shift_one, gain_two, shift_two = (owned(total[:, row]) for row in range(6))
    return (
        layer_out,
        grad_tokens.astype(F32),
        grad_query,
        grad_key,
        grad_value,
        grad_output,
        inner,
        grad_outer,
        vec_query,
        vec_value,
        vec_output,
        vec_inner,
        vec_outer,
        gain_one,
        shift_one,
        gain_two,
        shift_two,
    )


def solution(mesh):
    rows = P("shard", ("ctx", "tp"), None)
    down = P(None, "shard", "tp")
    across = P(None, "tp", "shard")
    vector = P(None, "shard")
    mats = (down, down, down, across, down, across)
    return jax.shard_map(
        per_device,
        mesh=mesh,
        in_specs=(rows, rows, P("shard", None), P("shard")) + mats + (vector,) * 9,
        out_specs=(rows, rows) + mats + (vector,) * 9,
        check_vma=False,
    )
```

```python
import functools

import jax
import jax.numpy as jnp
from jax import lax
from jax.experimental import pallas as pl
from jax.experimental.pallas import tpu as pltpu
from jax.sharding import PartitionSpec as P

HD = 64
LAYERS = 2
EPSILON = 1e-05
MESH = pl.DeviceIdType.MESH
F32 = jnp.float32
BF16 = jnp.bfloat16
NEG = -1e30
VEC_ROWS = 32
PIECES = 4
RING = 8
LAGS = (4, 6, 8, 10)
VEC_TICKS = (0, 1, 3, 5, 6, 8)


def nn(a, b):
    return jnp.dot(a, b, preferred_element_type=F32)


def nt(a, b):
    return lax.dot_general(a, b, (((1,), (1,)), ((), ())), preferred_element_type=F32)


def tn(a, b):
    return lax.dot_general(a, b, (((0,), (0,)), ((), ())), preferred_element_type=F32)


def norm_forward(resid, gain, shift):
    center = resid - jnp.mean(resid, axis=-1, keepdims=True)
    spread = jnp.mean(center * center, axis=-1, keepdims=True)
    rstd = lax.rsqrt(spread + EPSILON)
    xhat = center * rstd
    return xhat * gain + shift, xhat, rstd


def norm_backward(grad, xhat, rstd, gain):
    scaled = grad * gain
    first = jnp.mean(scaled, axis=-1, keepdims=True)
    second = jnp.mean(scaled * xhat, axis=-1, keepdims=True)
    return rstd * (scaled - first - xhat * second)


def step_kernel(dims, fused, *refs):
    (
        tok_ref,
        cot_ref,
        seg_ref,
        vec_refs,
        len_ref,
        wq_ref,
        wk_ref,
        wv_ref,
        wo_ref,
        wi_ref,
        wu_ref,
        out_tok,
        out_grad,
        out_mat,
        out_vec,
        WQ,
        WO,
        WI,
        WU,
        VB,
        IDC,
        IDR,
        H,
        N1,
        DR,
        DR1,
        TK,
        CO,
        OT,
        OG,
        XH1,
        XH2,
        SD1,
        SD2,
        XB,
        Q,
        K,
        V,
        OB,
        N1B,
        G,
        GP,
        PB,
        DF,
        DA,
        DU,
        DOB,
        DQ,
        DK,
        DV,
        DKF,
        DVF,
        PF,
        SB,
        RB,
        ZS,
        ZR,
        GO,
        GS,
        XR,
        YR,
        Y2,
        OV,
        VR,
        VQ,
        OW,
        wl_sem,
        ws_sem,
        wr_sem,
        wz_s,
        wz_r,
        v_s,
        v_r,
        rd_s,
        rd_r,
        g8_s,
        g8_r,
        g4_s,
        g4_r,
        rs_s,
        rs_r,
        rz_s,
        rz_r,
        xs_s,
        xs_r,
        z1_s,
        z1_r,
        z2_s,
        z2_r,
        z3_s,
        z3_r,
        om_sem,
    ) = refs[:3] + (refs[3:12],) + refs[12:]
    width, cols, units, half = dims
    seqs, part = tok_ref.shape[0], tok_ref.shape[1]
    rows = 2 * part
    own_rows = 4 * rows
    all_rows = 8 * rows
    tall = rows // PIECES
    s = lax.axis_index("shard")
    c = lax.axis_index("ctx")
    t = lax.axis_index("tp")
    hf = lax.rem(c, 2)
    y = t // 2
    k = lax.rem(t, 2)
    tc = t + 1 - 2 * k
    ty = lax.rem(t + 2, 4)
    zp = c + 1 - 2 * hf
    is_inner = jnp.logical_or(c == 1, c == 2)
    is_outer = jnp.logical_not(is_inner)
    z_in = jnp.where(c == 0, 1, 2)
    z_mid = 3 - c
    z_out = jnp.where(c == 1, 0, 3)

    def rc(src, dst, ssem, rsem, cc, tt, ss=None):
        return pltpu.make_async_remote_copy(
            src_ref=src,
            dst_ref=dst,
            send_sem=ssem,
            recv_sem=rsem,
            device_id=(s if ss is None else ss, cc, tt),
            device_id_type=MESH,
        )

    bar = pltpu.get_barrier_semaphore()
    for dc in range(4):
        for dt in range(4):
            if dc or dt:
                pl.semaphore_signal(
                    bar,
                    1,
                    device_id=(s, lax.rem(c + dc, 4), lax.rem(t + dt, 4)),
                    device_id_type=MESH,
                )
    if fused:
        pl.semaphore_signal(bar, 1, device_id=(1 - s, c, t), device_id_type=MESH)

    def unit_view(layer, item, side):
        at = pl.multiple_of(side * half, half)
        lanes = pl.ds(at, half)
        if item < 3:
            return WQ.at[layer, pl.ds(item * cols, cols), lanes]
        if item == 3:
            return WO.at[layer, :, lanes]
        if item < 8:
            return WI.at[layer, pl.ds(at + (item - 4) * (half // 4), half // 4)]
        return WU.at[layer, pl.ds((item - 8) * cols, cols), lanes]

    def unit_arg(layer, item):
        if item < 4:
            return (wq_ref, wk_ref, wv_ref, wo_ref)[item].at[layer]
        if item < 8:
            return wi_ref.at[layer, pl.ds((item - 4) * (half // 4), half // 4)]
        return wu_ref.at[layer, pl.ds((item - 8) * cols, cols)]

    def local_copy(layer, item):
        lanes = pl.ds(pl.multiple_of(s * half, half), half) if fused else pl.ds(0, width)
        if item < 3:
            src, dst = (wq_ref, wk_ref, wv_ref)[item], WQ.at[layer, pl.ds(item * cols, cols), lanes]
        elif item == 3:
            src, dst = wo_ref, WO.at[layer, :, lanes]
        elif item == 4:
            src, dst = wi_ref, WI.at[layer, lanes]
        else:
            src, dst = wu_ref, WU.at[layer, :, lanes]
        return pltpu.make_async_copy(src.at[layer], dst, wl_sem.at[layer, item])

    def over_x(layer, item):
        return rc(
            unit_arg(layer, item),
            unit_view(layer, item, s),
            ws_sem.at[layer, item if item < 4 else 2 + item // 2],
            wr_sem.at[layer, item if item < 4 else 2 + item // 2],
            c,
            t,
            1 - s,
        )

    def over_z(layer, item):
        view = unit_view(layer, item, 1 - s)
        return rc(view, view, wz_s.at[layer, item // 2], wz_r.at[layer, item // 2], zp, t)

    def direct(layer, item):
        return jnp.logical_and(layer == 0, item < 4)

    def mine_over_x(layer, item):
        return jnp.logical_or(direct(layer, item), hf == item % 2)

    def fetch_start(layer, item):
        @pl.when(mine_over_x(layer, item))
        def _():
            over_x(layer, item).start()

    def fetch_pass(layer, items):
        if fused:
            for item in items:

                @pl.when(hf == item % 2)
                def _():
                    over_x(layer, item).wait_recv()
                    over_z(layer, item).start()

    def fetch_wait(layer, items):
        for item in items:
            local_copy(layer, {0: 0, 1: 1, 2: 2, 3: 3, 4: 4, 8: 5}[item]).wait() if item in (0, 1, 2, 3, 4, 8) else None
            if fused:

                @pl.when(direct(layer, item))
                def _():
                    over_x(layer, item).wait_recv()

                @pl.when(jnp.logical_not(mine_over_x(layer, item)))
                def _():
                    over_z(layer, item).wait_recv()

    def fetch_drain(layer):
        for item in range(12):

            @pl.when(mine_over_x(layer, item))
            def _():
                over_x(layer, item).wait_send()

            @pl.when(jnp.logical_and(hf == item % 2, jnp.logical_not(direct(layer, item))))
            def _():
                over_z(layer, item).wait_send()

    def fill_vectors(side, at):
        for layer in range(LAYERS):
            for place, ref in ((0, vec_refs[0]), (2, vec_refs[1])):
                value = ref[...].astype(F32)[layer : layer + 1, at : at + half]
                VB[side, layer, place : place + 1, :cols] = value[:, :cols]
                VB[side, layer, place + 1 : place + 2, :cols] = value[:, cols:]
            for place, ref in zip((4, 5, 6, 7, 8, 9), vec_refs[2:4] + vec_refs[5:9]):
                VB[side, layer, place : place + 1] = ref[...].astype(F32)[layer : layer + 1, at : at + half]
            value = vec_refs[4][...].astype(F32)[layer : layer + 1, 4 * at : 4 * at + 4 * half]
            for j in range(4):
                VB[side, layer, 10 + j : 11 + j] = value[:, j * half : (j + 1) * half]

    for layer in range(LAYERS):
        for item in range(6):
            local_copy(layer, item).start()
    if fused:
        fill_vectors(s, 0)
    else:
        fill_vectors(0, 0)
        fill_vectors(1, half)
    b_me = c // 2
    ids = seg_ref[pl.ds(b_me, 1)]
    places = lax.broadcasted_iota(jnp.int32, ids.shape, 1)
    ids = jnp.where(places < len_ref[b_me], ids, -1).astype(F32)
    IDR[...] = jnp.broadcast_to(ids, IDR.shape)
    own_ids = jnp.where(hf == 0, ids[:, :own_rows], ids[:, own_rows:])
    IDC[...] = jnp.broadcast_to(own_ids, (128, own_rows)).T
    OV[...] = jnp.zeros_like(OV)
    pl.semaphore_wait(bar, 16 if fused else 15)

    spread_t = 2 * hf + y

    def spread_copies(src_ref, dst_ref, which):
        return [
            (
                jnp.logical_and(2 * b + c // 2 == c, spread_t == t),
                rc(
                    src_ref.at[b],
                    dst_ref.at[pl.ds(k * part, part)],
                    rd_s.at[which, b],
                    rd_r.at[which, k],
                    2 * b + c // 2,
                    spread_t,
                ),
            )
            for b in range(2)
        ]

    def spread_start(src_ref, dst_ref, which):
        for b, (mine, copy) in enumerate(spread_copies(src_ref, dst_ref, which)):

            @pl.when(mine)
            def _():
                dst_ref[pl.ds(pl.multiple_of(k * part, part), part), :] = src_ref[b]

            @pl.when(jnp.logical_not(mine))
            def _():
                copy.start()

    def spread_wait(src_ref, dst_ref, which):
        for mine, copy in spread_copies(src_ref, dst_ref, which):

            @pl.when(jnp.logical_not(mine))
            def _():
                copy.wait_send()

        for kk in range(2):
            mine = jnp.logical_and(2 * hf + y == c, 2 * k + kk == t)

            @pl.when(jnp.logical_not(mine))
            def _():
                rc(
                    src_ref.at[0],
                    dst_ref.at[pl.ds(kk * part, part)],
                    rd_s.at[which, 0],
                    rd_r.at[which, kk],
                    c,
                    t,
                ).wait_recv()

    def collect_copies(src_ref, dst_ref, which):
        return [
            (
                jnp.logical_and(2 * hf + y == c, 2 * k + kk == t),
                rc(
                    src_ref.at[pl.ds(kk * part, part)],
                    dst_ref.at[b_me],
                    rd_s.at[which, kk],
                    rd_r.at[which, b_me],
                    2 * hf + y,
                    2 * k + kk,
                ),
            )
            for kk in range(2)
        ]

    def collect_start(src_ref, dst_ref, which):
        for kk, (mine, copy) in enumerate(collect_copies(src_ref, dst_ref, which)):

            @pl.when(mine)
            def _():
                dst_ref[b_me] = src_ref[kk * part : (kk + 1) * part, :]

            @pl.when(jnp.logical_not(mine))
            def _():
                copy.start()

    def collect_wait(src_ref, dst_ref, which):
        for mine, copy in collect_copies(src_ref, dst_ref, which):

            @pl.when(jnp.logical_not(mine))
            def _():
                copy.wait_send()

        for b in range(2):
            mine = jnp.logical_and(2 * b + c // 2 == c, spread_t == t)

            @pl.when(jnp.logical_not(mine))
            def _():
                rc(
                    src_ref.at[pl.ds(0, part)],
                    dst_ref.at[b],
                    rd_s.at[which, 0],
                    rd_r.at[which, b],
                    c,
                    t,
                ).wait_recv()

    spread_start(tok_ref, TK, 0)
    if fused:
        vec_copy = rc(VB.at[s], VB.at[s], ws_sem.at[0, 8], wr_sem.at[0, 8], c, t, 1 - s)
        vec_copy.start()
        for layer in range(LAYERS):
            for item in range(12):
                fetch_start(layer, item)
    spread_start(cot_ref, CO, 1)

    def piece(ch):
        return slice(ch * tall, (ch + 1) * tall)

    def gather_copies(buf):
        def move(slot, ch, at, tt):
            view = buf.at[slot, pl.ds(ch * tall, tall)]
            return rc(view, view, g4_s.at[3 * ch + at], g4_r.at[3 * ch + at], c, tt)

        return [(move(t, ch, 0, tc), move(t, ch, 1, ty), move(ty, ch, 2, tc)) for ch in range(PIECES)]

    def gather_start(copies, ch):
        copies[ch][1].start()
        copies[ch][0].start()

    def gather_near(copies):
        for to_c, _, _ in copies:
            to_c.wait_recv()

    def gather_remote(copies):
        for _, to_y, y_to_c in copies:
            to_y.wait_recv()
            y_to_c.start()
        for _, _, y_to_c in copies:
            y_to_c.wait_recv()

    def gather_finish(copies):
        for moves in copies:
            for copy in moves:
                copy.wait_send()

    def sum_copies(slot, lane):
        def move(at, ch, tt):
            where = pl.ds(ch * tall, tall)
            sem = PIECES * at + ch
            return rc(SB.at[lane, at, where], RB.at[slot, at, where], rs_s.at[lane, sem], rs_r.at[lane, sem], c, tt)

        pairs = [(move(0, ch, tc), move(1, ch, ty)) for ch in range(PIECES)]
        last = 2 * PIECES
        return pairs, rc(SB.at[lane, 2], RB.at[slot, 2], rs_s.at[lane, last], rs_r.at[lane, last], c, tc)

    def sum_remote(copies, pf, slot, lane):
        for ch, (to_c, _) in enumerate(copies[0]):
            SB[lane, 0, piece(ch)] = pf[(1 - y) * 2 + 1 - k, piece(ch)].astype(BF16)
            to_c.start()
        for ch, (to_c, to_y) in enumerate(copies[0]):
            to_c.wait_recv()
            SB[lane, 1, piece(ch)] = (pf[ty, piece(ch)] + RB[slot, 0, piece(ch)].astype(F32)).astype(BF16)
            to_y.start()

    def sum_local(copies, pf, slot, lane):
        SB[lane, 2] = pf[tc].astype(BF16)
        copies[1].start()

    def sum_finish(copies, pf, slot, lane, ch):
        pairs, near = copies
        if ch == 0:
            near.wait_recv()
        partial = pf[t, piece(ch)] + RB[slot, 2, piece(ch)].astype(F32)
        pairs[ch][1].wait_recv()
        if ch == PIECES - 1:
            for to_c, to_y in pairs:
                to_c.wait_send()
                to_y.wait_send()
            near.wait_send()
        return partial + RB[slot, 1, piece(ch)].astype(F32)

    def full_vec(layer, row):
        return jnp.concatenate([VB[0, layer, row : row + 1], VB[1, layer, row : row + 1]], axis=1)

    def vec_at(layer, row, lanes):
        return VB[y, layer, pl.ds(row, 1)][:, :lanes]

    def put_vec(layer, row, value):
        OV[layer, pl.ds(row, 1), : value.shape[1]] = value

    if fused:
        vec_copy.wait()
    spread_wait(tok_ref, TK, 0)
    own = hf * 4
    far = (1 - hf) * 4

    def input_copies(layer):
        buf = XB.at[layer]

        def move(slot, ch, at, cc, tt):
            view = buf.at[slot, pl.ds(ch * tall, tall)]
            return rc(view, view, g8_s.at[layer, 7 * ch + at], g8_r.at[layer, 7 * ch + at], cc, tt)

        return [
            (
                move(own + t, ch, 0, c, ty),
                move(own + t, ch, 1, zp, t),
                move(own + t, ch, 2, c, tc),
                move(own + ty, ch, 3, c, tc),
                move(far + t, ch, 4, c, ty),
                move(far + t, ch, 5, c, tc),
                move(far + ty, ch, 6, c, tc),
            )
            for ch in range(PIECES)
        ]

    def input_start(layer, ch):
        for copy in input_copies(layer)[ch][:3]:
            copy.start()

    H[...] = TK[...].astype(F32)
    XB[0, own + t] = TK[...]
    for ch in range(PIECES):
        input_start(0, ch)
    lane_low = lax.broadcasted_iota(jnp.int32, (1, 2 * HD), 1) < HD

    def head_cols(value, head):
        if head == 2:
            return value[:, 2 * HD : 3 * HD]
        keep = lane_low if head == 0 else jnp.logical_not(lane_low)
        return jnp.where(keep, value[:, : 2 * HD], jnp.zeros_like(value[:, : 2 * HD]))

    def head_full(value, head):
        return value[:, 2 * HD : 3 * HD] if head == 2 else value[:, : 2 * HD]

    tile = own_rows // 2

    def forward_layer(layer, carry):
        arrivals = input_copies(layer)
        fetch_wait(layer, (0, 1, 2))

        def project(at, with_q):
            block = XB[layer, pl.ds(at, 2)].reshape(2 * rows, width)
            where = pl.ds(pl.multiple_of(at * rows, 2 * rows), 2 * rows)
            if with_q:
                mine = pl.ds(pl.multiple_of((at - own) * rows, 2 * rows), 2 * rows)
                qb = vec_at(layer, k, cols)
                q_low = (nt(block, WQ[layer, :cols]) + qb).astype(BF16)
                Q[layer, mine] = q_low * jnp.asarray(HD**-0.5, BF16)
            K[layer, where] = nt(block, WQ[layer, cols : 2 * cols]).astype(BF16)
            V[layer, where] = (nt(block, WQ[layer, 2 * cols :]) + vec_at(layer, 2 + k, cols)).astype(BF16)

        for moves in arrivals:
            moves[2].wait_recv()
        project(own + 2 * y, True)
        for moves in arrivals:
            moves[1].wait_recv()
            moves[4].start()
            moves[5].start()
            moves[0].wait_recv()
            moves[3].start()
        for moves in arrivals:
            moves[3].wait_recv()
        project(own + 2 * (1 - y), True)
        for moves in arrivals:
            moves[5].wait_recv()
        project(far + 2 * y, False)
        for moves in arrivals:
            moves[4].wait_recv()
            moves[6].start()
        for moves in arrivals:
            moves[6].wait_recv()
        project(far + 2 * (1 - y), False)
        for moves in arrivals:
            for copy in moves:
                copy.wait_send()
        fetch_pass(layer, (4, 5))

        def attend(at, inner):
            where = pl.ds(pl.multiple_of(at * tile, tile), tile)
            ids = IDC[where][:, :1] == IDR[:1]
            q_tile = Q[layer, where]
            mixed = []
            for head in range(3):
                scores = nt(head_cols(q_tile, head), head_full(K[layer], head))
                scores = jnp.where(ids, scores, NEG)
                top = jnp.max(scores, axis=-1, keepdims=True)
                expo = jnp.exp(scores - top)
                low = (expo / jnp.sum(expo, axis=-1, keepdims=True)).astype(BF16)
                PB[layer, head, where] = low
                mixed.append(nn(low, head_full(V[layer], head)))
            OB[layer, where, : 2 * HD] = jnp.where(lane_low, mixed[0], mixed[1]).astype(BF16)
            OB[layer, where, 2 * HD :] = mixed[2].astype(BF16)
            return inner

        lax.fori_loop(0, 2, attend, 0)
        fetch_wait(layer, (3,))
        fetch_pass(layer, (6, 7))

        def project_out(at):
            where = pl.ds(pl.multiple_of(at * 2 * rows, 2 * rows), 2 * rows)
            PF[pl.ds(at * 2, 2)] = nn(OB[layer, where], WO[layer]).reshape(2, rows, width)

        copies = sum_copies(0, 0)
        project_out(1 - y)
        sum_remote(copies, PF, 0, 0)
        project_out(y)
        sum_local(copies, PF, 0, 0)
        fetch_pass(layer, (8, 9))
        moves = gather_copies(N1B.at[layer])
        for ch in range(PIECES):
            branch = sum_finish(copies, PF, 0, 0, ch) + full_vec(layer, 4)
            resid = H[piece(ch)] + branch
            normed, xhat, rstd = norm_forward(resid, full_vec(layer, 6), full_vec(layer, 7))
            N1B[layer, t, piece(ch)] = normed.astype(BF16)
            gather_start(moves, ch)
            N1[piece(ch)] = normed
            XH1[layer, piece(ch)] = xhat
            SD1[layer, piece(ch)] = jnp.broadcast_to(rstd, (tall, 128))
        fetch_pass(layer, (10, 11))
        fetch_wait(layer, (4, 5, 6, 7))

        def feed(at):
            where = pl.ds(pl.multiple_of(at * 2 * rows, 2 * rows), 2 * rows)
            block = N1B[layer, pl.ds(at * 2, 2)].reshape(2 * rows, width)
            bias = jnp.concatenate([vec_at(layer, 10 + 2 * k, half), vec_at(layer, 11 + 2 * k, half)], axis=1)
            pre = nn(block, WI[layer]) + bias
            phi = 0.5 * (1.0 + lax.erf(pre * (0.5**0.5)))
            low = (pre * phi).astype(BF16)
            G[layer, where] = low
            density = jnp.exp(pre * pre * -0.5) * ((0.5 / jnp.pi) ** 0.5)
            GP[layer, where] = (phi + pre * density).astype(GP.dtype)
            PF[pl.ds(at * 2, 2)] = nn(low, WU[layer]).reshape(2, rows, width)

        copies = sum_copies(1, 0)
        gather_near(moves)
        fetch_wait(layer, (8, 9, 10, 11))
        feed(y)
        sum_local(copies, PF, 1, 0)

        @pl.when(layer == 0)
        def _():
            fetch_pass(1, (0, 1, 2, 3))

        gather_remote(moves)
        feed(1 - y)
        sum_remote(copies, PF, 1, 0)
        gather_finish(moves)
        following = jnp.minimum(layer + 1, LAYERS - 1)
        for ch in range(PIECES):
            second = N1[piece(ch)] + sum_finish(copies, PF, 1, 0, ch) + full_vec(layer, 5)
            result, xhat, rstd = norm_forward(second, full_vec(layer, 8), full_vec(layer, 9))
            low = result.astype(BF16)
            TK[piece(ch)] = low

            @pl.when(layer + 1 < LAYERS)
            def _():
                XB[following, own + t, piece(ch)] = low
                input_start(following, ch)

            XH2[layer, piece(ch)] = xhat
            SD2[layer, piece(ch)] = jnp.broadcast_to(rstd, (tall, 128))
            H[piece(ch)] = result
        return carry

    lax.fori_loop(0, LAYERS, forward_layer, 0)

    spread_wait(cot_ref, CO, 1)

    total_units = 12 * LAYERS

    def x_copy(unit):
        return rc(GS.at[lax.rem(unit, 12)], XR.at[unit], xs_s.at[lax.rem(unit, 12)], xs_r.at[unit], c, t, 1 - s)

    def z1_copy(unit):
        return rc(GO.at[unit], YR.at[unit], z1_s.at[lax.rem(unit, RING)], z1_r.at[lax.rem(unit, RING)], z_in, t)

    def z2_copy(unit):
        return rc(GO.at[unit], Y2.at[unit], z2_s.at[lax.rem(unit, RING)], z2_r.at[lax.rem(unit, RING)], z_mid, t)

    def z3_copy(unit):
        return rc(GO.at[unit], YR.at[unit], z3_s.at[lax.rem(unit, RING)], z3_r.at[lax.rem(unit, RING)], z_out, t)

    def add_into(unit, other):
        GO[unit] = (GO[unit].astype(F32) + other.astype(F32)).astype(BF16)

    def stage_z1(unit):
        x_copy(unit).wait()
        add_into(unit, XR[unit])

        @pl.when(is_outer)
        def _():
            z1_copy(unit).start()

    def stage_z2(unit):
        @pl.when(is_inner)
        def _():
            z1_copy(unit).wait_recv()
            add_into(unit, YR[unit])
            z2_copy(unit).start()

        @pl.when(is_outer)
        def _():
            z1_copy(unit).wait_send()

    def stage_z3(unit):
        @pl.when(is_inner)
        def _():
            z2_copy(unit).wait()
            add_into(unit, Y2[unit])
            z3_copy(unit).start()

    def out_copy(src, unit):
        return pltpu.make_async_copy(src.at[unit], out_mat.at[unit], om_sem.at[lax.rem(unit, RING)])

    def stage_out(unit):
        @pl.when(unit >= RING)
        def _():
            out_copy(GO, unit - RING).wait()

        @pl.when(is_inner)
        def _():
            z3_copy(unit).wait_send()
            out_copy(GO, unit).start()

        @pl.when(is_outer)
        def _():
            z3_copy(unit).wait_recv()
            out_copy(YR, unit).start()

    stages = ((stage_out, LAGS[3]), (stage_z3, LAGS[2]), (stage_z2, LAGS[1]), (stage_z1, LAGS[0]))

    def advance(tick):
        for stage, lag in stages:
            unit = tick - lag

            @pl.when(jnp.logical_and(unit >= 0, unit < total_units))
            def _(stage=stage, unit=unit):
                stage(unit)

    def vec_step(at):
        partner = (
            (s, c, tc),
            (s, c, ty),
            (1 - s, c, t),
            (s, zp, t),
            (s, lax.rem(c + 2, 4), t),
            (s, c, tc),
            (s, c, ty),
        )[at]
        if at < 2:
            src, dst = OV, VR.at[at]
        elif at < 5:
            src, dst = OW.at[:, vec_rows(t)], VQ.at[at - 2]
        elif at == 5:
            src = dst = OW.at[:, vec_rows(t)]
        else:
            src = dst = OW.at[:, pl.ds(pl.multiple_of(y * (VEC_ROWS // 2), VEC_ROWS // 2), VEC_ROWS // 2)]
        return pltpu.make_async_remote_copy(
            src_ref=src,
            dst_ref=dst,
            send_sem=v_s.at[at],
            recv_sem=v_r.at[at],
            device_id=partner,
            device_id_type=MESH,
        )

    def vec_rows(place):
        count = VEC_ROWS // 4
        return pl.ds(pl.multiple_of(place * count, count), count)

    def vec_move(at):
        if fused:
            if at > 0:
                vec_step(at - 1).wait()
                if at == 1:
                    OV[...] += VR[0]
                elif at == 2:
                    OW[:, vec_rows(t)] = OV[:, vec_rows(t)] + VR[1, :, vec_rows(t)]
                elif at <= 5:
                    OW[:, vec_rows(t)] += VQ[at - 3]
            if at < 7:
                vec_step(at).start()

    def side_of(own_side):
        if fused:
            return pl.multiple_of((s if own_side else 1 - s) * half, half)
        return 0 if own_side else half

    def put_units(own_side, base, step, count, value):
        value = value.astype(BF16).reshape(count, cols, half)
        if own_side:
            GO[pl.ds(base + step, count)] = value
        elif fused:
            GS[pl.ds(step, count)] = value
        else:
            XR[pl.ds(base + step, count)] = value

    def send_units(base, step, count):
        if fused:
            for i in range(step, step + count):
                x_copy(base + i).start()

    def split_grad(a, b_ref_at, base, step, count):
        for own_side in (False, True):
            put_units(own_side, base, step, count, tn(a, b_ref_at(side_of(own_side))))
            if not own_side:
                send_units(base, step, count)

    def across(layer, ch):
        where = pl.ds(ch * tall, tall)
        return rc(ZS.at[where], ZR.at[layer, where], rz_s.at[layer, ch], rz_r.at[layer, ch], zp, t)

    def layer_grad(layer, ch):
        near = sum_finish(sum_copies(4, 0), PF.at[pl.ds(own, 4)], 4, 0, ch)
        across(layer, ch).wait()
        return DR1[piece(ch)] + near + ZR[layer, piece(ch)].astype(F32)

    def backward_layer(turn, carry):
        layer = LAYERS - 1 - turn
        base = turn * 12

        def tick(*places):
            if fused:
                for i in places:
                    advance(base + i)

        moves = gather_copies(DF)
        above = jnp.minimum(layer + 1, LAYERS - 1)
        for ch in range(PIECES):

            @pl.when(turn == 0)
            def _():
                H[piece(ch)] = CO[piece(ch)].astype(F32)

            @pl.when(turn > 0)
            def _():
                H[piece(ch)] = layer_grad(above, ch)

            rstd = SD2[layer, piece(ch)][:, :1]
            d_second = norm_backward(H[piece(ch)], XH2[layer, piece(ch)], rstd, full_vec(layer, 8))
            DF[t, piece(ch)] = d_second.astype(BF16)
            gather_start(moves, ch)
            DR[piece(ch)] = d_second

        @pl.when(turn == 0)
        def _():
            collect_start(TK, OT, 2)

        put_vec(layer, 4, jnp.sum(H[...] * XH2[layer], axis=0, keepdims=True))
        put_vec(layer, 5, jnp.sum(H[...], axis=0, keepdims=True))
        copies = sum_copies(2, 0)

        def back_feed(at):
            where = pl.ds(pl.multiple_of(at * 2 * rows, 2 * rows), 2 * rows)
            block = DF[pl.ds(at * 2, 2)].reshape(2 * rows, width)
            d_act = nt(block, WU[layer])
            low = (d_act * GP[layer, where].astype(F32)).astype(BF16)
            DU[where] = low
            PF[pl.ds(at * 2, 2)] = nt(low, WI[layer]).reshape(2, rows, width)

        gather_near(moves)
        back_feed(y)
        sum_local(copies, PF, 2, 0)
        tick(0, 1)
        gather_remote(moves)
        back_feed(1 - y)
        sum_remote(copies, PF, 2, 0)
        gather_finish(moves)

        def halves(ref):
            return lambda at: ref[:, :, pl.ds(at, half)].reshape(-1, half)

        split_grad(G[layer], halves(DF), base, 0, 4)
        tick(2)
        for own_side in (False, True):
            left = N1B[layer, :, :, pl.ds(side_of(own_side), half)].reshape(own_rows, half)
            for at in range(2):
                put_units(own_side, base, 4 + 2 * at, 2, tn(left, DU[:, at * half : (at + 1) * half]))
            if not own_side:
                send_units(base, 4, 4)
        tick(3)
        only = jnp.where(t == 0, 1.0, 0.0)
        put_vec(layer, 0, only * jnp.sum(DF[...].reshape(own_rows, width).astype(F32), axis=0, keepdims=True))
        put_vec(layer, 14 + t, jnp.sum(DU[...].astype(F32), axis=0, keepdims=True))

        moves = gather_copies(DA)
        for ch in range(PIECES):
            d_normed = DR[piece(ch)] + sum_finish(copies, PF, 2, 0, ch)
            rstd = SD1[layer, piece(ch)][:, :1]
            d_first = norm_backward(d_normed, XH1[layer, piece(ch)], rstd, full_vec(layer, 6))
            DA[t, piece(ch)] = d_first.astype(BF16)
            gather_start(moves, ch)
            DR1[piece(ch)] = d_first
            DR[piece(ch)] = d_normed
        put_vec(layer, 2, jnp.sum(DR[...] * XH1[layer], axis=0, keepdims=True))
        put_vec(layer, 3, jnp.sum(DR[...], axis=0, keepdims=True))

        def back_out(at):
            where = pl.ds(pl.multiple_of(at * 2 * rows, 2 * rows), 2 * rows)
            block = DA[pl.ds(at * 2, 2)].reshape(2 * rows, width)
            DOB[where] = nt(block, WO[layer]).astype(BF16)

        gather_near(moves)
        back_out(y)
        tick(4, 5)
        gather_remote(moves)
        back_out(1 - y)
        gather_finish(moves)
        split_grad(OB[layer], halves(DA), base, 8, 1)
        put_vec(layer, 1, only * jnp.sum(DA[...].reshape(own_rows, width).astype(F32), axis=0, keepdims=True))

        DKF[...] = jnp.zeros_like(DKF)
        DVF[...] = jnp.zeros_like(DVF)

        def back_attend(at, inner):
            where = pl.ds(pl.multiple_of(at * tile, tile), tile)
            grad_tile = DOB[where]
            q_tile = Q[layer, where]
            product = grad_tile.astype(F32) * OB[layer, where].astype(F32)
            d_query = []
            for head in range(3):
                lanes = slice(2 * HD, 3 * HD) if head == 2 else slice(0, 2 * HD)
                d_mix = head_cols(grad_tile, head)
                d_prob = nt(d_mix, head_full(V[layer], head))
                total = jnp.sum(head_cols(product, head), axis=-1, keepdims=True)
                low = PB[layer, head, where]
                d_score = (low.astype(F32) * (d_prob - total)).astype(BF16)
                d_query.append(nn(d_score, head_full(K[layer], head)))
                DKF[:, lanes] += tn(d_score, head_cols(q_tile, head))
                DVF[:, lanes] += tn(low, d_mix)
            scale = HD**-0.5
            DQ[where, : 2 * HD] = (jnp.where(lane_low, d_query[0], d_query[1]) * scale).astype(BF16)
            DQ[where, 2 * HD :] = (d_query[2] * scale).astype(BF16)
            return inner

        tick(6)
        lax.fori_loop(0, 2, back_attend, 0)
        tick(7, 8)
        DK[...] = DKF[...].astype(BF16)
        DV[...] = DVF[...].astype(BF16)

        def back_in(at, with_q):
            where = pl.ds(pl.multiple_of(at * rows, 2 * rows), 2 * rows)
            total = nn(DK[where], WQ[layer, cols : 2 * cols]) + nn(DV[where], WQ[layer, 2 * cols :])
            if with_q:
                mine = pl.ds(pl.multiple_of((at - own) * rows, 2 * rows), 2 * rows)
                total = total + nn(DQ[mine], WQ[layer, :cols])
            PF[pl.ds(at, 2)] = total.reshape(2, rows, width)

        pf_far = PF.at[pl.ds(far, 4)]
        pf_own = PF.at[pl.ds(own, 4)]
        far_copies = sum_copies(3, 1)
        back_in(far + 2 * (1 - y), False)
        sum_remote(far_copies, pf_far, 3, 1)
        back_in(far + 2 * y, False)
        sum_local(far_copies, pf_far, 3, 1)
        copies = sum_copies(4, 0)
        back_in(own + 2 * (1 - y), True)
        sum_remote(copies, pf_own, 4, 0)
        back_in(own + 2 * y, True)
        sum_local(copies, pf_own, 4, 0)
        for ch in range(PIECES):
            ZS[piece(ch)] = sum_finish(far_copies, pf_far, 3, 1, ch).astype(BF16)
            across(layer, ch).start()
        tick(9)

        def block_cols(ref, start, count):
            return lambda at: ref[pl.ds(start, count), :, pl.ds(at, half)].reshape(-1, half)

        xb = XB.at[layer]
        split_grad(DQ[...], block_cols(xb, own, 4), base, 9, 1)
        split_grad(DK[...], block_cols(xb, 0, 8), base, 10, 1)
        split_grad(DV[...], block_cols(xb, 0, 8), base, 11, 1)
        tick(10)
        put_vec(layer, 6 + t, jnp.sum(DQ[...].astype(F32), axis=0, keepdims=True))
        put_vec(layer, 10 + t, jnp.sum(DV[...].astype(F32), axis=0, keepdims=True))

        tick(11)
        return carry

    lax.fori_loop(0, LAYERS, backward_layer, 0)
    for ch in range(PIECES):
        CO[piece(ch)] = layer_grad(0, ch).astype(BF16)
    collect_start(CO, OG, 3)
    vec_move(0)
    if fused:
        more = LAGS[3]
        for i in range(more):
            if i in VEC_TICKS:
                vec_move(1 + VEC_TICKS.index(i))
            advance(total_units + i)
        vec_move(7)

        def drain(i, carry):
            out_copy(GO, i).wait()
            return carry

        lax.fori_loop(total_units - RING, total_units, drain, 0)
        for layer in range(LAYERS):
            fetch_drain(layer)
    else:
        own_out = pltpu.make_async_copy(GO, out_mat.at[0], om_sem.at[0])
        far_out = pltpu.make_async_copy(XR, out_mat.at[1], om_sem.at[1])
        own_out.start()
        far_out.start()
        own_out.wait()
        far_out.wait()
    out_vec[...] = (OW if fused else OV)[...]
    collect_wait(TK, OT, 2)
    out_tok[...] = OT[...]
    collect_wait(CO, OG, 3)
    out_grad[...] = OG[...]


def finish_kernel(dims, *refs):
    tok_ref, grad_ref, mat_ref, vec_ref = refs[:4]
    out_tok, out_grad, out_q, out_k, out_v, out_o, out_i, out_u = refs[4:12]
    vec_q, vec_v, vec_o, vec_i, vec_u, gain_1, shift_1, gain_2, shift_2 = refs[12:]
    width, cols, units, half = dims
    layer = pl.program_id(0)
    s = lax.axis_index("shard")

    @pl.when(layer == 0)
    def _():
        out_tok[...] = tok_ref[...]
        out_grad[...] = grad_ref[...].astype(F32)

    for i in range(4):
        out_u[0, i * cols : (i + 1) * cols, :] = mat_ref[i].astype(F32)
        r, cc = i % 2, i // 2
        out_i[0, r * cols : (r + 1) * cols, cc * half : (cc + 1) * half] = mat_ref[4 + i].astype(F32)
    out_o[0] = mat_ref[8].astype(F32)
    out_q[0] = mat_ref[9].astype(F32)
    out_k[0] = mat_ref[10].astype(F32)
    out_v[0] = mat_ref[11].astype(F32)
    line = pl.ds(layer, 1)
    at = pl.ds(pl.multiple_of(s * half, half), half)
    for row, ref in ((0, vec_u), (1, vec_o), (2, gain_1), (3, shift_1), (4, gain_2), (5, shift_2)):
        ref[line, :] = vec_ref[0, row : row + 1, at]
    for row, ref in ((6, vec_q), (10, vec_v)):
        first = vec_ref[0, pl.ds(row + 2 * s, 1), :cols]
        second = vec_ref[0, pl.ds(row + 1 + 2 * s, 1), :cols]
        ref[line, :] = jnp.concatenate([first, second], axis=1)
    vec_i[line, :width] = vec_ref[0, pl.ds(14 + 2 * s, 1)]
    vec_i[line, width:] = vec_ref[0, pl.ds(15 + 2 * s, 1)]


def per_device(
    tokens,
    cotangent,
    segment_ids,
    lengths,
    query_weight,
    key_weight,
    value_weight,
    output_weight,
    inner_weight,
    outer_weight,
    query_bias,
    value_bias,
    output_bias,
    inner_bias,
    outer_bias,
    first_gain,
    first_shift,
    second_gain,
    second_shift,
):
    shards = lax.axis_size("shard")
    assert lax.axis_size("ctx") == 4 and lax.axis_size("tp") == 4 and tokens.shape[0] == 2
    fused = shards == 2
    seqs, part, width = tokens.shape
    cols = query_weight.shape[2]
    units = inner_weight.shape[2]
    half = width // 2
    rows = 2 * part
    own_rows, all_rows = 4 * rows, 8 * rows
    assert cols == 3 * HD and segment_ids.shape[1] == all_rows and units == width == 4 * cols

    def turned(mat):
        return jnp.swapaxes(mat, 1, 2)

    mats = (
        turned(query_weight),
        turned(key_weight),
        turned(value_weight),
        output_weight,
        inner_weight,
        outer_weight,
    )
    vecs = (query_bias, value_bias, output_bias, outer_bias, inner_bias, first_gain, first_shift, second_gain, second_shift)
    if not fused:
        mats = tuple(
            lax.all_gather(mat, "shard", axis=axis, tiled=True) for mat, axis in zip(mats, (2, 2, 2, 2, 1, 2))
        )
        vecs = tuple(lax.all_gather(vec, "shard", axis=1, tiled=True) for vec in vecs)

    n_units = 12 * LAYERS
    out_shape = [
        jax.ShapeDtypeStruct((2, part, width), BF16),
        jax.ShapeDtypeStruct((2, part, width), BF16),
        jax.ShapeDtypeStruct((n_units, cols, half) if fused else (2, n_units, cols, half), BF16),
        jax.ShapeDtypeStruct((LAYERS, VEC_ROWS, width), F32),
    ]
    vm = pltpu.VMEM
    dma = pltpu.SemaphoreType.DMA
    scratch = [
        vm((LAYERS, 3 * cols, width), BF16),
        vm((LAYERS, cols, width), BF16),
        vm((LAYERS, width, units), BF16),
        vm((LAYERS, units, width), BF16),
        vm((2, LAYERS, 16, half), F32),
        vm((own_rows, 128), F32),
        vm((8, all_rows), F32),
        vm((rows, width), F32),
        vm((rows, width), F32),
        vm((rows, width), F32),
        vm((rows, width), F32),
        vm((rows, width), BF16),
        vm((rows, width), BF16),
        vm((2, part, width), BF16),
        vm((2, part, width), BF16),
        vm((LAYERS, rows, width), F32),
        vm((LAYERS, rows, width), F32),
        vm((LAYERS, rows, 128), F32),
        vm((LAYERS, rows, 128), F32),
        vm((LAYERS, 8, rows, width), BF16),
        vm((LAYERS, own_rows, cols), BF16),
        vm((LAYERS, all_rows, cols), BF16),
        vm((LAYERS, all_rows, cols), BF16),
        vm((LAYERS, own_rows, cols), BF16),
        vm((LAYERS, 4, rows, width), BF16),
        vm((LAYERS, own_rows, units), BF16),
        vm((LAYERS, own_rows, units), BF16),
        vm((LAYERS, 3, own_rows, all_rows), BF16),
        vm((4, rows, width), BF16),
        vm((4, rows, width), BF16),
        vm((own_rows, units), BF16),
        vm((own_rows, cols), BF16),
        vm((own_rows, cols), BF16),
        vm((all_rows, cols), BF16),
        vm((all_rows, cols), BF16),
        vm((all_rows, cols), F32),
        vm((all_rows, cols), F32),
        vm((8, rows, width), F32),
        vm((2, 3, rows, width), BF16),
        vm((5, 3, rows, width), BF16),
        vm((rows, width), BF16),
        vm((LAYERS, rows, width), BF16),
        vm((n_units, cols, half), BF16),
        vm((12, cols, half), BF16),
        vm((n_units, cols, half), BF16),
        vm((n_units, cols, half), BF16),
        vm((n_units, cols, half), BF16),
        vm((LAYERS, VEC_ROWS, width), F32),
        vm((2, LAYERS, VEC_ROWS, width), F32),
        vm((3, LAYERS, VEC_ROWS // 4, width), F32),
        vm((LAYERS, VEC_ROWS, width), F32),
        dma((LAYERS, 6)),
        dma((LAYERS, 9)),
        dma((LAYERS, 9)),
        dma((LAYERS, 6)),
        dma((LAYERS, 6)),
        dma((7,)),
        dma((7,)),
        dma((4, 2)),
        dma((4, 2)),
        dma((LAYERS, 7 * PIECES)),
        dma((LAYERS, 7 * PIECES)),
        dma((3 * PIECES,)),
        dma((3 * PIECES,)),
        dma((2, 2 * PIECES + 1)),
        dma((2, 2 * PIECES + 1)),
        dma((LAYERS, PIECES)),
        dma((LAYERS, PIECES)),
        dma((12,)),
        dma((n_units,)),
        dma((RING,)),
        dma((RING,)),
        dma((RING,)),
        dma((RING,)),
        dma((RING,)),
        dma((RING,)),
        dma((RING,)),
    ]
    vmem = pl.BlockSpec(memory_space=pltpu.VMEM)
    hbm = pl.BlockSpec(memory_space=pl.ANY)
    layer_out, grad_tokens, grad_mats, grad_vecs = pl.pallas_call(
        functools.partial(step_kernel, (width, cols, units, half), fused),
        out_shape=out_shape,
        in_specs=[vmem] * 12 + [pl.BlockSpec(memory_space=pltpu.SMEM)] + [hbm] * 6,
        out_specs=[vmem, vmem, hbm, vmem],
        scratch_shapes=scratch,
        compiler_params=pltpu.CompilerParams(
            collective_id=0, has_side_effects=True, vmem_limit_bytes=67043328
        ),
        name="encoder_step",
    )(tokens, cotangent, segment_ids, *vecs, lengths, *mats)

    if fused:
        dims = (width, cols, units, half)
        layer_block = lambda *shape: pl.BlockSpec((1,) + shape, lambda i: (i,) + (0,) * len(shape))
        whole = lambda *shape: pl.BlockSpec(shape, lambda i: (0,) * len(shape))
        mat_shapes = [(cols, half)] * 4 + [(half, units), (units, half)]
        vec_lens = (half, half, half, 4 * half, half, half, half, half, half)
        outs = pl.pallas_call(
            functools.partial(finish_kernel, dims),
            grid=(LAYERS,),
            out_shape=[
                jax.ShapeDtypeStruct((2, part, width), BF16),
                jax.ShapeDtypeStruct((2, part, width), F32),
            ]
            + [jax.ShapeDtypeStruct((LAYERS,) + shape, F32) for shape in mat_shapes]
            + [jax.ShapeDtypeStruct((LAYERS, count), F32) for count in vec_lens],
            in_specs=[
                whole(2, part, width),
                whole(2, part, width),
                pl.BlockSpec((12, cols, half), lambda i: (LAYERS - 1 - i, 0, 0)),
                layer_block(VEC_ROWS, width),
            ],
            out_specs=[whole(2, part, width), whole(2, part, width)]
            + [layer_block(*shape) for shape in mat_shapes]
            + [whole(LAYERS, count) for count in vec_lens],
            name="write_out",
        )(layer_out, grad_tokens, grad_mats, grad_vecs)
        return tuple(outs[:2]) + tuple(turned(mat) for mat in outs[2:5]) + tuple(outs[5:])

    mats = grad_mats.reshape(2, LAYERS, 12, cols, half)[:, ::-1]
    wide = jnp.concatenate([mats[0], mats[1]], axis=-1)
    wide = jnp.concatenate([wide[:, :4], wide[:, 8:]], axis=1)
    wide = lax.psum(lax.psum_scatter(wide, "shard", scatter_dimension=3, tiled=True), "ctx").astype(F32)
    inner = mats[:, :, 4:8].reshape(2, LAYERS, 2, 2, cols, half)
    inner = jnp.transpose(inner, (1, 0, 3, 4, 2, 5)).reshape(LAYERS, width, units)
    inner = lax.psum(lax.psum_scatter(inner, "shard", scatter_dimension=1, tiled=True), "ctx").astype(F32)
    grad_outer = wide[:, :4].reshape(LAYERS, units, -1)
    grad_output = wide[:, 4]
    grad_query, grad_key, grad_value = (turned(wide[:, 5 + at]) for at in range(3))

    total = lax.psum(grad_vecs, ("shard", "ctx", "tp"))
    at = lax.axis_index("shard")

    def owned(vec):
        count = vec.shape[1] // shards
        return lax.dynamic_slice_in_dim(vec, at * count, count, 1)

    vec_query = owned(total[:, 6:10, :cols].reshape(LAYERS, -1))
    vec_value = owned(total[:, 10:14, :cols].reshape(LAYERS, -1))
    vec_inner = owned(total[:, 14:18].reshape(LAYERS, -1))
    vec_outer, vec_output, gain_one, shift_one, gain_two, shift_two = (owned(total[:, row]) for row in range(6))
    return (
        layer_out,
        grad_tokens.astype(F32),
        grad_query,
        grad_key,
        grad_value,
        grad_output,
        inner,
        grad_outer,
        vec_query,
        vec_value,
        vec_output,
        vec_inner,
        vec_outer,
        gain_one,
        shift_one,
        gain_two,
        shift_two,
    )


def solution(mesh):
    rows = P("shard", ("ctx", "tp"), None)
    down = P(None, "shard", "tp")
    across = P(None, "tp", "shard")
    vector = P(None, "shard")
    mats = (down, down, down, across, down, across)
    return jax.shard_map(
        per_device,
        mesh=mesh,
        in_specs=(rows, rows, P("shard", None), P("shard")) + mats + (vector,) * 9,
        out_specs=(rows, rows) + mats + (vector,) * 9,
        check_vma=False,
    )
```
